512 devices in a mesh: tm: 32 (over z, y_hi), feat: 8 (over x, core), rep: 2 (over y_lo).
Axes of the slice: x: 4, y: 4 (y_hi: 2, y_lo: 2; y = y_hi * 2 + y_lo), z: 16, core: 2. Of those that a mesh axis runs over, the one named last changes fastest.
Arguments:
- frames: bfloat16 [2, 8192, 16384], P('rep', 'tm', 'feat'), may hold values from -50 to 50, as said below
- panel_low: bfloat16 [16384, 512], P('feat', 'tm'), may hold values from -0.046875 to 0.046875
- panel_high: bfloat16 [16384, 512], P('feat', 'tm'), may hold values from -0.046875 to 0.046875
- lags: int32 [2], P('rep'), may hold values from 1 to 64, as said below
- seg_lengths: int32 [2, 64], P('rep'), may hold values from 1 to 1024, 8192 in all within a row
- ridge: float32 [32], replicated, may hold values from 0.01 to 10
Outputs:
- covariances: float32 [3, 1024, 1024], P(None, ('tm', 'feat', 'rep'))
- scores: float32 [1024, 32], P(('tm', 'feat', 'rep'))
The draws below stay inside these ranges and needn't reach their ends.
Inputs may be any that keep to these rules, and one draw needn't show every extreme that they name: The frames of each run follow one trajectory in time. `lags`: one run has the lag 64. `seg_lengths`: each row sums to 8192.
All inputs are finite; a program needn't handle non-finite values.
Results may differ from the reference program's by a relative error of at most 0.003.
Values may be sent and summed in bfloat16 or wider, within the bound.
No kernel may reach another device: no remote copies, remote signals or barrier semaphores. Data moves between devices by JAX's collectives and lax.ppermute only.
A program may use at most 64 MiB of HBM per device.

```python
import math
import jax
import jax.numpy as jnp
import numpy as np
from jax import lax

F = 16384
K = 512
T_DEV = 256
SEGS = 64
NR = 32
LAG_MAX = 64
FRAMES = 8192
REPS = 2
SEG_MOST = 1024
N_FEAT = 8


def draw_frames(key, part):
    span = 2 * LAG_MAX

    def one_run(run_key):
        slow_part = jnp.clip(jax.random.normal(jax.random.fold_in(run_key, 1), (FRAMES // span + 2, F), jnp.float32), -5.0, 5.0)
        slow_full = jnp.repeat(slow_part, span, axis=0)[LAG_MAX:LAG_MAX + FRAMES]
        fast_part = jnp.clip(jax.random.normal(jax.random.fold_in(run_key, 2), (FRAMES, F), jnp.float32), -5.0, 5.0)
        ramp = jnp.exp(jnp.log(3.0) * jnp.arange(FRAMES, dtype=jnp.float32) / FRAMES)
        values = (slow_full + 0.6 * fast_part) * ramp[:, None]
        return values.astype(jnp.bfloat16)
    run_keys = jax.random.split(jax.random.fold_in(key, 7), REPS)
    return lax.map(one_run, run_keys)


def draw_lags(key, part):
    chosen = jax.random.randint(jax.random.fold_in(key, 21), (), 0, REPS)
    others = jax.random.randint(jax.random.fold_in(key, 22), (REPS,), 1, LAG_MAX + 1)
    return jnp.where(jnp.arange(REPS) == chosen, LAG_MAX, others).astype(jnp.int32)


def block_levels(key, extent, cuts, smallest, high):
    def one(position, blocks):
        steps = jax.random.uniform(jax.random.fold_in(jax.random.fold_in(key, 6), position), (blocks,), jnp.float32, smallest / len(cuts), high / len(cuts))
        return jnp.repeat(jnp.exp(steps), extent[position] // blocks).reshape((-1,) + (1,) * (len(extent) - position - 1))

    gain = one(*cuts[0])
    for cut in cuts[1:]:
        gain = gain * one(*cut)
    return gain


def length_profile(amount, total, bound, slope):
    weights = [(1 << 20) // math.isqrt(grade ** slope) + 1 for grade in range(2, amount + 1)]
    spare, counts = total - bound - (amount - 1), [1] * (amount - 1)
    while spare > 0:
        movable = [i for i in range(amount - 1) if counts[i] < bound]
        whole, remaining = sum([weights[i] for i in movable]), spare
        for i in movable:
            extra = min(bound - counts[i], max(1, remaining * weights[i] // whole), spare)
            counts[i] = counts[i] + extra
            spare = spare - extra
    return np.array([bound] + counts)


def uneven_parts(own_key, number_of, total, reach, lean):
    if number_of == 2:
        one = jax.random.randint(own_key, (), max(1, total - reach), min(reach, total - 1) + 1)
        return jnp.stack([one, total - one])
    lengths = jnp.asarray(length_profile(number_of, total, reach, lean), jnp.int32)
    couples = (number_of - 1) // 2
    donor, taker = lengths[1:1 + 2 * couples:2], lengths[2:2 + 2 * couples:2]
    room = jnp.minimum(donor - 1, reach - taker)
    passed = jax.random.randint(jax.random.fold_in(own_key, 1), (couples,), 0, 1 << 20) % (room + 1)
    lengths = lengths.at[1:1 + 2 * couples:2].set(donor - passed).at[2:2 + 2 * couples:2].set(taker + passed)
    return lengths[jax.random.permutation(jax.random.fold_in(own_key, 2), number_of)]


def gaussian(rng, shape, scale, bound, shards=(), kind=jnp.bfloat16):
    loudness = block_levels(rng, shape, shards, -0.22, 0.18) if shards else 1.0
    values = jax.random.normal(rng, shape, jnp.float32) * scale * loudness
    return jnp.minimum(jnp.maximum(values, -bound), bound).astype(kind)


def setup_inputs(seed: int = 0) -> dict:
    arg_keys = jax.random.split(jax.random.key(seed), 7)
    return {
        "frames": draw_frames(jax.random.fold_in(arg_keys[6], 71), 0),
        "panel_low": gaussian(arg_keys[1], (F, K), F ** -0.5, 0.046875, ((0, 8), (1, 32))),
        "panel_high": gaussian(arg_keys[2], (F, K), F ** -0.5, 0.046875, ((0, 8), (1, 32))),
        "lags": draw_lags(jax.random.fold_in(arg_keys[6], 71), 0),
        "seg_lengths": jax.vmap(lambda own: uneven_parts(own, SEGS, FRAMES, SEG_MOST, 2))(jax.random.split(arg_keys[4], REPS)).reshape((REPS, SEGS)).astype(jnp.int32),
        "ridge": jnp.clip(jnp.exp(jax.random.uniform(arg_keys[5], (NR,), jnp.float32, math.log(0.01), math.log(10.0))), 0.01, 10.0),
    }


def project_block(frame_block, panels):
    width = F // N_FEAT
    summed = jnp.zeros((frame_block.shape[0], 2 * K), jnp.float32)
    for feature_group in range(N_FEAT):
        partial_term = jnp.dot(frame_block[:, feature_group * width:(feature_group + 1) * width],
                               panels[feature_group * width:(feature_group + 1) * width],
                               preferred_element_type=jnp.float32)
        rounded = lax.optimization_barrier(partial_term.astype(jnp.bfloat16))
        summed = summed + rounded.astype(jnp.float32)
    return summed.astype(jnp.bfloat16)


def reference(frames, panel_low, panel_high, lags, seg_lengths, ridge):
    panels = jnp.concatenate([panel_low, panel_high], axis=1)
    frame_blocks = frames.reshape(REPS * FRAMES // T_DEV, T_DEV, F)
    basis = lax.map(lambda blk_rows: project_block(blk_rows, panels), frame_blocks)
    basis = basis.reshape(REPS, FRAMES, 2 * K)
    positions = jnp.arange(FRAMES, dtype=jnp.int32)
    cov_inst = jnp.zeros((2 * K, 2 * K), jnp.float32)
    cov_cross = jnp.zeros((2 * K, 2 * K), jnp.float32)
    cov_lagged = jnp.zeros((2 * K, 2 * K), jnp.float32)
    for replica in range(REPS):
        lag_now = lags[replica].astype(jnp.int32)
        padded = jnp.concatenate([basis[replica], jnp.zeros((LAG_MAX, 2 * K), jnp.bfloat16)], axis=0)
        lagged = lax.dynamic_slice_in_dim(padded, lag_now, FRAMES, 0)
        seg_ends = jnp.cumsum(seg_lengths[replica]).astype(jnp.int32)
        end_of = jnp.min(jnp.where(seg_ends[None, :] > positions[:, None], seg_ends[None, :], FRAMES), axis=1)
        keep_mask = (positions + lag_now < end_of).astype(jnp.bfloat16)[:, None]
        masked = basis[replica] * keep_mask
        lag_masked = lagged * keep_mask
        cov_inst = cov_inst + jnp.dot(masked.T, basis[replica], preferred_element_type=jnp.float32)
        cov_cross = cov_cross + jnp.dot(masked.T, lagged, preferred_element_type=jnp.float32)
        cov_lagged = cov_lagged + jnp.dot(lag_masked.T, lagged, preferred_element_type=jnp.float32)
    inverse_count = 1.0 / (REPS * FRAMES)
    cov_inst = cov_inst * inverse_count
    cov_cross = cov_cross * inverse_count
    cov_lagged = cov_lagged * inverse_count
    diag_inst = jnp.diagonal(cov_inst)
    diag_lagged = jnp.diagonal(cov_lagged)
    inverse_lagged = 1.0 / (diag_lagged[:, None] + ridge[None, :])
    weighted = jnp.dot(jnp.square(cov_cross), inverse_lagged, precision=lax.Precision.HIGHEST,
                       preferred_element_type=jnp.float32)
    scores = weighted / (diag_inst[:, None] + ridge[None, :])
    covariances = jnp.stack([cov_inst, cov_cross, cov_lagged], axis=0)
    return (covariances, scores)
```

```python
import jax
import jax.numpy as jnp
import numpy as np
from jax import lax
from jax.experimental import pallas as pl
from jax.experimental.pallas import tpu as pltpu
from jax.sharding import Mesh, PartitionSpec as P

BF = jnp.bfloat16
F32 = jnp.float32
I32 = jnp.int32
HI = lax.Precision.HIGHEST
NT = (((1,), (1,)), ((), ()))
VMEM = pltpu.CompilerParams(vmem_limit_bytes=48 * 1024 * 1024)

Z = ("zh", "zl")
FE = ("x", "c")
CHUNKS = ("yh", "yl", "x", "c")


def one_hot(rows, cols, hit):
    r = lax.broadcasted_iota(I32, (rows, cols), 0)
    c = lax.broadcasted_iota(I32, (rows, cols), 1)
    return jnp.where(hit(r, c), 1.0, 0.0).astype(BF)


def pack_kernel(yl_ref, low_ref, high_ref, out_ref):
    yl = yl_ref[0]
    src = one_hot(16, 16, lambda r, c: c == ((r >> 1) & 3) * 4 + (r >> 3) * 2 + (r & 1))
    for yh in range(2):
        off = pl.multiple_of((yl * 2 + yh) * 512, 512)
        for half, ref in enumerate((low_ref, high_ref)):
            rows = ref[:, pl.ds(off, 512)]
            out_ref[yh, half] = jnp.dot(src, rows, preferred_element_type=F32).astype(BF)


def project_kernel(pa_ref, pb_ref, frames_ref, out_ref, panel_ref):
    @pl.when(pl.program_id(0) == 0)
    def _():
        for zl in range(4):
            for zh in range(4):
                ref = pa_ref if zh < 2 else pb_ref
                for half in range(2):
                    for yl in range(2):
                        chunk = ((zl & 1) * 2 + yl) * 8 + half * 4 + zh
                        row = chunk * 32 + (zl >> 1) * 16
                        panel_ref[row : row + 16, :] = ref[zl, zh & 1, half, yl]

    out_ref[...] = lax.dot_general(
        panel_ref[...], frames_ref[...], NT, preferred_element_type=F32
    ).astype(BF)


def cov_kernel(lags_ref, place_ref, seg_ref, left_ref, right_ref, out_ref):
    z = place_ref[0]
    perm = one_hot(
        128,
        128,
        lambda r, c: c
        == ((r >> 5) & 1) * 64 + ((r >> 1) & 1) * 32 + (r >> 6) * 16 + ((r >> 2) & 7) * 2 + (r & 1),
    )
    right = jnp.dot(perm, right_ref[...], preferred_element_type=F32)
    halo = right[:, 1024:1152]
    tri = lax.broadcasted_iota(I32, (64, 64), 1) <= lax.broadcasted_iota(I32, (64, 64), 0)
    seg = seg_ref[...].astype(F32)
    keep, keep_end, lagged = [], [], []
    for rep in range(2):
        lag = lags_ref[rep]
        ends = jnp.sum(jnp.where(tri, seg[rep : rep + 1, :], 0.0), axis=1, keepdims=True)
        pos = lax.broadcasted_iota(I32, (1, 512), 1) + z * 512
        here = pos.astype(F32)
        ahead = (pos + lag).astype(F32)
        behind = (pos - lag).astype(F32)
        cut = jnp.where((ends > here) & (ends <= ahead), 1.0, 0.0)
        keep.append(1.0 - jnp.max(cut, axis=0, keepdims=True))
        cut_end = jnp.where((ends > behind) & (ends <= here), 1.0, 0.0)
        inside = jnp.where(behind >= 0.0, 1.0, 0.0)
        keep_end.append((1.0 - jnp.max(cut_end, axis=0, keepdims=True)) * inside)
        tail = halo if rep == 0 else pltpu.roll(halo, 64, 1)
        ext = jnp.concatenate([right[:, rep * 512 : (rep + 1) * 512], tail], axis=1)
        lagged.append(pltpu.roll(ext, 640 - lag, 1)[:, :512].astype(BF))
    keep = jnp.concatenate(keep, axis=1)
    keep_end = jnp.concatenate(keep_end, axis=1)
    lagged = jnp.concatenate(lagged, axis=1)
    now = right[:, :1024]
    now_bf = now.astype(BF)
    left = left_ref[...]
    left_start = left * keep.astype(BF)
    left_end = left * keep_end.astype(BF)
    for m, (lhs, rhs) in enumerate(
        ((left_start, now_bf), (left_start, lagged), (left_end, now_bf))
    ):
        block = lax.dot_general(lhs, rhs, NT, preferred_element_type=F32)
        for d in range(16):
            out_ref[d, m * 16 : (m + 1) * 16, :] = block[d * 16 : (d + 1) * 16, :]
    var = lax.dot_general(
        jnp.ones((8, 1024), F32), now * now * keep_end, NT, precision=HI, preferred_element_type=F32
    )
    for d in range(16):
        out_ref[d, 48:56, :] = var


def rows_kernel(scale, parts_ref, ridge_ref, out_ref):
    total = parts_ref[0]
    for d in range(1, 16):
        total = total + parts_ref[d]
    total = total * scale
    var = total[48:49, :]
    inverse = 1.0 / (var + ridge_ref[...])
    cross = total[16:32, :]
    inverse = jnp.concatenate([inverse, jnp.zeros((96, 128), F32)], axis=0)
    weighted = lax.dot_general(cross * cross, inverse, NT, precision=HI, preferred_element_type=F32)
    for d in range(8):
        for m in range(3):
            out_ref[d, m * 2 : m * 2 + 2, :] = total[m * 16 + d * 2 : m * 16 + d * 2 + 2, :]
        out_ref[d, 6:8, :] = weighted[d * 2 : d * 2 + 2, :]


def final_kernel(place_ref, parts_ref, ridge_ref, cov_ref, score_ref):
    first = place_ref[1]
    weighted = parts_ref[0, 6:8, :]
    for f in range(1, 8):
        weighted = weighted + parts_ref[f, 6:8, :]
    lane = lax.broadcasted_iota(I32, (2, 128), 1)
    row = lax.broadcasted_iota(I32, (2, 128), 0)
    diag = jnp.zeros((2, 1), F32)
    for f in range(8):
        for m in range(3):
            cov_ref[m, :, f * 128 : (f + 1) * 128] = parts_ref[f, m * 2 : m * 2 + 2, :]
        own = lane + f * 128 == first + row
        diag = diag + jnp.sum(
            jnp.where(own, parts_ref[f, 0:2, :], 0.0), axis=1, keepdims=True
        )
    score_ref[...] = weighted[:, :32] / (diag + ridge_ref[...])


def local(frames, panel_low, panel_high, lags, seg_lengths, ridge):
    z = lax.axis_index(Z).astype(I32)
    yl = lax.axis_index("yl").astype(I32)
    own_first = ((z * 2 + lax.axis_index("yh")) * 8 + lax.axis_index(FE)) * 4 + yl * 2
    place = jnp.stack([z, own_first.astype(I32)])
    smem = pl.BlockSpec(memory_space=pltpu.SMEM)
    vmem = pl.BlockSpec(memory_space=pltpu.VMEM)

    mine = jnp.concatenate([lags.reshape(1, 1), seg_lengths], axis=1)
    other = lax.ppermute(mine, "yl", [(0, 1), (1, 0)])
    both = jnp.where(
        yl == 0, jnp.concatenate([mine, other], axis=0), jnp.concatenate([other, mine], axis=0)
    )

    packed = pl.pallas_call(
        pack_kernel,
        out_shape=jax.ShapeDtypeStruct((2, 2, 16, 512), BF),
        in_specs=[smem, vmem, vmem],
        out_specs=vmem,
        compiler_params=VMEM,
    )(yl[None], panel_low.T, panel_high.T)
    swapped = lax.all_to_all(packed, "yh", split_axis=0, concat_axis=0, tiled=True)
    swapped = swapped.reshape(2, 2, 2, 8, 512).transpose(1, 2, 0, 3, 4)
    stage = lax.all_gather(swapped.reshape(64, 512), "zh", axis=0, tiled=True)
    panel_a = lax.all_gather(stage[:128], "zl", axis=0, tiled=True).reshape(4, 2, 2, 2, 16, 512)
    panel_b = lax.all_gather(stage[128:], "zl", axis=0, tiled=True).reshape(4, 2, 2, 2, 16, 512)

    quarters = frames[0].reshape(256, 4, 512).transpose(1, 0, 2)
    frames_q = lax.all_to_all(quarters, ("yl", "yh"), split_axis=0, concat_axis=0, tiled=True)
    frames_q = frames_q.reshape(1024, 512)

    partial = pl.pallas_call(
        project_kernel,
        grid=(4,),
        out_shape=jax.ShapeDtypeStruct((1024, 1024), BF),
        in_specs=[
            pl.BlockSpec((4, 2, 2, 2, 16, 512), lambda i: (0, 0, 0, 0, 0, 0)),
            pl.BlockSpec((4, 2, 2, 2, 16, 512), lambda i: (0, 0, 0, 0, 0, 0)),
            pl.BlockSpec((256, 512), lambda i: (i, 0)),
        ],
        out_specs=pl.BlockSpec((1024, 256), lambda i: (0, i)),
        scratch_shapes=[pltpu.VMEM((1024, 512), BF)],
        compiler_params=VMEM,
    )(panel_a, panel_b, frames_q)

    pieces = lax.all_to_all(
        partial.reshape(32, 32, 1024), CHUNKS, split_axis=0, concat_axis=0, tiled=True
    )
    basis = jnp.sum(pieces.astype(F32), axis=0).astype(BF)

    head = jnp.concatenate([basis[:, 0:64], basis[:, 512:576]], axis=1)
    halo = lax.ppermute(head, Z, [(i + 1, i) for i in range(15)])
    left = lax.all_gather(basis, FE, axis=0, tiled=True)
    right = lax.all_gather(
        jnp.concatenate([basis, halo], axis=1), ("yh", "yl"), axis=0, tiled=True
    )

    terms = pl.pallas_call(
        cov_kernel,
        out_shape=jax.ShapeDtypeStruct((16, 56, 128), F32),
        in_specs=[smem, smem, vmem, vmem, vmem],
        out_specs=vmem,
        compiler_params=VMEM,
    )(both[:, 0], place, both[:, 1:], left, right)
    by_z = lax.all_to_all(terms, Z, split_axis=0, concat_axis=0, tiled=True)

    rows = pl.pallas_call(
        lambda *refs: rows_kernel(1.0 / 16384.0, *refs),
        out_shape=jax.ShapeDtypeStruct((8, 8, 128), F32),
        in_specs=[vmem, vmem],
        out_specs=vmem,
        compiler_params=VMEM,
    )(by_z, ridge[:, None])
    by_fe = lax.all_to_all(rows, FE, split_axis=0, concat_axis=0, tiled=True)

    return pl.pallas_call(
        final_kernel,
        out_shape=(
            jax.ShapeDtypeStruct((3, 2, 1024), F32),
            jax.ShapeDtypeStruct((2, 32), F32),
        ),
        in_specs=[smem, vmem, vmem],
        out_specs=(vmem, vmem),
        compiler_params=VMEM,
    )(place, by_fe, ridge[None, :])


def solution(mesh):
    fine = Mesh(
        np.asarray(mesh.devices).reshape(4, 4, 2, 4, 2, 2), ("zh", "zl", "yh", "x", "c", "yl")
    )
    tm = ("zh", "zl", "yh")
    in_specs = (P("yl", tm, FE), P(FE, tm), P(FE, tm), P("yl"), P("yl", None), P())
    rows = tm + FE + ("yl",)
    out_specs = (P(None, rows, None), P(rows, None))
    return jax.shard_map(local, mesh=fine, in_specs=in_specs, out_specs=out_specs, check_vma=False)
```

```python
import jax
import jax.numpy as jnp
import numpy as np
from jax import lax
from jax.experimental import pallas as pl
from jax.experimental.pallas import tpu as pltpu
from jax.sharding import Mesh, PartitionSpec as P

BF = jnp.bfloat16
F32 = jnp.float32
I32 = jnp.int32
HI = lax.Precision.HIGHEST
NT = (((1,), (1,)), ((), ()))
VMEM = pltpu.CompilerParams(vmem_limit_bytes=48 * 1024 * 1024)

Z = ("zh", "zl")
FE = ("x", "c")
MAIN = 896
CHUNKS = ("yh", "yl", "x", "c")


def one_hot(rows, cols, hit):
    r = lax.broadcasted_iota(I32, (rows, cols), 0)
    c = lax.broadcasted_iota(I32, (rows, cols), 1)
    return jnp.where(hit(r, c), 1.0, 0.0).astype(BF)


def pack_kernel(yl_ref, low_ref, high_ref, main_ref, rest_ref):
    off = pl.multiple_of(yl_ref[0] * 1024, 1024)
    src = one_hot(16, 16, lambda r, c: c == ((r >> 1) & 3) * 4 + (r >> 3) * 2 + (r & 1))
    for half, ref in enumerate((low_ref, high_ref)):
        rows = jnp.dot(src, ref[:, pl.ds(off, 1024)], preferred_element_type=F32).astype(BF)
        main_ref[half * 16 : half * 16 + 16, :] = rows[:, :MAIN]
        for z in range(16):
            rest_ref[z, half * 16 : half * 16 + 16, :] = rows[:, MAIN:]


def project_kernel(main_ref, rest_ref, frames_ref, out_ref):
    acc = lax.dot_general(main_ref[...], frames_ref[:, :MAIN], NT, preferred_element_type=F32)
    acc = acc + lax.dot_general(
        rest_ref[...], frames_ref[:, MAIN:], NT, preferred_element_type=F32
    )
    for yh in range(2):
        for yl in range(2):
            for half in range(2):
                for zh in range(4):
                    row = (zh * 4 + yh) * 32 + half * 16 + yl * 8
                    both = jnp.concatenate([acc[row : row + 8], acc[row + 64 : row + 72]], axis=0)
                    chunk = (yh * 2 + yl) * 8 + half * 4 + zh
                    out_ref[chunk * 16 : chunk * 16 + 16, :] = both.astype(BF)


def sum_kernel(parts_ref, basis_ref, head_ref):
    sums = []
    for yh in range(2):
        total = parts_ref[yh, 0, 0].astype(F32)
        for i in range(1, 16):
            total = total + parts_ref[yh, i // 8, i % 8].astype(F32)
        sums.append(total)
    basis = jnp.concatenate([sums[0][:8], sums[1][:8], sums[0][8:], sums[1][8:]], axis=0)
    basis_ref[...] = basis.astype(BF)
    lane = lax.broadcasted_iota(I32, (32, 128), 1)
    head = jnp.where(lane < 64, basis[:, :128], pltpu.roll(basis[:, 512:640], 64, 1))
    head_ref[...] = head.astype(BF)


def cov_kernel(lags_ref, place_ref, seg_ref, left_ref, right_ref, out_ref):
    z = place_ref[0]
    perm = one_hot(
        128,
        128,
        lambda r, c: c
        == ((r >> 5) & 1) * 64 + ((r >> 1) & 1) * 32 + (r >> 6) * 16 + ((r >> 2) & 7) * 2 + (r & 1),
    )
    right = jnp.dot(perm, right_ref[...], preferred_element_type=F32)
    halo = right[:, 1024:1152]
    tri = lax.broadcasted_iota(I32, (64, 64), 1) <= lax.broadcasted_iota(I32, (64, 64), 0)
    seg = seg_ref[...].astype(F32)
    keep, keep_end, lagged = [], [], []
    for rep in range(2):
        lag = lags_ref[rep]
        ends = jnp.sum(jnp.where(tri, seg[rep : rep + 1, :], 0.0), axis=1, keepdims=True)
        pos = lax.broadcasted_iota(I32, (1, 512), 1) + z * 512
        here = pos.astype(F32)
        ahead = (pos + lag).astype(F32)
        behind = (pos - lag).astype(F32)
        cut = jnp.where((ends > here) & (ends <= ahead), 1.0, 0.0)
        keep.append(1.0 - jnp.max(cut, axis=0, keepdims=True))
        cut_end = jnp.where((ends > behind) & (ends <= here), 1.0, 0.0)
        inside = jnp.where(behind >= 0.0, 1.0, 0.0)
        keep_end.append((1.0 - jnp.max(cut_end, axis=0, keepdims=True)) * inside)
        tail = halo if rep == 0 else pltpu.roll(halo, 64, 1)
        ext = jnp.concatenate([right[:, rep * 512 : (rep + 1) * 512], tail], axis=1)
        lagged.append(pltpu.roll(ext, 640 - lag, 1)[:, :512].astype(BF))
    keep = jnp.concatenate(keep, axis=1)
    keep_end = jnp.concatenate(keep_end, axis=1)
    lagged = jnp.concatenate(lagged, axis=1)
    now = right[:, :1024]
    now_bf = now.astype(BF)
    left = left_ref[...]
    left_start = left * keep.astype(BF)
    left_end = left * keep_end.astype(BF)
    for m, (lhs, rhs) in enumerate(
        ((left_start, now_bf), (left_start, lagged), (left_end, now_bf))
    ):
        block = lax.dot_general(lhs, rhs, NT, preferred_element_type=F32)
        for d in range(16):
            out_ref[d % 4, d // 4, m * 16 : (m + 1) * 16, :] = block[d * 16 : (d + 1) * 16, :]
    var = lax.dot_general(
        jnp.ones((8, 1024), F32), now * now * keep_end, NT, precision=HI, preferred_element_type=F32
    )
    for d in range(16):
        out_ref[d % 4, d // 4, 48:56, :] = var


def rows_kernel(parts_ref, out_ref):
    for zh in range(4):
        total = (parts_ref[0, zh] + parts_ref[1, zh]) + (parts_ref[2, zh] + parts_ref[3, zh])
        for f in range(8):
            for m in range(3):
                src = m * 16 + f * 2
                out_ref[zh, f, m * 2 : m * 2 + 2, :] = total[src : src + 2, :]
            out_ref[zh, f, 6:8, :] = total[48:50, :]


def final_kernel(scale, place_ref, parts_ref, ridge_ref, row_ref, cov_ref, score_ref):
    first = place_ref[1]
    ridge = ridge_ref[...]
    lane = lax.broadcasted_iota(I32, (2, 128), 1)
    row = lax.broadcasted_iota(I32, (2, 128), 0)
    diag = jnp.zeros((2, 1), F32)
    weighted = [jnp.zeros((32, 128), F32) for _ in range(2)]
    for f in range(8):
        total = (parts_ref[0, f] + parts_ref[1, f]) + (parts_ref[2, f] + parts_ref[3, f])
        total = total * scale
        for m in range(3):
            cov_ref[m, :, f * 128 : (f + 1) * 128] = total[m * 2 : m * 2 + 2, :]
        own = lane + f * 128 == first + row
        diag = diag + jnp.sum(jnp.where(own, total[0:2, :], 0.0), axis=1, keepdims=True)
        inverse = 1.0 / (total[6:7, :] + ridge)
        for e in range(2):
            cross = total[2 + e : 3 + e, :]
            weighted[e] = weighted[e] + (cross * cross) * inverse
    ones = jnp.ones((8, 128), F32)
    pad = jnp.zeros((96, 128), F32)
    score = [
        lax.dot_general(
            ones,
            jnp.concatenate([w, pad], axis=0),
            NT,
            precision=HI,
            preferred_element_type=F32,
        )[0:1, :32]
        for w in weighted
    ]
    for e in range(2):
        score_ref[e : e + 1, :] = score[e] / (diag[e : e + 1, :] + row_ref[...])


def local(frames, panel_low, panel_high, lags, seg_lengths, ridge):
    z = lax.axis_index(Z).astype(I32)
    yl = lax.axis_index("yl").astype(I32)
    own_first = ((z * 2 + lax.axis_index("yh")) * 8 + lax.axis_index(FE)) * 4 + yl * 2
    place = jnp.stack([z, own_first.astype(I32)])
    smem = pl.BlockSpec(memory_space=pltpu.SMEM)
    vmem = pl.BlockSpec(memory_space=pltpu.VMEM)

    mine = jnp.concatenate([lags.reshape(1, 1), seg_lengths], axis=1)
    other = lax.ppermute(mine, "yl", [(0, 1), (1, 0)])
    both = jnp.where(
        yl == 0, jnp.concatenate([mine, other], axis=0), jnp.concatenate([other, mine], axis=0)
    )

    low, high = frames[:, :, :1024], frames[:, :, 1024:]
    halves = jnp.concatenate([low, low, high, high], axis=0)
    frames_h = lax.all_to_all(halves, ("yl", "yh"), split_axis=0, concat_axis=0, tiled=True)

    main, rest = pl.pallas_call(
        pack_kernel,
        out_shape=(
            jax.ShapeDtypeStruct((32, MAIN), BF),
            jax.ShapeDtypeStruct((16, 32, 1024 - MAIN), BF),
        ),
        in_specs=[smem, vmem, vmem],
        out_specs=(vmem, vmem),
        compiler_params=VMEM,
    )(yl[None], panel_low.T, panel_high.T)
    main, rest, both = lax.optimization_barrier((main, rest, both))
    panel_rest = lax.all_to_all(rest, Z, split_axis=0, concat_axis=0, tiled=True)
    panel_main = lax.all_gather(main, Z, axis=0, tiled=True)

    partial = pl.pallas_call(
        project_kernel,
        grid=(4,),
        out_shape=jax.ShapeDtypeStruct((512, 1024), BF),
        in_specs=[
            pl.BlockSpec((512, MAIN), lambda i: (0, 0)),
            pl.BlockSpec((512, 1024 - MAIN), lambda i: (0, 0)),
            pl.BlockSpec((256, 1024), lambda i: (i, 0)),
        ],
        out_specs=pl.BlockSpec((512, 256), lambda i: (0, i)),
        compiler_params=VMEM,
    )(panel_main, panel_rest.reshape(512, 1024 - MAIN), frames_h.reshape(1024, 1024))

    parts = lax.all_to_all(
        partial.reshape(32, 16, 1024), CHUNKS, split_axis=0, concat_axis=0, tiled=True
    )
    basis, head = pl.pallas_call(
        sum_kernel,
        out_shape=(
            jax.ShapeDtypeStruct((32, 1024), BF),
            jax.ShapeDtypeStruct((32, 128), BF),
        ),
        in_specs=[vmem],
        out_specs=(vmem, vmem),
        compiler_params=VMEM,
    )(parts.reshape(2, 2, 8, 16, 1024))

    halo = lax.ppermute(head, Z, [(i + 1, i) for i in range(15)])
    left = lax.all_gather(basis, FE, axis=0, tiled=True)
    right = lax.all_gather(
        jnp.concatenate([basis, halo], axis=1), ("yh", "yl"), axis=0, tiled=True
    )

    terms = pl.pallas_call(
        cov_kernel,
        out_shape=jax.ShapeDtypeStruct((4, 4, 56, 128), F32),
        in_specs=[smem, smem, vmem, vmem, vmem],
        out_specs=vmem,
        compiler_params=VMEM,
    )(both[:, 0], place, both[:, 1:], left, right)
    by_zl = lax.all_to_all(terms, "zl", split_axis=0, concat_axis=0, tiled=True)
    rows = pl.pallas_call(
        rows_kernel,
        out_shape=jax.ShapeDtypeStruct((4, 8, 8, 128), F32),
        in_specs=[vmem],
        out_specs=vmem,
        compiler_params=VMEM,
    )(by_zl)
    by_row = lax.all_to_all(
        rows.reshape(32, 8, 128), ("zh", "x", "c"), split_axis=0, concat_axis=0, tiled=True
    )
    return pl.pallas_call(
        lambda *refs: final_kernel(1.0 / 16384.0, *refs),
        out_shape=(
            jax.ShapeDtypeStruct((3, 2, 1024), F32),
            jax.ShapeDtypeStruct((2, 32), F32),
        ),
        in_specs=[smem, vmem, vmem, vmem],
        out_specs=(vmem, vmem),
        compiler_params=VMEM,
    )(place, by_row.reshape(4, 8, 8, 128), ridge[:, None], ridge[None, :])


def solution(mesh):
    fine = Mesh(
        np.asarray(mesh.devices).reshape(4, 4, 2, 4, 2, 2), ("zh", "zl", "yh", "x", "c", "yl")
    )
    tm = ("zh", "zl", "yh")
    in_specs = (P("yl", tm, FE), P(FE, tm), P(FE, tm), P("yl"), P("yl", None), P())
    rows = tm + FE + ("yl",)
    out_specs = (P(None, rows, None), P(rows, None))
    return jax.shard_map(local, mesh=fine, in_specs=in_specs, out_specs=out_specs, check_vma=False)
```

```python
import jax
import jax.numpy as jnp
import numpy as np
from jax import lax
from jax.experimental import pallas as pl
from jax.experimental.pallas import tpu as pltpu
from jax.sharding import Mesh, PartitionSpec as P

BF = jnp.bfloat16
F32 = jnp.float32
I32 = jnp.int32
HI = lax.Precision.HIGHEST
NT = (((1,), (1,)), ((), ()))
VMEM = pltpu.CompilerParams(vmem_limit_bytes=48 * 1024 * 1024)

Z = ("z3", "z2", "z1", "z0")
Z8 = ("z3", "z2", "z1")
FE = ("x", "c")


def one_hot(rows, cols, hit):
    r = lax.broadcasted_iota(I32, (rows, cols), 0)
    c = lax.broadcasted_iota(I32, (rows, cols), 1)
    return jnp.where(hit(r, c), 1.0, 0.0).astype(BF)


def pack_kernel(yl_ref, low_ref, high_ref, out_ref):
    off = pl.multiple_of(yl_ref[0] * 1024, 1024)
    src = one_hot(16, 16, lambda r, c: c == ((r >> 1) & 3) * 4 + (r >> 3) * 2 + (r & 1))
    for half, ref in enumerate((low_ref, high_ref)):
        rows = jnp.dot(src, ref[:, pl.ds(off, 1024)], preferred_element_type=F32)
        out_ref[half * 16 : half * 16 + 16, :] = rows.astype(BF)


def halves_kernel(frames_ref, out_ref):
    for half in range(2):
        rows = frames_ref[0, :, half * 1024 : (half + 1) * 1024]
        out_ref[half * 2] = rows
        out_ref[half * 2 + 1] = rows


def project_kernel(place_ref, own_ref, other_ref, frames_ref, keep_ref, send_ref):
    z0 = place_ref[0] & 1
    c = place_ref[2]
    frames = frames_ref[...]
    own = lax.dot_general(own_ref[...], frames, NT, preferred_element_type=F32)
    other = lax.dot_general(other_ref[...], frames, NT, preferred_element_type=F32)

    def store(even, odd, keep_ref, send_ref, own_c):
        for yh, acc in enumerate((even, odd)):
            for yl in range(2):
                for half in range(2):
                    for zh in range(4):
                        row = zh * 64 + half * 16 + yl * 8
                        both = jnp.concatenate(
                            [acc[row : row + 8], acc[row + 32 : row + 40]], axis=0
                        )
                        chunk = (yh * 2 + yl) * 4 + half * 2 + (zh >> 1)
                        ref = keep_ref if (zh & 1) == own_c else send_ref
                        ref[chunk * 16 : chunk * 16 + 16, :] = both.astype(BF)

    for own_z0 in range(2):
        for own_c in range(2):

            @pl.when((z0 == own_z0) & (c == own_c))
            def _(own_z0=own_z0, own_c=own_c):
                pair = (own, other) if own_z0 == 0 else (other, own)
                store(*pair, keep_ref, send_ref, own_c)


def sum_kernel(parts_ref, basis_ref, tail_ref):
    sums = []
    for yh in range(2):
        total = parts_ref[yh, 0, 0].astype(F32)
        for i in range(1, 8):
            total = total + parts_ref[yh, i // 4, i % 4].astype(F32)
        sums.append(total)
    basis = jnp.concatenate([sums[0][:8], sums[1][:8], sums[0][8:], sums[1][8:]], axis=0)
    basis_ref[...] = basis.astype(BF)
    lane = lax.broadcasted_iota(I32, (32, 128), 1)
    tail = jnp.where(lane < 64, pltpu.roll(basis[:, 384:512], 64, 1), basis[:, 896:])
    tail_ref[...] = tail.astype(BF)


def cov_kernel(lags_ref, place_ref, seg_ref, left_ref, right_ref, out_ref):
    z = place_ref[0]
    perm = one_hot(
        128,
        128,
        lambda r, c: c
        == ((r >> 5) & 1) * 64 + ((r >> 1) & 1) * 32 + (r >> 6) * 16 + ((r >> 2) & 7) * 2 + (r & 1),
    )
    now = jnp.dot(perm, right_ref[...], preferred_element_type=F32)
    now_bf = now.astype(BF)
    tri = lax.broadcasted_iota(I32, (64, 64), 1) <= lax.broadcasted_iota(I32, (64, 64), 0)
    seg = seg_ref[...].astype(F32)
    tails = left_ref[:, 1024:].astype(F32)
    keep, keep_end, lagged = [], [], []
    for rep in range(2):
        lag = lags_ref[rep]
        ends = jnp.sum(jnp.where(tri, seg[rep : rep + 1, :], 0.0), axis=1, keepdims=True)
        pos = lax.broadcasted_iota(I32, (1, 512), 1) + z * 512
        here = pos.astype(F32)
        ahead = (pos + lag).astype(F32)
        behind = (pos - lag).astype(F32)
        cut = jnp.where((ends > here) & (ends <= ahead), 1.0, 0.0)
        keep.append(1.0 - jnp.max(cut, axis=0, keepdims=True))
        cut_end = jnp.where((ends > behind) & (ends <= here), 1.0, 0.0)
        inside = jnp.where(behind >= 0.0, 1.0, 0.0)
        keep_end.append((1.0 - jnp.max(cut_end, axis=0, keepdims=True)) * inside)
        tail = tails if rep == 1 else pltpu.roll(tails, 64, 1)
        block = left_ref[:, rep * 512 : (rep + 1) * 512].astype(F32)
        ext = jnp.concatenate([tail, block], axis=1)
        lagged.append(pltpu.roll(ext, lag + 512, 1)[:, :512].astype(BF))
    keep = jnp.concatenate(keep, axis=1)
    keep_end = jnp.concatenate(keep_end, axis=1)
    lagged = jnp.concatenate(lagged, axis=1)
    left = left_ref[:, :1024]
    start_bf, end_bf = keep.astype(BF), keep_end.astype(BF)
    for m, lhs in enumerate((left * start_bf, lagged * end_bf, left * end_bf)):
        block = lax.dot_general(lhs, now_bf, NT, preferred_element_type=F32)
        for d in range(16):
            out_ref[d % 2, d // 2, m * 16 : (m + 1) * 16, :] = block[d * 16 : (d + 1) * 16, :]
    var = lax.dot_general(
        jnp.ones((8, 1024), F32), now * now * keep_end, NT, precision=HI, preferred_element_type=F32
    )
    for d in range(16):
        out_ref[d % 2, d // 2, 48:56, :] = var


def pair_kernel(parts_ref, out_ref):
    out_ref[...] = parts_ref[0] + parts_ref[1]


def rows_kernel(parts_ref, out_ref):
    total = parts_ref[0]
    for d in range(1, 8):
        total = total + parts_ref[d]
    for f in range(8):
        for m in range(3):
            src = m * 16 + f * 2
            out_ref[f, m * 2 : m * 2 + 2, :] = total[src : src + 2, :]
        out_ref[f, 6:8, :] = total[48:50, :]


def final_kernel(scale, place_ref, parts_ref, ridge_ref, row_ref, cov_ref, score_ref):
    first = place_ref[1]
    ridge = ridge_ref[...]
    lane = lax.broadcasted_iota(I32, (2, 128), 1)
    row = lax.broadcasted_iota(I32, (2, 128), 0)
    diag = jnp.zeros((2, 1), F32)
    weighted = [jnp.zeros((32, 128), F32) for _ in range(2)]
    for f in range(8):
        total = parts_ref[f] * scale
        for m in range(3):
            cov_ref[m, :, f * 128 : (f + 1) * 128] = total[m * 2 : m * 2 + 2, :]
        own = lane + f * 128 == first + row
        diag = diag + jnp.sum(jnp.where(own, total[0:2, :], 0.0), axis=1, keepdims=True)
        inverse = 1.0 / (total[6:7, :] + ridge)
        for e in range(2):
            cross = total[2 + e : 3 + e, :]
            weighted[e] = weighted[e] + (cross * cross) * inverse
    ones = jnp.ones((8, 128), F32)
    pad = jnp.zeros((96, 128), F32)
    score = [
        lax.dot_general(
            ones,
            jnp.concatenate([w, pad], axis=0),
            NT,
            precision=HI,
            preferred_element_type=F32,
        )[0:1, :32]
        for w in weighted
    ]
    for e in range(2):
        score_ref[e : e + 1, :] = score[e] / (diag[e : e + 1, :] + row_ref[...])


def call(kernel, out, *args, smem=0, **kw):
    specs = [pl.BlockSpec(memory_space=pltpu.SMEM)] * smem
    specs += [pl.BlockSpec(memory_space=pltpu.VMEM)] * (len(args) - smem)
    shapes = [jax.ShapeDtypeStruct(*o) for o in out]
    outs = [pl.BlockSpec(memory_space=pltpu.VMEM)] * len(out)
    got = pl.pallas_call(
        kernel, out_shape=shapes, in_specs=specs, out_specs=outs, compiler_params=VMEM
    )(*args)
    return got[0] if len(out) == 1 else got


def all_to_all(x, axes):
    return lax.all_to_all(x, axes, split_axis=0, concat_axis=0, tiled=True)


def local(frames, panel_low, panel_high, lags, seg_lengths, ridge):
    z = lax.axis_index(Z).astype(I32)
    yl = lax.axis_index("yl").astype(I32)
    c = lax.axis_index("c").astype(I32)
    own_first = ((z * 2 + lax.axis_index("yh")) * 8 + lax.axis_index(FE)) * 4 + yl * 2
    place = jnp.stack([z, own_first.astype(I32), c])

    mine = jnp.concatenate([lags.reshape(1, 1), seg_lengths], axis=1)
    other = lax.ppermute(mine, "yl", [(0, 1), (1, 0)])

    halves = pl.pallas_call(
        halves_kernel,
        grid=(4,),
        out_shape=jax.ShapeDtypeStruct((4, 256, 1024), BF),
        in_specs=[pl.BlockSpec((1, 64, 2048), lambda i: (0, i, 0))],
        out_specs=pl.BlockSpec((4, 64, 1024), lambda i: (0, i, 0)),
        compiler_params=VMEM,
    )(frames)
    frames_h = all_to_all(halves, ("yl", "yh")).reshape(1024, 1024)

    packed = call(
        pack_kernel, [((32, 1024), BF)], yl[None], panel_low.T, panel_high.T, smem=1
    )
    panel_own = lax.all_gather(packed, Z8, axis=0, tiled=True)
    panel_other = lax.ppermute(panel_own, "z0", [(0, 1), (1, 0)])
    panel_other, other = lax.optimization_barrier((panel_other, other))
    both = jnp.where(
        yl == 0, jnp.concatenate([mine, other], axis=0), jnp.concatenate([other, mine], axis=0)
    )

    whole = pl.BlockSpec((256, 1024), lambda i: (0, 0))
    column = pl.BlockSpec((256, 256), lambda i: (0, i))
    keep, send = pl.pallas_call(
        project_kernel,
        grid=(4,),
        out_shape=[jax.ShapeDtypeStruct((256, 1024), BF)] * 2,
        in_specs=[
            pl.BlockSpec(memory_space=pltpu.SMEM),
            whole,
            whole,
            pl.BlockSpec((256, 1024), lambda i: (i, 0)),
        ],
        out_specs=[column, column],
        compiler_params=VMEM,
    )(place, panel_own, panel_other, frames_h)
    got = lax.ppermute(send, "c", [(0, 1), (1, 0)])
    pairs = (keep.astype(F32) + got.astype(F32)).astype(BF)
    parts = all_to_all(pairs.reshape(16, 16, 1024), ("yh", "yl", "x"))
    basis, tail = call(
        sum_kernel, [((32, 1024), BF), ((32, 128), BF)], parts.reshape(2, 2, 4, 16, 1024)
    )

    before = lax.ppermute(tail, Z, [(i, i + 1) for i in range(15)])
    right = all_to_all(jnp.broadcast_to(basis[None], (4, 32, 1024)), ("yh", "yl"))
    left = lax.all_gather(jnp.concatenate([basis, before], axis=1), FE, axis=0, tiled=True)

    terms = call(
        cov_kernel,
        [((2, 8, 56, 128), F32)],
        both[:, 0],
        place,
        both[:, 1:],
        left,
        right.reshape(128, 1024),
        smem=2,
    )
    pair = call(pair_kernel, [((8, 56, 128), F32)], all_to_all(terms, "z0"))
    rows = call(rows_kernel, [((8, 8, 128), F32)], all_to_all(pair, Z8))
    by_row = all_to_all(rows, FE)
    return call(
        lambda *refs: final_kernel(1.0 / 16384.0, *refs),
        [((3, 2, 1024), F32), ((2, 32), F32)],
        place,
        by_row,
        ridge[:, None],
        ridge[None, :],
        smem=1,
    )


def solution(mesh):
    fine = Mesh(
        np.asarray(mesh.devices).reshape(2, 2, 2, 2, 2, 4, 2, 2),
        ("z3", "z2", "z1", "z0", "yh", "x", "c", "yl"),
    )
    tm = Z + ("yh",)
    in_specs = (P("yl", tm, FE), P(FE, tm), P(FE, tm), P("yl"), P("yl", None), P())
    rows = tm + FE + ("yl",)
    out_specs = (P(None, rows, None), P(rows, None))
    return jax.shard_map(local, mesh=fine, in_specs=in_specs, out_specs=out_specs, check_vma=False)
```

```python
import jax
import jax.numpy as jnp
import numpy as np
from jax import lax
from jax.experimental import pallas as pl
from jax.experimental.pallas import tpu as pltpu
from jax.sharding import Mesh, PartitionSpec as P

BF = jnp.bfloat16
F32 = jnp.float32
I32 = jnp.int32
HI = lax.Precision.HIGHEST
NT = (((1,), (1,)), ((), ()))
VMEM = pltpu.CompilerParams(vmem_limit_bytes=48 * 1024 * 1024)

Z = ("z3", "z2", "z1", "z0")
Z8 = ("z3", "z2", "z1")
FE = ("x", "c")


def one_hot(rows, cols, hit):
    r = lax.broadcasted_iota(I32, (rows, cols), 0)
    c = lax.broadcasted_iota(I32, (rows, cols), 1)
    return jnp.where(hit(r, c), 1.0, 0.0).astype(BF)


def pack_kernel(yl_ref, low_ref, high_ref, out_ref):
    off = pl.multiple_of(yl_ref[0] * 1024, 1024)
    src = one_hot(16, 16, lambda r, c: c == ((r >> 1) & 3) * 4 + (r >> 3) * 2 + (r & 1))
    for half, ref in enumerate((low_ref, high_ref)):
        rows = jnp.dot(src, ref[:, pl.ds(off, 1024)], preferred_element_type=F32)
        out_ref[half * 16 : half * 16 + 16, :] = rows.astype(BF)


def halves_kernel(frames_ref, out_ref):
    for half in range(2):
        rows = frames_ref[0, :, half * 1024 : (half + 1) * 1024]
        out_ref[half * 2] = rows
        out_ref[half * 2 + 1] = rows


def project_kernel(place_ref, own_ref, other_ref, frames_ref, keep_ref, send_ref):
    z0 = place_ref[0] & 1
    c = place_ref[2]
    frames = frames_ref[...]
    own = lax.dot_general(own_ref[...], frames, NT, preferred_element_type=F32)
    other = lax.dot_general(other_ref[...], frames, NT, preferred_element_type=F32)

    def store(even, odd, keep_ref, send_ref, own_c):
        for yh, acc in enumerate((even, odd)):
            for z1 in range(2):
                for yl in range(2):
                    for half in range(2):
                        for z2 in range(2):
                            row = (z2 * 2 + z1) * 32 + half * 16 + yl * 8
                            both = jnp.concatenate(
                                [acc[row : row + 8], acc[row + 128 : row + 136]], axis=0
                            )
                            chunk = ((z1 * 2 + yh) * 2 + yl) * 4 + half * 2
                            ref = keep_ref if z2 == own_c else send_ref
                            ref[chunk * 8 : chunk * 8 + 16, :] = both.astype(BF)

    for own_z0 in range(2):
        for own_c in range(2):

            @pl.when((z0 == own_z0) & (c == own_c))
            def _(own_z0=own_z0, own_c=own_c):
                pair = (own, other) if own_z0 == 0 else (other, own)
                store(*pair, keep_ref, send_ref, own_c)


def sum_kernel(parts_ref, basis_ref, tail_ref):
    for z0 in range(2):
        sums = []
        for yh in range(2):
            total = parts_ref[z0, yh, 0, 0].astype(F32)
            for i in range(1, 8):
                total = total + parts_ref[z0, yh, i // 4, i % 4].astype(F32)
            sums.append(total)
        basis = jnp.concatenate(sums, axis=0)
        for rep in range(2):
            at = rep * 1024 + z0 * 512
            basis_ref[:, at : at + 512] = basis[:, rep * 512 : (rep + 1) * 512].astype(BF)
        if z0 == 1:
            lane = lax.broadcasted_iota(I32, (16, 128), 1)
            tail = jnp.where(lane < 64, pltpu.roll(basis[:, 384:512], 64, 1), basis[:, 896:])
            tail_ref[...] = tail.astype(BF)


def cov_kernel(lags_ref, place_ref, seg_ref, left_ref, right_ref, out_ref):
    first = (place_ref[0] >> 1) * 1024
    perm = one_hot(
        128,
        128,
        lambda r, c: c
        == (r >> 5) * 32 + ((r >> 1) & 1) * 16 + ((r >> 2) & 7) * 2 + (r & 1),
    )
    now = jnp.dot(perm, right_ref[...], preferred_element_type=F32)
    now_bf = now.astype(BF)
    tri = lax.broadcasted_iota(I32, (64, 64), 1) <= lax.broadcasted_iota(I32, (64, 64), 0)
    seg = seg_ref[...].astype(F32)
    tails = left_ref[:, 2048:].astype(F32)
    keep, keep_end, lagged = [], [], []
    for rep in range(2):
        lag = lags_ref[rep]
        ends = jnp.sum(jnp.where(tri, seg[rep : rep + 1, :], 0.0), axis=1, keepdims=True)
        pos = lax.broadcasted_iota(I32, (1, 1024), 1) + first
        here = pos.astype(F32)
        ahead = (pos + lag).astype(F32)
        behind = (pos - lag).astype(F32)
        cut = jnp.where((ends > here) & (ends <= ahead), 1.0, 0.0)
        keep.append(1.0 - jnp.max(cut, axis=0, keepdims=True))
        cut_end = jnp.where((ends > behind) & (ends <= here), 1.0, 0.0)
        inside = jnp.where(behind >= 0.0, 1.0, 0.0)
        keep_end.append((1.0 - jnp.max(cut_end, axis=0, keepdims=True)) * inside)
        tail = tails if rep == 1 else pltpu.roll(tails, 64, 1)
        block = left_ref[:, rep * 1024 : (rep + 1) * 1024].astype(F32)
        ext = jnp.concatenate([tail, block], axis=1)
        lagged.append(pltpu.roll(ext, lag + 1024, 1)[:, :1024].astype(BF))
    keep = jnp.concatenate(keep, axis=1)
    keep_end = jnp.concatenate(keep_end, axis=1)
    lagged = jnp.concatenate(lagged, axis=1)
    left = left_ref[:, :2048]
    start_bf, end_bf = keep.astype(BF), keep_end.astype(BF)
    for m, lhs in enumerate((left * start_bf, lagged * end_bf, left * end_bf)):
        block = lax.dot_general(lhs, now_bf, NT, preferred_element_type=F32)
        for d in range(8):
            out_ref[d, m * 16 : (m + 1) * 16, :] = block[d * 16 : (d + 1) * 16, :]
    var = lax.dot_general(
        jnp.ones((8, 2048), F32), now * now * keep_end, NT, precision=HI, preferred_element_type=F32
    )
    for d in range(8):
        out_ref[d, 48:56, :] = var


def rows_kernel(parts_ref, out_ref):
    total = parts_ref[0]
    for d in range(1, 8):
        total = total + parts_ref[d]
    for f in range(8):
        for m in range(3):
            src = m * 16 + f * 2
            out_ref[f, m * 2 : m * 2 + 2, :] = total[src : src + 2, :]
        out_ref[f, 6:8, :] = total[48:50, :]


def final_kernel(scale, place_ref, parts_ref, ridge_ref, row_ref, cov_ref, score_ref):
    first = place_ref[1]
    ridge = ridge_ref[...]
    lane = lax.broadcasted_iota(I32, (2, 128), 1)
    row = lax.broadcasted_iota(I32, (2, 128), 0)
    diag = jnp.zeros((2, 1), F32)
    weighted = [jnp.zeros((32, 128), F32) for _ in range(2)]
    for f in range(8):
        total = parts_ref[f] * scale
        for m in range(3):
            cov_ref[m, :, f * 128 : (f + 1) * 128] = total[m * 2 : m * 2 + 2, :]
        own = lane + f * 128 == first + row
        diag = diag + jnp.sum(jnp.where(own, total[0:2, :], 0.0), axis=1, keepdims=True)
        inverse = 1.0 / (total[6:7, :] + ridge)
        for e in range(2):
            cross = total[2 + e : 3 + e, :]
            weighted[e] = weighted[e] + (cross * cross) * inverse
    ones = jnp.ones((8, 128), F32)
    pad = jnp.zeros((96, 128), F32)
    score = [
        lax.dot_general(
            ones,
            jnp.concatenate([w, pad], axis=0),
            NT,
            precision=HI,
            preferred_element_type=F32,
        )[0:1, :32]
        for w in weighted
    ]
    for e in range(2):
        score_ref[e : e + 1, :] = score[e] / (diag[e : e + 1, :] + row_ref[...])


def call(kernel, out, *args, smem=0, **kw):
    specs = [pl.BlockSpec(memory_space=pltpu.SMEM)] * smem
    specs += [pl.BlockSpec(memory_space=pltpu.VMEM)] * (len(args) - smem)
    shapes = [jax.ShapeDtypeStruct(*o) for o in out]
    outs = [pl.BlockSpec(memory_space=pltpu.VMEM)] * len(out)
    got = pl.pallas_call(
        kernel, out_shape=shapes, in_specs=specs, out_specs=outs, compiler_params=VMEM
    )(*args)
    return got[0] if len(out) == 1 else got


def all_to_all(x, axes):
    return lax.all_to_all(x, axes, split_axis=0, concat_axis=0, tiled=True)


def local(frames, panel_low, panel_high, lags, seg_lengths, ridge):
    z = lax.axis_index(Z).astype(I32)
    yl = lax.axis_index("yl").astype(I32)
    c = lax.axis_index("c").astype(I32)
    own_first = ((z * 2 + lax.axis_index("yh")) * 8 + lax.axis_index(FE)) * 4 + yl * 2
    place = jnp.stack([z, own_first.astype(I32), c])

    mine = jnp.concatenate([lags.reshape(1, 1), seg_lengths], axis=1)
    other = lax.ppermute(mine, "yl", [(0, 1), (1, 0)])

    halves = pl.pallas_call(
        halves_kernel,
        grid=(4,),
        out_shape=jax.ShapeDtypeStruct((4, 256, 1024), BF),
        in_specs=[pl.BlockSpec((1, 64, 2048), lambda i: (0, i, 0))],
        out_specs=pl.BlockSpec((4, 64, 1024), lambda i: (0, i, 0)),
        compiler_params=VMEM,
    )(frames)
    frames_h = all_to_all(halves, ("yl", "yh")).reshape(1024, 1024)

    packed = call(
        pack_kernel, [((32, 1024), BF)], yl[None], panel_low.T, panel_high.T, smem=1
    )
    panel_own = lax.all_gather(packed, Z8, axis=0, tiled=True)
    panel_other = lax.ppermute(panel_own, "z0", [(0, 1), (1, 0)])
    panel_other, other = lax.optimization_barrier((panel_other, other))
    both = jnp.where(
        yl == 0, jnp.concatenate([mine, other], axis=0), jnp.concatenate([other, mine], axis=0)
    )

    whole = pl.BlockSpec((256, 1024), lambda i: (0, 0))
    column = pl.BlockSpec((256, 256), lambda i: (0, i))
    keep, send = pl.pallas_call(
        project_kernel,
        grid=(4,),
        out_shape=[jax.ShapeDtypeStruct((256, 1024), BF)] * 2,
        in_specs=[
            pl.BlockSpec(memory_space=pltpu.SMEM),
            whole,
            whole,
            pl.BlockSpec((256, 1024), lambda i: (i, 0)),
        ],
        out_specs=[column, column],
        compiler_params=VMEM,
    )(place, panel_own, panel_other, frames_h)
    got = lax.ppermute(send, "c", [(0, 1), (1, 0)])
    pairs = (keep.astype(F32) + got.astype(F32)).astype(BF)
    parts = all_to_all(pairs.reshape(32, 8, 1024), ("z0", "yh", "yl", "x"))
    basis, tail = call(
        sum_kernel, [((16, 2048), BF), ((16, 128), BF)], parts.reshape(2, 2, 2, 4, 8, 1024)
    )

    before = lax.ppermute(tail, Z8, [(i, i + 1) for i in range(7)])
    right = all_to_all(jnp.broadcast_to(basis[None], (8, 16, 2048)), ("z0", "yh", "yl"))
    left = lax.all_gather(jnp.concatenate([basis, before], axis=1), FE, axis=0, tiled=True)

    terms = call(
        cov_kernel,
        [((8, 56, 128), F32)],
        both[:, 0],
        place,
        both[:, 1:],
        left,
        right.reshape(128, 2048),
        smem=2,
    )
    rows = call(rows_kernel, [((8, 8, 128), F32)], all_to_all(terms, Z8))
    by_row = all_to_all(rows, FE)
    return call(
        lambda *refs: final_kernel(1.0 / 16384.0, *refs),
        [((3, 2, 1024), F32), ((2, 32), F32)],
        place,
        by_row,
        ridge[:, None],
        ridge[None, :],
        smem=1,
    )


def solution(mesh):
    fine = Mesh(
        np.asarray(mesh.devices).reshape(2, 2, 2, 2, 2, 4, 2, 2),
        ("z3", "z2", "z1", "z0", "yh", "x", "c", "yl"),
    )
    tm = Z + ("yh",)
    in_specs = (P("yl", tm, FE), P(FE, tm), P(FE, tm), P("yl"), P("yl", None), P())
    rows = tm + FE + ("yl",)
    out_specs = (P(None, rows, None), P(rows, None))
    return jax.shard_map(local, mesh=fine, in_specs=in_specs, out_specs=out_specs, check_vma=False)
```

```python
import jax
import jax.numpy as jnp
import numpy as np
from jax import lax
from jax.experimental import pallas as pl
from jax.experimental.pallas import tpu as pltpu
from jax.sharding import Mesh, PartitionSpec as P

BF = jnp.bfloat16
F32 = jnp.float32
I32 = jnp.int32
HI = lax.Precision.HIGHEST
NT = (((1,), (1,)), ((), ()))
VMEM = pltpu.CompilerParams(vmem_limit_bytes=48 * 1024 * 1024)

Z = ("z3", "z2", "z1", "z0")
Z8 = ("z3", "z2", "z1")
FE = ("x", "c")


def one_hot(rows, cols, hit):
    r = lax.broadcasted_iota(I32, (rows, cols), 0)
    c = lax.broadcasted_iota(I32, (rows, cols), 1)
    return jnp.where(hit(r, c), 1.0, 0.0).astype(BF)


def pack_kernel(yl_ref, low_ref, high_ref, out_ref):
    off = pl.multiple_of(yl_ref[0] * 1024, 1024)
    src = one_hot(16, 16, lambda r, c: c == ((r >> 1) & 3) * 4 + (r >> 3) * 2 + (r & 1))
    for half, ref in enumerate((low_ref, high_ref)):
        rows = jnp.dot(src, ref[:, pl.ds(off, 1024)], preferred_element_type=F32)
        out_ref[half * 16 : half * 16 + 16, :] = rows.astype(BF)


def halves_kernel(frames_ref, out_ref):
    for half in range(2):
        rows = frames_ref[0, :, half * 1024 : (half + 1) * 1024]
        out_ref[half * 2] = rows
        out_ref[half * 2 + 1] = rows


def project_kernel(place_ref, panel_ref, frames_ref, keep_ref, send_ref):
    acc = lax.dot_general(panel_ref[...], frames_ref[...], NT, preferred_element_type=F32)

    def store(refs):
        for z1 in range(2):
            for yl in range(2):
                for half in range(2):
                    for z2 in range(2):
                        row = (z2 * 2 + z1) * 32 + half * 16 + yl * 8
                        both = jnp.concatenate(
                            [acc[row : row + 8], acc[row + 128 : row + 136]], axis=0
                        )
                        at = ((z1 * 2 + yl) * 4 + half * 2) * 8
                        refs[z2][at : at + 16, :] = both.astype(BF)

    pl.when(place_ref[2] == 0)(lambda: store((keep_ref, send_ref)))
    pl.when(place_ref[2] == 1)(lambda: store((send_ref, keep_ref)))


def join_kernel(place_ref, keep_a, got_a, keep_b, got_b, out_ref):
    own = place_ref[0] & 1
    for yh, keep, got in ((own, keep_a, got_a), (1 - own, keep_b, got_b)):
        for z0 in range(2):
            rows = slice(z0 * 64, z0 * 64 + 64)
            pair = keep[rows, :].astype(F32) + got[rows, :].astype(F32)
            out_ref[z0 * 2 + yh] = pair.astype(BF)


def sum_kernel(parts_ref, basis_ref, tail_ref, tiled_ref):
    for z0 in range(2):
        sums = []
        for yh in range(2):
            total = parts_ref[z0, yh, 0, 0].astype(F32)
            for i in range(1, 8):
                total = total + parts_ref[z0, yh, i // 4, i % 4].astype(F32)
            sums.append(total)
        basis = jnp.concatenate(sums, axis=0)
        for rep in range(2):
            at = rep * 1024 + z0 * 512
            block = basis[:, rep * 512 : (rep + 1) * 512].astype(BF)
            basis_ref[:, at : at + 512] = block
            for d in range(8):
                tiled_ref[d, :, at : at + 512] = block
        if z0 == 1:
            lane = lax.broadcasted_iota(I32, (16, 128), 1)
            tail = jnp.where(lane < 64, pltpu.roll(basis[:, 384:512], 64, 1), basis[:, 896:])
            tail_ref[...] = tail.astype(BF)


def mask_kernel(lags_ref, place_ref, seg_ref, out_ref):
    first = (place_ref[0] >> 1) * 1024
    tri = lax.broadcasted_iota(I32, (64, 64), 1) <= lax.broadcasted_iota(I32, (64, 64), 0)
    seg = seg_ref[...].astype(F32)
    for rep in range(2):
        lag = lags_ref[rep]
        ends = jnp.sum(jnp.where(tri, seg[rep : rep + 1, :], 0.0), axis=1, keepdims=True)
        pos = lax.broadcasted_iota(I32, (1, 1024), 1) + first
        here = pos.astype(F32)
        ahead = (pos + lag).astype(F32)
        behind = (pos - lag).astype(F32)
        cut = jnp.where((ends > here) & (ends <= ahead), 1.0, 0.0)
        cut_end = jnp.where((ends > behind) & (ends <= here), 1.0, 0.0)
        inside = jnp.where(behind >= 0.0, 1.0, 0.0)
        at = slice(rep * 1024, (rep + 1) * 1024)
        out_ref[0:1, at] = 1.0 - jnp.max(cut, axis=0, keepdims=True)
        out_ref[1:2, at] = (1.0 - jnp.max(cut_end, axis=0, keepdims=True)) * inside


def cov_kernel(lags_ref, mask_ref, left_ref, right_ref, out_ref):
    perm = one_hot(
        128,
        128,
        lambda r, c: c
        == (r >> 5) * 32 + ((r >> 1) & 1) * 16 + ((r >> 2) & 7) * 2 + (r & 1),
    )
    now = jnp.dot(perm, right_ref[...], preferred_element_type=F32)
    now_bf = now.astype(BF)
    tails = left_ref[:, 2048:].astype(F32)
    lagged = []
    for rep in range(2):
        tail = tails if rep == 1 else pltpu.roll(tails, 64, 1)
        block = left_ref[:, rep * 1024 : (rep + 1) * 1024].astype(F32)
        ext = jnp.concatenate([tail, block], axis=1)
        lagged.append(pltpu.roll(ext, lags_ref[rep] + 1024, 1)[:, :1024].astype(BF))
    lagged = jnp.concatenate(lagged, axis=1)
    keep, keep_end = mask_ref[0:1, :], mask_ref[1:2, :]
    left = left_ref[:, :2048]
    start_bf, end_bf = keep.astype(BF), keep_end.astype(BF)
    for m, lhs in enumerate((left * start_bf, lagged * end_bf, left * end_bf)):
        block = lax.dot_general(lhs, now_bf, NT, preferred_element_type=F32)
        for d in range(8):
            out_ref[d, m * 16 : (m + 1) * 16, :] = block[d * 16 : (d + 1) * 16, :]
    var = lax.dot_general(
        jnp.ones((8, 2048), F32), now * now * keep_end, NT, precision=HI, preferred_element_type=F32
    )
    for d in range(8):
        out_ref[d, 48:56, :] = var


def rows_kernel(parts_ref, out_ref):
    total = parts_ref[0]
    for d in range(1, 8):
        total = total + parts_ref[d]
    for f in range(8):
        for m in range(3):
            src = m * 16 + f * 2
            out_ref[f, m * 2 : m * 2 + 2, :] = total[src : src + 2, :]
        out_ref[f, 6:8, :] = total[48:50, :]


def final_kernel(scale, place_ref, parts_ref, ridge_ref, row_ref, cov_ref, score_ref):
    first = place_ref[1]
    ridge = ridge_ref[...]
    lane = lax.broadcasted_iota(I32, (2, 128), 1)
    row = lax.broadcasted_iota(I32, (2, 128), 0)
    diag = jnp.zeros((2, 1), F32)
    weighted = [jnp.zeros((32, 128), F32) for _ in range(2)]
    for f in range(8):
        total = parts_ref[f] * scale
        for m in range(3):
            cov_ref[m, :, f * 128 : (f + 1) * 128] = total[m * 2 : m * 2 + 2, :]
        own = lane + f * 128 == first + row
        diag = diag + jnp.sum(jnp.where(own, total[0:2, :], 0.0), axis=1, keepdims=True)
        inverse = 1.0 / (total[6:7, :] + ridge)
        for e in range(2):
            cross = total[2 + e : 3 + e, :]
            weighted[e] = weighted[e] + (cross * cross) * inverse
    ones = jnp.ones((8, 128), F32)
    pad = jnp.zeros((96, 128), F32)
    score = [
        lax.dot_general(
            ones,
            jnp.concatenate([w, pad], axis=0),
            NT,
            precision=HI,
            preferred_element_type=F32,
        )[0:1, :32]
        for w in weighted
    ]
    for e in range(2):
        score_ref[e : e + 1, :] = score[e] / (diag[e : e + 1, :] + row_ref[...])


def call(kernel, out, *args, smem=0, **kw):
    specs = [pl.BlockSpec(memory_space=pltpu.SMEM)] * smem
    specs += [pl.BlockSpec(memory_space=pltpu.VMEM)] * (len(args) - smem)
    shapes = [jax.ShapeDtypeStruct(*o) for o in out]
    outs = [pl.BlockSpec(memory_space=pltpu.VMEM)] * len(out)
    got = pl.pallas_call(
        kernel, out_shape=shapes, in_specs=specs, out_specs=outs, compiler_params=VMEM
    )(*args)
    return got[0] if len(out) == 1 else got


def all_to_all(x, axes):
    return lax.all_to_all(x, axes, split_axis=0, concat_axis=0, tiled=True)


def local(frames, panel_low, panel_high, lags, seg_lengths, ridge):
    z = lax.axis_index(Z).astype(I32)
    yl = lax.axis_index("yl").astype(I32)
    c = lax.axis_index("c").astype(I32)
    own_first = ((z * 2 + lax.axis_index("yh")) * 8 + lax.axis_index(FE)) * 4 + yl * 2
    place = jnp.stack([z, own_first.astype(I32), c])

    mine = jnp.concatenate([lags.reshape(1, 1), seg_lengths], axis=1)
    other = lax.ppermute(mine, "yl", [(0, 1), (1, 0)])

    halves = pl.pallas_call(
        halves_kernel,
        grid=(4,),
        out_shape=pltpu.HBM((4, 256, 1024), BF),
        in_specs=[pl.BlockSpec((1, 64, 2048), lambda i: (0, i, 0))],
        out_specs=pl.BlockSpec((4, 64, 1024), lambda i: (0, i, 0)),
        compiler_params=VMEM,
    )(pltpu.with_memory_space_constraint(frames, pltpu.HBM))
    frames_h = all_to_all(halves, ("yl", "yh")).reshape(1024, 1024)

    packed = call(
        pack_kernel, [((32, 1024), BF)], yl[None], panel_low.T, panel_high.T, smem=1
    )
    panel_own = lax.all_gather(packed, Z8, axis=0, tiled=True)
    panel_other = lax.ppermute(panel_own, "z0", [(0, 1), (1, 0)])
    both = jnp.where(
        yl == 0, jnp.concatenate([mine, other], axis=0), jnp.concatenate([other, mine], axis=0)
    )
    run_lags = both[:, 0]
    masks = call(mask_kernel, [((8, 2048), F32)], run_lags, place, both[:, 1:], smem=2)

    def project(panel):
        column = pl.BlockSpec((128, 256), lambda i: (0, i))
        keep, send = pl.pallas_call(
            project_kernel,
            grid=(4,),
            out_shape=[jax.ShapeDtypeStruct((128, 1024), BF)] * 2,
            in_specs=[
                pl.BlockSpec(memory_space=pltpu.SMEM),
                pl.BlockSpec((256, 1024), lambda i: (0, 0)),
                pl.BlockSpec((256, 1024), lambda i: (i, 0)),
            ],
            out_specs=[column, column],
            compiler_params=VMEM,
        )(place, panel, frames_h)
        return keep, lax.ppermute(send, "c", [(0, 1), (1, 0)])

    first = project(panel_own)
    panel_other, masks, run_lags, first = lax.optimization_barrier(
        (panel_other, masks, run_lags, first)
    )
    second = project(panel_other)
    pairs = call(join_kernel, [((4, 64, 1024), BF)], place, *first, *second, smem=1)
    parts = all_to_all(pairs.reshape(32, 8, 1024), ("z0", "yh", "yl", "x"))
    basis, tail, tiled = call(
        sum_kernel,
        [((16, 2048), BF), ((16, 128), BF), ((8, 16, 2048), BF)],
        parts.reshape(2, 2, 2, 4, 8, 1024),
    )

    before = lax.ppermute(tail, Z8, [(i, i + 1) for i in range(7)])
    right = all_to_all(tiled, ("z0", "yh", "yl"))
    left = lax.all_gather(jnp.concatenate([basis, before], axis=1), FE, axis=0, tiled=True)

    terms = call(
        cov_kernel,
        [((8, 56, 128), F32)],
        run_lags,
        masks,
        left,
        right.reshape(128, 2048),
        smem=1,
    )
    rows = call(rows_kernel, [((8, 8, 128), F32)], all_to_all(terms, Z8))
    by_row = all_to_all(rows, FE)
    return call(
        lambda *refs: final_kernel(1.0 / 16384.0, *refs),
        [((3, 2, 1024), F32), ((2, 32), F32)],
        place,
        by_row,
        ridge[:, None],
        ridge[None, :],
        smem=1,
    )


def solution(mesh):
    fine = Mesh(
        np.asarray(mesh.devices).reshape(2, 2, 2, 2, 2, 4, 2, 2),
        ("z3", "z2", "z1", "z0", "yh", "x", "c", "yl"),
    )
    tm = Z + ("yh",)
    in_specs = (P("yl", tm, FE), P(FE, tm), P(FE, tm), P("yl"), P("yl", None), P())
    rows = tm + FE + ("yl",)
    out_specs = (P(None, rows, None), P(rows, None))
    return jax.shard_map(local, mesh=fine, in_specs=in_specs, out_specs=out_specs, check_vma=False)
```

```python
import jax
import jax.numpy as jnp
import numpy as np
from jax import lax
from jax.experimental import pallas as pl
from jax.experimental.pallas import tpu as pltpu
from jax.sharding import Mesh, PartitionSpec as P

BF = jnp.bfloat16
F32 = jnp.float32
I32 = jnp.int32
HI = lax.Precision.HIGHEST
NT = (((1,), (1,)), ((), ()))
VMEM = pltpu.CompilerParams(vmem_limit_bytes=48 * 1024 * 1024)

Z = ("z3", "z2", "z1", "z0")
Z8 = ("z3", "z2", "z1")
FE = ("x", "c")


def one_hot(rows, cols, hit):
    r = lax.broadcasted_iota(I32, (rows, cols), 0)
    c = lax.broadcasted_iota(I32, (rows, cols), 1)
    return jnp.where(hit(r, c), 1.0, 0.0).astype(BF)


def pack_kernel(yl_ref, low_ref, high_ref, out_ref):
    off = pl.multiple_of(yl_ref[0] * 1024, 1024)
    src = one_hot(16, 16, lambda r, c: c == ((r >> 1) & 3) * 4 + (r >> 3) * 2 + (r & 1))
    for half, ref in enumerate((low_ref, high_ref)):
        rows = jnp.dot(src, ref[:, pl.ds(off, 1024)], preferred_element_type=F32)
        out_ref[half * 16 : half * 16 + 16, :] = rows.astype(BF)


def halves_kernel(lag_ref, seg_ref, frames_ref, out_ref, info_ref, sems):
    copies = []
    for i in range(4):
        half = frames_ref.at[0, :, pl.ds((i // 2) * 1024, 1024)]
        copies.append(pltpu.make_async_copy(half, out_ref.at[i, pl.ds(0, 256)], sems.at[i]))
    for copy in copies:
        copy.start()
    seg = jnp.concatenate([seg_ref[...], jnp.zeros((1, 64), I32)], axis=1)
    row = lax.broadcasted_iota(I32, (16, 128), 0)
    info = jnp.where(row == 0, seg >> 8, jnp.where(row == 1, seg & 255, lag_ref[0]))
    info_ref[:, :128] = info.astype(F32).astype(BF)
    info_ref[:, 128:] = jnp.zeros((16, 896), BF)
    for i in range(4):
        copy = pltpu.make_async_copy(info_ref, out_ref.at[i, pl.ds(256, 16)], sems.at[4 + i])
        copy.start()
        copies.append(copy)
    for copy in copies:
        copy.wait()


def project_kernel(place_ref, own_ref, other_ref, frames_ref, tails_ref, keep_ref, send_ref):
    own_yh = place_ref[0] & 1
    for t in range(5):
        frames = frames_ref[t, :256] if t < 4 else tails_ref[...]
        lanes = slice(t * 256, t * 256 + 256) if t < 4 else slice(1024, 1152)
        for yh, panel_ref in ((own_yh, own_ref), (1 - own_yh, other_ref)):
            acc = lax.dot_general(panel_ref[...], frames, NT, preferred_element_type=F32)

            def store(refs, acc=acc, yh=yh, lanes=lanes):
                for z1 in range(2):
                    for yl in range(2):
                        for half in range(2):
                            for z2 in range(2):
                                row = (z2 * 2 + z1) * 32 + half * 16 + yl * 8
                                both = jnp.concatenate(
                                    [acc[row : row + 8], acc[row + 128 : row + 136]], axis=0
                                )
                                at = (yl * 4 + half * 2) * 8
                                refs[z2][z1 * 2 + yh, at : at + 16, lanes] = both.astype(BF)

            pl.when(place_ref[2] == 0)(lambda store=store: store((keep_ref, send_ref)))
            pl.when(place_ref[2] == 1)(lambda store=store: store((send_ref, keep_ref)))


def sum_kernel(parts_ref, basis_ref, tiled_ref):
    for z0 in range(2):
        sums = []
        for yh in range(2):
            total = parts_ref[z0, yh, 0, 0].astype(F32)
            for i in range(1, 8):
                total = total + parts_ref[z0, yh, i // 4, i % 4].astype(F32)
            sums.append(total)
        basis = jnp.concatenate(sums, axis=0).astype(BF)
        for rep in range(2):
            at = rep * 1024 + z0 * 512
            block = basis[:, rep * 512 : (rep + 1) * 512]
            basis_ref[:, at : at + 512] = block
            for d in range(8):
                tiled_ref[d, :, at : at + 512] = block
        if z0 == 0:
            basis_ref[:, 2048:] = basis[:, 1024:]


def mask_kernel(place_ref, info_ref, out_ref):
    first = (place_ref[0] >> 1) * 1024
    tri = lax.broadcasted_iota(I32, (64, 64), 1) <= lax.broadcasted_iota(I32, (64, 64), 0)
    for rep in range(2):
        info = info_ref[rep].astype(F32)
        seg = info[0:1, :64] * 256.0 + info[1:2, :64]
        lag = info[2:3, 0:1]
        ends = jnp.sum(jnp.where(tri, seg, 0.0), axis=1, keepdims=True)
        here = (lax.broadcasted_iota(I32, (1, 1024), 1) + first).astype(F32)
        ahead = here + lag
        behind = here - lag
        cut = jnp.where((ends > here) & (ends <= ahead), 1.0, 0.0)
        cut_end = jnp.where((ends > behind) & (ends <= here), 1.0, 0.0)
        inside = jnp.where(behind >= 0.0, 1.0, 0.0)
        at = slice(rep * 1024, (rep + 1) * 1024)
        out_ref[0:1, at] = 1.0 - jnp.max(cut, axis=0, keepdims=True)
        out_ref[1:2, at] = (1.0 - jnp.max(cut_end, axis=0, keepdims=True)) * inside
        out_ref[2 + rep : 3 + rep, :] = jnp.broadcast_to(lag, (1, 2048))


def cov_kernel(mask_ref, left_ref, right_ref, out_ref):
    perm = one_hot(
        128,
        128,
        lambda r, c: c
        == (r >> 5) * 32 + ((r >> 1) & 1) * 16 + ((r >> 2) & 7) * 2 + (r & 1),
    )
    now = jnp.dot(perm, right_ref[...], preferred_element_type=F32)
    now_bf = now.astype(BF)
    lane = lax.broadcasted_iota(I32, (128, 128), 1)
    lagged = []
    for rep in range(2):
        lag = jnp.max(mask_ref[2 + rep : 3 + rep, :128]).astype(I32)
        tails = left_ref[:, 2048:].astype(F32)
        before = pltpu.roll(tails, lag if rep == 1 else lag + 64, 1)
        for j in range(8):
            at = rep * 1024 + j * 128
            block = pltpu.roll(left_ref[:, at : at + 128].astype(F32), lag, 1)
            lagged.append(jnp.where(lane < lag, before, block).astype(BF))
            before = block
    lagged = jnp.concatenate(lagged, axis=1)
    keep, keep_end = mask_ref[0:1, :], mask_ref[1:2, :]
    left = left_ref[:, :2048]
    start_bf, end_bf = keep.astype(BF), keep_end.astype(BF)
    for m, lhs in enumerate((left * start_bf, lagged * end_bf, left * end_bf)):
        block = lax.dot_general(lhs, now_bf, NT, preferred_element_type=F32)
        for d in range(8):
            out_ref[d, m * 16 : (m + 1) * 16, :] = block[d * 16 : (d + 1) * 16, :]
    var = lax.dot_general(
        jnp.ones((8, 2048), F32), now * now * keep_end, NT, precision=HI, preferred_element_type=F32
    )
    for d in range(8):
        out_ref[d, 48:56, :] = var


def rows_kernel(parts_ref, out_ref):
    total = parts_ref[0]
    for d in range(1, 8):
        total = total + parts_ref[d]
    for f in range(8):
        for m in range(3):
            src = m * 16 + f * 2
            out_ref[f, m * 2 : m * 2 + 2, :] = total[src : src + 2, :]
        out_ref[f, 6:8, :] = total[48:50, :]


def final_kernel(scale, place_ref, parts_ref, ridge_ref, row_ref, cov_ref, score_ref):
    first = place_ref[1]
    ridge = ridge_ref[...]
    lane = lax.broadcasted_iota(I32, (2, 128), 1)
    row = lax.broadcasted_iota(I32, (2, 128), 0)
    diag = jnp.zeros((2, 1), F32)
    weighted = [jnp.zeros((32, 128), F32) for _ in range(2)]
    for f in range(8):
        total = parts_ref[f] * scale
        for m in range(3):
            cov_ref[m, :, f * 128 : (f + 1) * 128] = total[m * 2 : m * 2 + 2, :]
        own = lane + f * 128 == first + row
        diag = diag + jnp.sum(jnp.where(own, total[0:2, :], 0.0), axis=1, keepdims=True)
        inverse = 1.0 / (total[6:7, :] + ridge)
        for e in range(2):
            cross = total[2 + e : 3 + e, :]
            weighted[e] = weighted[e] + (cross * cross) * inverse
    ones = jnp.ones((8, 128), F32)
    pad = jnp.zeros((96, 128), F32)
    score = [
        lax.dot_general(
            ones,
            jnp.concatenate([w, pad], axis=0),
            NT,
            precision=HI,
            preferred_element_type=F32,
        )[0:1, :32]
        for w in weighted
    ]
    for e in range(2):
        score_ref[e : e + 1, :] = score[e] / (diag[e : e + 1, :] + row_ref[...])


def call(kernel, out, *args, smem=0, **kw):
    specs = [pl.BlockSpec(memory_space=pltpu.SMEM)] * smem
    specs += [pl.BlockSpec(memory_space=pltpu.VMEM)] * (len(args) - smem)
    shapes = [jax.ShapeDtypeStruct(*o) for o in out]
    outs = [pl.BlockSpec(memory_space=pltpu.VMEM)] * len(out)
    got = pl.pallas_call(
        kernel, out_shape=shapes, in_specs=specs, out_specs=outs, compiler_params=VMEM
    )(*args)
    return got[0] if len(out) == 1 else got


def all_to_all(x, axes):
    return lax.all_to_all(x, axes, split_axis=0, concat_axis=0, tiled=True)


def local(frames, panel_low, panel_high, lags, seg_lengths, ridge):
    z = lax.axis_index(Z).astype(I32)
    yl = lax.axis_index("yl").astype(I32)
    c = lax.axis_index("c").astype(I32)
    own_first = ((z * 2 + lax.axis_index("yh")) * 8 + lax.axis_index(FE)) * 4 + yl * 2
    place = jnp.stack([z, own_first.astype(I32), c])

    halves = pl.pallas_call(
        halves_kernel,
        out_shape=pltpu.HBM((4, 272, 1024), BF),
        in_specs=[
            pl.BlockSpec(memory_space=pltpu.SMEM),
            pl.BlockSpec(memory_space=pltpu.VMEM),
            pl.BlockSpec(memory_space=pltpu.HBM),
        ],
        out_specs=pl.BlockSpec(memory_space=pltpu.HBM),
        scratch_shapes=[pltpu.VMEM((16, 1024), BF), pltpu.SemaphoreType.DMA((8,))],
        compiler_params=VMEM,
    )(lags, seg_lengths, pltpu.with_memory_space_constraint(frames, pltpu.HBM))
    frames_h = all_to_all(halves, ("yl", "yh"))

    packed = call(
        pack_kernel, [((32, 1024), BF)], yl[None], panel_low.T, panel_high.T, smem=1
    )
    panel_own = lax.all_gather(packed, Z8, axis=0, tiled=True)
    panel_other = lax.ppermute(panel_own, "z0", [(0, 1), (1, 0)])

    by_run = frames_h.reshape(2, 2, 272, 1024)
    tails = lax.ppermute(
        by_run[:, 1, 192:256].reshape(128, 1024), Z, [(i, i + 1) for i in range(1, 15, 2)]
    )
    masks = call(mask_kernel, [((8, 2048), F32)], place, by_run[:, 0, 256:, :128], smem=1)
    panel_other, masks = lax.optimization_barrier((panel_other, masks))

    keep, send = call(
        project_kernel,
        [((4, 64, 1152), BF)] * 2,
        place,
        panel_own,
        panel_other,
        frames_h,
        tails,
        smem=1,
    )
    got = lax.ppermute(send, "c", [(0, 1), (1, 0)])
    pairs = (keep.astype(F32) + got.astype(F32)).astype(BF)
    parts = all_to_all(pairs.reshape(32, 8, 1152), ("z0", "yh", "yl", "x"))
    basis, tiled = call(
        sum_kernel,
        [((16, 2176), BF), ((8, 16, 2048), BF)],
        parts.reshape(2, 2, 2, 4, 8, 1152),
    )

    right = all_to_all(tiled, ("z0", "yh", "yl"))
    left = lax.all_gather(basis, FE, axis=0, tiled=True)

    terms = call(
        cov_kernel, [((8, 56, 128), F32)], masks, left, right.reshape(128, 2048)
    )
    rows = call(rows_kernel, [((8, 8, 128), F32)], all_to_all(terms, Z8))
    by_row = all_to_all(rows, FE)
    return call(
        lambda *refs: final_kernel(1.0 / 16384.0, *refs),
        [((3, 2, 1024), F32), ((2, 32), F32)],
        place,
        by_row,
        ridge[:, None],
        ridge[None, :],
        smem=1,
    )


def solution(mesh):
    fine = Mesh(
        np.asarray(mesh.devices).reshape(2, 2, 2, 2, 2, 4, 2, 2),
        ("z3", "z2", "z1", "z0", "yh", "x", "c", "yl"),
    )
    tm = Z + ("yh",)
    in_specs = (P("yl", tm, FE), P(FE, tm), P(FE, tm), P("yl"), P("yl", None), P())
    rows = tm + FE + ("yl",)
    out_specs = (P(None, rows, None), P(rows, None))
    return jax.shard_map(local, mesh=fine, in_specs=in_specs, out_specs=out_specs, check_vma=False)
```

```python
import jax
import jax.numpy as jnp
import numpy as np
from jax import lax
from jax.experimental import pallas as pl
from jax.experimental.pallas import tpu as pltpu
from jax.sharding import Mesh, PartitionSpec as P

BF = jnp.bfloat16
F32 = jnp.float32
I32 = jnp.int32
HI = lax.Precision.HIGHEST
NT = (((1,), (1,)), ((), ()))
VMEM = pltpu.CompilerParams(vmem_limit_bytes=48 * 1024 * 1024)

Z = ("z3", "z2", "z1", "z0")
Z8 = ("z3", "z2", "z1")
FE = ("x", "c")


def one_hot(rows, cols, hit):
    r = lax.broadcasted_iota(I32, (rows, cols), 0)
    c = lax.broadcasted_iota(I32, (rows, cols), 1)
    return jnp.where(hit(r, c), 1.0, 0.0).astype(BF)


def pack_kernel(yl_ref, low_ref, high_ref, out_ref):
    off = pl.multiple_of(yl_ref[0] * 1024, 1024)
    src = one_hot(16, 16, lambda r, c: c == ((r >> 1) & 3) * 4 + (r >> 3) * 2 + (r & 1))
    for half, ref in enumerate((low_ref, high_ref)):
        rows = jnp.dot(src, ref[:, pl.ds(off, 1024)], preferred_element_type=F32)
        out_ref[half * 16 : half * 16 + 16, :] = rows.astype(BF)


def halves_kernel(lag_ref, seg_ref, frames_ref, out_ref, rows_ref, sems):
    loads = []
    for half in range(2):
        part = frames_ref.at[0, :, pl.ds(half * 1024, 1024)]
        load = pltpu.make_async_copy(part, rows_ref.at[half, pl.ds(0, 256)], sems.at[half])
        load.start()
        loads.append(load)
    seg = jnp.concatenate([seg_ref[...], jnp.zeros((1, 64), I32)], axis=1)
    row = lax.broadcasted_iota(I32, (16, 128), 0)
    info = jnp.where(row == 0, seg >> 8, jnp.where(row == 1, seg & 255, lag_ref[0]))
    stores = []
    for half in range(2):
        rows_ref[half, 256:, :128] = info.astype(F32).astype(BF)
        rows_ref[half, 256:, 128:] = jnp.zeros((16, 896), BF)
        loads[half].wait()
        for i in (half * 2, half * 2 + 1):
            store = pltpu.make_async_copy(rows_ref.at[half], out_ref.at[i], sems.at[2 + i])
            store.start()
            stores.append(store)
    for store in stores:
        store.wait()


def project_kernel(
    place_ref, own_ref, other_ref, frames_ref, tails_ref, keep_ref, send_ref, panel_ref
):
    own_yh = place_ref[0] & 1
    c = place_ref[2]
    for kind in range(2):
        z2 = c if kind == 0 else 1 - c
        for yh, ref in ((own_yh, own_ref), (1 - own_yh, other_ref)):
            for z3 in range(2):
                src = pl.multiple_of(z3 * 128 + z2 * 64, 64)
                dst = pl.multiple_of(kind * 256 + yh * 128 + z3 * 64, 64)
                panel_ref[pl.ds(dst, 64), :] = ref[pl.ds(src, 64), :]
    panel = panel_ref[...]
    for t in range(5):
        frames = frames_ref[t, :256] if t < 4 else tails_ref[...]
        lanes = slice(t * 256, t * 256 + 256) if t < 4 else slice(1024, 1152)
        acc = lax.dot_general(panel, frames, NT, preferred_element_type=F32)
        for kind, ref in enumerate((keep_ref, send_ref)):
            for yh in range(2):
                for z1 in range(2):
                    for half in range(2):
                        for yl in range(2):
                            row = kind * 256 + yh * 128 + z1 * 32 + half * 16 + yl * 8
                            both = jnp.concatenate(
                                [acc[row : row + 8], acc[row + 64 : row + 72]], axis=0
                            )
                            at = (yl * 4 + half * 2) * 8
                            ref[z1 * 2 + yh, at : at + 16, lanes] = both.astype(BF)


def sum_kernel(parts_ref, basis_ref, tiled_ref):
    for z0 in range(2):
        sums = []
        for yh in range(2):
            total = parts_ref[z0, yh, 0, 0].astype(F32)
            for i in range(1, 8):
                total = total + parts_ref[z0, yh, i // 4, i % 4].astype(F32)
            sums.append(total)
        basis = jnp.concatenate(sums, axis=0).astype(BF)
        for rep in range(2):
            at = rep * 1024 + z0 * 512
            block = basis[:, rep * 512 : (rep + 1) * 512]
            basis_ref[:, at : at + 512] = block
            for d in range(8):
                tiled_ref[d, :, at : at + 512] = block
        if z0 == 0:
            basis_ref[:, 2048:] = basis[:, 1024:]


def mask_kernel(place_ref, info_ref, out_ref):
    first = (place_ref[0] >> 1) * 1024
    tri = lax.broadcasted_iota(I32, (64, 64), 1) <= lax.broadcasted_iota(I32, (64, 64), 0)
    for rep in range(2):
        info = info_ref[rep].astype(F32)
        seg = info[0:1, :64] * 256.0 + info[1:2, :64]
        lag = info[2:3, 0:1]
        ends = jnp.sum(jnp.where(tri, seg, 0.0), axis=1, keepdims=True)
        here = (lax.broadcasted_iota(I32, (1, 1024), 1) + first).astype(F32)
        ahead = here + lag
        behind = here - lag
        cut = jnp.where((ends > here) & (ends <= ahead), 1.0, 0.0)
        cut_end = jnp.where((ends > behind) & (ends <= here), 1.0, 0.0)
        inside = jnp.where(behind >= 0.0, 1.0, 0.0)
        at = slice(rep * 1024, (rep + 1) * 1024)
        out_ref[0:1, at] = 1.0 - jnp.max(cut, axis=0, keepdims=True)
        out_ref[1:2, at] = (1.0 - jnp.max(cut_end, axis=0, keepdims=True)) * inside
        out_ref[2 + rep : 3 + rep, :] = jnp.broadcast_to(lag, (1, 2048))


def cov_kernel(mask_ref, left_ref, right_ref, out_ref):
    perm = one_hot(
        128,
        128,
        lambda r, c: c
        == (r >> 5) * 32 + ((r >> 1) & 1) * 16 + ((r >> 2) & 7) * 2 + (r & 1),
    )
    now = jnp.dot(perm, right_ref[...], preferred_element_type=F32)
    now_bf = now.astype(BF)
    lane = lax.broadcasted_iota(I32, (128, 128), 1)
    lagged = []
    for rep in range(2):
        lag = jnp.max(mask_ref[2 + rep : 3 + rep, :128]).astype(I32)
        tails = left_ref[:, 2048:].astype(F32)
        before = pltpu.roll(tails, lag if rep == 1 else lag + 64, 1)
        for j in range(8):
            at = rep * 1024 + j * 128
            block = pltpu.roll(left_ref[:, at : at + 128].astype(F32), lag, 1)
            lagged.append(jnp.where(lane < lag, before, block).astype(BF))
            before = block
    lagged = jnp.concatenate(lagged, axis=1)
    keep, keep_end = mask_ref[0:1, :], mask_ref[1:2, :]
    left = left_ref[:, :2048]
    start_bf, end_bf = keep.astype(BF), keep_end.astype(BF)
    for m, lhs in enumerate((left * start_bf, lagged * end_bf, left * end_bf)):
        block = lax.dot_general(lhs, now_bf, NT, preferred_element_type=F32)
        for d in range(8):
            out_ref[d, m * 16 : (m + 1) * 16, :] = block[d * 16 : (d + 1) * 16, :]
    var = lax.dot_general(
        jnp.ones((8, 2048), F32), now * now * keep_end, NT, precision=HI, preferred_element_type=F32
    )
    for d in range(8):
        out_ref[d, 48:56, :] = var


def rows_kernel(parts_ref, out_ref):
    total = parts_ref[0]
    for d in range(1, 8):
        total = total + parts_ref[d]
    for f in range(8):
        for m in range(3):
            src = m * 16 + f * 2
            out_ref[f, m * 2 : m * 2 + 2, :] = total[src : src + 2, :]
        out_ref[f, 6:8, :] = total[48:50, :]


def final_kernel(scale, place_ref, parts_ref, ridge_ref, row_ref, cov_ref, score_ref):
    first = place_ref[1]
    ridge = ridge_ref[...]
    lane = lax.broadcasted_iota(I32, (2, 128), 1)
    row = lax.broadcasted_iota(I32, (2, 128), 0)
    diag = jnp.zeros((2, 1), F32)
    weighted = [jnp.zeros((32, 128), F32) for _ in range(2)]
    for f in range(8):
        total = parts_ref[f] * scale
        for m in range(3):
            cov_ref[m, :, f * 128 : (f + 1) * 128] = total[m * 2 : m * 2 + 2, :]
        own = lane + f * 128 == first + row
        diag = diag + jnp.sum(jnp.where(own, total[0:2, :], 0.0), axis=1, keepdims=True)
        inverse = 1.0 / (total[6:7, :] + ridge)
        for e in range(2):
            cross = total[2 + e : 3 + e, :]
            weighted[e] = weighted[e] + (cross * cross) * inverse
    ones = jnp.ones((8, 128), F32)
    pad = jnp.zeros((96, 128), F32)
    score = [
        lax.dot_general(
            ones,
            jnp.concatenate([w, pad], axis=0),
            NT,
            precision=HI,
            preferred_element_type=F32,
        )[0:1, :32]
        for w in weighted
    ]
    for e in range(2):
        score_ref[e : e + 1, :] = score[e] / (diag[e : e + 1, :] + row_ref[...])


def call(kernel, out, *args, smem=0, scratch=()):
    specs = [pl.BlockSpec(memory_space=pltpu.SMEM)] * smem
    specs += [pl.BlockSpec(memory_space=pltpu.VMEM)] * (len(args) - smem)
    shapes = [jax.ShapeDtypeStruct(*o) for o in out]
    outs = [pl.BlockSpec(memory_space=pltpu.VMEM)] * len(out)
    got = pl.pallas_call(
        kernel,
        out_shape=shapes,
        in_specs=specs,
        out_specs=outs,
        scratch_shapes=scratch,
        compiler_params=VMEM,
    )(*args)
    return got[0] if len(out) == 1 else got


def all_to_all(x, axes):
    return lax.all_to_all(x, axes, split_axis=0, concat_axis=0, tiled=True)


def local(frames, panel_low, panel_high, lags, seg_lengths, ridge):
    z = lax.axis_index(Z).astype(I32)
    yl = lax.axis_index("yl").astype(I32)
    c = lax.axis_index("c").astype(I32)
    own_first = ((z * 2 + lax.axis_index("yh")) * 8 + lax.axis_index(FE)) * 4 + yl * 2
    place = jnp.stack([z, own_first.astype(I32), c])

    halves = pl.pallas_call(
        halves_kernel,
        out_shape=pltpu.HBM((4, 272, 1024), BF),
        in_specs=[
            pl.BlockSpec(memory_space=pltpu.SMEM),
            pl.BlockSpec(memory_space=pltpu.VMEM),
            pl.BlockSpec(memory_space=pltpu.HBM),
        ],
        out_specs=pl.BlockSpec(memory_space=pltpu.HBM),
        scratch_shapes=[pltpu.VMEM((2, 272, 1024), BF), pltpu.SemaphoreType.DMA((6,))],
        compiler_params=VMEM,
    )(lags, seg_lengths, pltpu.with_memory_space_constraint(frames, pltpu.HBM))
    frames_h = all_to_all(halves, ("yl", "yh"))

    packed = call(
        pack_kernel, [((32, 1024), BF)], yl[None], panel_low.T, panel_high.T, smem=1
    )
    panel_own = lax.all_gather(packed, Z8, axis=0, tiled=True)
    panel_other = lax.ppermute(panel_own, "z0", [(0, 1), (1, 0)])

    by_run = frames_h.reshape(2, 2, 272, 1024)
    tails = lax.ppermute(
        by_run[:, 1, 192:256].reshape(128, 1024), Z, [(i, i + 1) for i in range(1, 15, 2)]
    )
    masks = call(mask_kernel, [((8, 2048), F32)], place, by_run[:, 0, 256:, :128], smem=1)
    panel_other, masks = lax.optimization_barrier((panel_other, masks))

    keep, send = call(
        project_kernel,
        [((4, 64, 1152), BF)] * 2,
        place,
        panel_own,
        panel_other,
        frames_h,
        tails,
        smem=1,
        scratch=[pltpu.VMEM((512, 1024), BF)],
    )
    got = lax.ppermute(send, "c", [(0, 1), (1, 0)])
    pairs = (keep.astype(F32) + got.astype(F32)).astype(BF)
    parts = all_to_all(pairs.reshape(32, 8, 1152), ("z0", "yh", "yl", "x"))
    basis, tiled = call(
        sum_kernel,
        [((16, 2176), BF), ((8, 16, 2048), BF)],
        parts.reshape(2, 2, 2, 4, 8, 1152),
    )

    right = all_to_all(tiled, ("z0", "yh", "yl"))
    left = lax.all_gather(basis, FE, axis=0, tiled=True)

    terms = call(
        cov_kernel, [((8, 56, 128), F32)], masks, left, right.reshape(128, 2048)
    )
    rows = call(rows_kernel, [((8, 8, 128), F32)], all_to_all(terms, Z8))
    by_row = all_to_all(rows, FE)
    return call(
        lambda *refs: final_kernel(1.0 / 16384.0, *refs),
        [((3, 2, 1024), F32), ((2, 32), F32)],
        place,
        by_row,
        ridge[:, None],
        ridge[None, :],
        smem=1,
    )


def solution(mesh):
    fine = Mesh(
        np.asarray(mesh.devices).reshape(2, 2, 2, 2, 2, 4, 2, 2),
        ("z3", "z2", "z1", "z0", "yh", "x", "c", "yl"),
    )
    tm = Z + ("yh",)
    in_specs = (P("yl", tm, FE), P(FE, tm), P(FE, tm), P("yl"), P("yl", None), P())
    rows = tm + FE + ("yl",)
    out_specs = (P(None, rows, None), P(rows, None))
    return jax.shard_map(local, mesh=fine, in_specs=in_specs, out_specs=out_specs, check_vma=False)
```

```python
import jax
import jax.numpy as jnp
import numpy as np
from jax import lax
from jax.experimental import pallas as pl
from jax.experimental.pallas import tpu as pltpu
from jax.sharding import Mesh, PartitionSpec as P

BF = jnp.bfloat16
F32 = jnp.float32
I32 = jnp.int32
HI = lax.Precision.HIGHEST
NT = (((1,), (1,)), ((), ()))
VMEM = pltpu.CompilerParams(vmem_limit_bytes=48 * 1024 * 1024)

Z = ("z3", "z2", "z1", "z0")
Z8 = ("z3", "z2", "z1")
FE = ("x", "c")


def one_hot(rows, cols, hit):
    r = lax.broadcasted_iota(I32, (rows, cols), 0)
    c = lax.broadcasted_iota(I32, (rows, cols), 1)
    return jnp.where(hit(r, c), 1.0, 0.0).astype(BF)


def pack_kernel(yl_ref, low_ref, high_ref, out_ref):
    off = pl.multiple_of(yl_ref[0] * 1024, 1024)
    src = one_hot(16, 16, lambda r, c: c == ((r >> 1) & 3) * 4 + (r >> 3) * 2 + (r & 1))
    for half, ref in enumerate((low_ref, high_ref)):
        rows = jnp.dot(src, ref[:, pl.ds(off, 1024)], preferred_element_type=F32)
        out_ref[half * 16 : half * 16 + 16, :] = rows.astype(BF)


def halves_kernel(lag_ref, seg_hbm, frames_ref, out_ref, rows_ref, seg_ref, sems):
    seg_load = pltpu.make_async_copy(seg_hbm, seg_ref, sems.at[6])
    seg_load.start()
    loads = []
    for half in range(2):
        part = frames_ref.at[0, :, pl.ds(half * 1024, 1024)]
        load = pltpu.make_async_copy(part, rows_ref.at[half, pl.ds(0, 256)], sems.at[half])
        load.start()
        loads.append(load)
    seg_load.wait()
    seg = jnp.concatenate([seg_ref[...], jnp.zeros((1, 64), I32)], axis=1)
    row = lax.broadcasted_iota(I32, (16, 128), 0)
    info = jnp.where(row == 0, seg >> 8, jnp.where(row == 1, seg & 255, lag_ref[0]))
    stores = []
    for half in range(2):
        rows_ref[half, 256:, :128] = info.astype(F32).astype(BF)
        rows_ref[half, 256:, 128:] = jnp.zeros((16, 896), BF)
        loads[half].wait()
        for i in (half * 2, half * 2 + 1):
            store = pltpu.make_async_copy(rows_ref.at[half], out_ref.at[i], sems.at[2 + i])
            store.start()
            stores.append(store)
    for store in stores:
        store.wait()


def project_kernel(
    place_ref, own_ref, other_ref, frames_ref, tails_ref, keep_ref, send_ref, panel_ref
):
    own_yh = place_ref[0] & 1
    c = place_ref[2]
    for kind in range(2):
        z2 = c if kind == 0 else 1 - c
        for yh, ref in ((own_yh, own_ref), (1 - own_yh, other_ref)):
            for z3 in range(2):
                src = pl.multiple_of(z3 * 128 + z2 * 64, 64)
                dst = pl.multiple_of(kind * 256 + yh * 128 + z3 * 64, 64)
                panel_ref[pl.ds(dst, 64), :] = ref[pl.ds(src, 64), :]
    panel = panel_ref[...]
    for t in range(5):
        frames = frames_ref[t, :256] if t < 4 else tails_ref[...]
        lanes = slice(t * 256, t * 256 + 256) if t < 4 else slice(1024, 1152)
        acc = lax.dot_general(panel, frames, NT, preferred_element_type=F32)
        for kind, ref in enumerate((keep_ref, send_ref)):
            for yh in range(2):
                for z1 in range(2):
                    for half in range(2):
                        for yl in range(2):
                            row = kind * 256 + yh * 128 + z1 * 32 + half * 16 + yl * 8
                            both = jnp.concatenate(
                                [acc[row : row + 8], acc[row + 64 : row + 72]], axis=0
                            )
                            at = (yl * 4 + half * 2) * 8
                            ref[z1 * 2 + yh, at : at + 16, lanes] = both.astype(BF)


def sum_kernel(parts_ref, basis_ref, tiled_ref):
    for z0 in range(2):
        sums = []
        for yh in range(2):
            total = parts_ref[z0, yh, 0, 0].astype(F32)
            for i in range(1, 8):
                total = total + parts_ref[z0, yh, i // 4, i % 4].astype(F32)
            sums.append(total)
        basis = jnp.concatenate(sums, axis=0).astype(BF)
        for rep in range(2):
            at = rep * 1024 + z0 * 512
            block = basis[:, rep * 512 : (rep + 1) * 512]
            basis_ref[:, at : at + 512] = block
            for d in range(8):
                tiled_ref[d, :, at : at + 512] = block
        if z0 == 0:
            basis_ref[:, 2048:] = basis[:, 1024:]


def mask_kernel(place_ref, info_ref, out_ref):
    first = (place_ref[0] >> 1) * 1024
    tri = lax.broadcasted_iota(I32, (64, 64), 1) <= lax.broadcasted_iota(I32, (64, 64), 0)
    for rep in range(2):
        info = info_ref[rep].astype(F32)
        seg = info[0:1, :64] * 256.0 + info[1:2, :64]
        lag = info[2:3, 0:1]
        ends = jnp.sum(jnp.where(tri, seg, 0.0), axis=1, keepdims=True)
        here = (lax.broadcasted_iota(I32, (1, 1024), 1) + first).astype(F32)
        ahead = here + lag
        behind = here - lag
        cut = jnp.where((ends > here) & (ends <= ahead), 1.0, 0.0)
        cut_end = jnp.where((ends > behind) & (ends <= here), 1.0, 0.0)
        inside = jnp.where(behind >= 0.0, 1.0, 0.0)
        at = slice(rep * 1024, (rep + 1) * 1024)
        out_ref[0:1, at] = 1.0 - jnp.max(cut, axis=0, keepdims=True)
        out_ref[1:2, at] = (1.0 - jnp.max(cut_end, axis=0, keepdims=True)) * inside
        out_ref[2 + rep : 3 + rep, :] = jnp.broadcast_to(lag, (1, 2048))


def cov_kernel(mask_ref, left_ref, right_ref, out_ref):
    perm = one_hot(
        128,
        128,
        lambda r, c: c
        == (r >> 5) * 32 + ((r >> 1) & 1) * 16 + ((r >> 2) & 7) * 2 + (r & 1),
    )
    now = jnp.dot(perm, right_ref[...], preferred_element_type=F32)
    now_bf = now.astype(BF)
    lane = lax.broadcasted_iota(I32, (128, 128), 1)
    lagged = []
    for rep in range(2):
        lag = jnp.max(mask_ref[2 + rep : 3 + rep, :128]).astype(I32)
        tails = left_ref[:, 2048:].astype(F32)
        before = pltpu.roll(tails, lag if rep == 1 else lag + 64, 1)
        for j in range(8):
            at = rep * 1024 + j * 128
            block = pltpu.roll(left_ref[:, at : at + 128].astype(F32), lag, 1)
            lagged.append(jnp.where(lane < lag, before, block).astype(BF))
            before = block
    lagged = jnp.concatenate(lagged, axis=1)
    keep, keep_end = mask_ref[0:1, :], mask_ref[1:2, :]
    left = left_ref[:, :2048]
    start_bf, end_bf = keep.astype(BF), keep_end.astype(BF)
    for m, lhs in enumerate((left * start_bf, lagged * end_bf, left * end_bf)):
        block = lax.dot_general(lhs, now_bf, NT, preferred_element_type=F32)
        for d in range(8):
            out_ref[d % 2, d // 2, m * 16 : (m + 1) * 16, :] = block[d * 16 : (d + 1) * 16, :]
    var = lax.dot_general(
        jnp.ones((8, 2048), F32), now * now * keep_end, NT, precision=HI, preferred_element_type=F32
    )
    for d in range(8):
        out_ref[d % 2, d // 2, 48:56, :] = var


def rows_kernel(parts_ref, out_ref):
    for d in range(4):
        total = parts_ref[0, d] + parts_ref[1, d]
        for f in range(8):
            for m in range(3):
                src = m * 16 + f * 2
                out_ref[d, f, m * 2 : m * 2 + 2, :] = total[src : src + 2, :]
            out_ref[d, f, 6:8, :] = total[48:50, :]


def final_kernel(scale, place_ref, parts_ref, ridge_ref, row_ref, cov_ref, score_ref):
    first = place_ref[1]
    ridge = ridge_ref[...]
    lane = lax.broadcasted_iota(I32, (2, 128), 1)
    row = lax.broadcasted_iota(I32, (2, 128), 0)
    diag = jnp.zeros((2, 1), F32)
    weighted = [jnp.zeros((32, 128), F32) for _ in range(2)]
    for f in range(8):
        total = (parts_ref[0, f] + parts_ref[1, f]) + (parts_ref[2, f] + parts_ref[3, f])
        total = total * scale
        for m in range(3):
            cov_ref[m, :, f * 128 : (f + 1) * 128] = total[m * 2 : m * 2 + 2, :]
        own = lane + f * 128 == first + row
        diag = diag + jnp.sum(jnp.where(own, total[0:2, :], 0.0), axis=1, keepdims=True)
        inverse = 1.0 / (total[6:7, :] + ridge)
        for e in range(2):
            cross = total[2 + e : 3 + e, :]
            weighted[e] = weighted[e] + (cross * cross) * inverse
    ones = jnp.ones((8, 128), F32)
    pad = jnp.zeros((96, 128), F32)
    score = [
        lax.dot_general(
            ones,
            jnp.concatenate([w, pad], axis=0),
            NT,
            precision=HI,
            preferred_element_type=F32,
        )[0:1, :32]
        for w in weighted
    ]
    for e in range(2):
        score_ref[e : e + 1, :] = score[e] / (diag[e : e + 1, :] + row_ref[...])


def call(kernel, out, *args, smem=0, scratch=()):
    specs = [pl.BlockSpec(memory_space=pltpu.SMEM)] * smem
    specs += [pl.BlockSpec(memory_space=pltpu.VMEM)] * (len(args) - smem)
    shapes = [jax.ShapeDtypeStruct(*o) for o in out]
    outs = [pl.BlockSpec(memory_space=pltpu.VMEM)] * len(out)
    got = pl.pallas_call(
        kernel,
        out_shape=shapes,
        in_specs=specs,
        out_specs=outs,
        scratch_shapes=scratch,
        compiler_params=VMEM,
    )(*args)
    return got[0] if len(out) == 1 else got


def all_to_all(x, axes):
    return lax.all_to_all(x, axes, split_axis=0, concat_axis=0, tiled=True)


def local(frames, panel_low, panel_high, lags, seg_lengths, ridge):
    z = lax.axis_index(Z).astype(I32)
    yl = lax.axis_index("yl").astype(I32)
    c = lax.axis_index("c").astype(I32)
    own_first = ((z * 2 + lax.axis_index("yh")) * 8 + lax.axis_index(FE)) * 4 + yl * 2
    place = jnp.stack([z, own_first.astype(I32), c])

    halves = pl.pallas_call(
        halves_kernel,
        out_shape=pltpu.HBM((4, 272, 1024), BF),
        in_specs=[
            pl.BlockSpec(memory_space=pltpu.SMEM),
            pl.BlockSpec(memory_space=pltpu.HBM),
            pl.BlockSpec(memory_space=pltpu.HBM),
        ],
        out_specs=pl.BlockSpec(memory_space=pltpu.HBM),
        scratch_shapes=[
            pltpu.VMEM((2, 272, 1024), BF),
            pltpu.VMEM((1, 64), I32),
            pltpu.SemaphoreType.DMA((7,)),
        ],
        compiler_params=VMEM,
    )(
        lags,
        pltpu.with_memory_space_constraint(seg_lengths, pltpu.HBM),
        pltpu.with_memory_space_constraint(frames, pltpu.HBM),
    )
    frames_h = all_to_all(halves, ("yl", "yh"))

    packed = call(
        pack_kernel, [((32, 1024), BF)], yl[None], panel_low.T, panel_high.T, smem=1
    )
    panel_own = lax.all_gather(packed, Z8, axis=0, tiled=True)
    panel_other = lax.ppermute(panel_own, "z0", [(0, 1), (1, 0)])

    by_run = frames_h.reshape(2, 2, 272, 1024)
    tails = lax.ppermute(
        by_run[:, 1, 192:256].reshape(128, 1024), Z, [(i, i + 1) for i in range(1, 15, 2)]
    )
    masks = call(mask_kernel, [((8, 2048), F32)], place, by_run[:, 0, 256:, :128], smem=1)
    panel_other, masks = lax.optimization_barrier((panel_other, masks))

    keep, send = call(
        project_kernel,
        [((4, 64, 1152), BF)] * 2,
        place,
        panel_own,
        panel_other,
        frames_h,
        tails,
        smem=1,
        scratch=[pltpu.VMEM((512, 1024), BF)],
    )
    got = lax.ppermute(send, "c", [(0, 1), (1, 0)])
    pairs = (keep.astype(F32) + got.astype(F32)).astype(BF)
    parts = all_to_all(pairs.reshape(32, 8, 1152), ("z0", "yh", "yl", "x"))
    basis, tiled = call(
        sum_kernel,
        [((16, 2176), BF), ((8, 16, 2048), BF)],
        parts.reshape(2, 2, 2, 4, 8, 1152),
    )

    right = all_to_all(tiled, ("z0", "yh", "yl"))
    left = lax.all_gather(basis, FE, axis=0, tiled=True)

    terms = call(
        cov_kernel, [((2, 4, 56, 128), F32)], masks, left, right.reshape(128, 2048)
    )
    rows = call(rows_kernel, [((4, 8, 8, 128), F32)], all_to_all(terms, "z1"))
    by_row = all_to_all(rows.reshape(32, 8, 128), ("z3", "z2") + FE)
    return call(
        lambda *refs: final_kernel(1.0 / 16384.0, *refs),
        [((3, 2, 1024), F32), ((2, 32), F32)],
        place,
        by_row.reshape(4, 8, 8, 128),
        ridge[:, None],
        ridge[None, :],
        smem=1,
    )


def solution(mesh):
    fine = Mesh(
        np.asarray(mesh.devices).reshape(2, 2, 2, 2, 2, 4, 2, 2),
        ("z3", "z2", "z1", "z0", "yh", "x", "c", "yl"),
    )
    tm = Z + ("yh",)
    in_specs = (P("yl", tm, FE), P(FE, tm), P(FE, tm), P("yl"), P("yl", None), P())
    rows = tm + FE + ("yl",)
    out_specs = (P(None, rows, None), P(rows, None))
    return jax.shard_map(local, mesh=fine, in_specs=in_specs, out_specs=out_specs, check_vma=False)
```

```python
import jax
import jax.numpy as jnp
import numpy as np
from jax import lax
from jax.experimental import pallas as pl
from jax.experimental.pallas import tpu as pltpu
from jax.sharding import Mesh, PartitionSpec as P

BF = jnp.bfloat16
F32 = jnp.float32
I32 = jnp.int32
HI = lax.Precision.HIGHEST
NT = (((1,), (1,)), ((), ()))
VMEM = pltpu.CompilerParams(vmem_limit_bytes=48 * 1024 * 1024)

Z = ("z3", "z2", "z1", "z0")
Z8 = ("z3", "z2", "z1")
FE = ("x", "c")
PLANE = ("yl", "x", "yh", "z0")
RIGHT = ("yl", "z0", "yh")
FAR = ("z2", "z3", "z1")


def one_hot(rows, cols, hit):
    r = lax.broadcasted_iota(I32, (rows, cols), 0)
    c = lax.broadcasted_iota(I32, (rows, cols), 1)
    return jnp.where(hit(r, c), 1.0, 0.0).astype(BF)


def pack_kernel(yl_ref, low_ref, high_ref, out_ref):
    off = pl.multiple_of(yl_ref[0] * 1024, 1024)
    src = one_hot(16, 16, lambda r, c: c == ((r >> 1) & 3) * 4 + (r >> 3) * 2 + (r & 1))
    for half, ref in enumerate((low_ref, high_ref)):
        rows = jnp.dot(src, ref[:, pl.ds(off, 1024)], preferred_element_type=F32)
        out_ref[half * 16 : half * 16 + 16, :] = rows.astype(BF)


def halves_kernel(lag_ref, seg_hbm, frames_ref, out_ref, rows_ref, seg_ref, sems):
    seg_load = pltpu.make_async_copy(seg_hbm, seg_ref, sems.at[6])
    seg_load.start()
    loads = []
    for half in range(2):
        part = frames_ref.at[0, :, pl.ds(half * 1024, 1024)]
        load = pltpu.make_async_copy(part, rows_ref.at[half, pl.ds(0, 256)], sems.at[half])
        load.start()
        loads.append(load)
    seg_load.wait()
    seg = jnp.concatenate([seg_ref[...], jnp.zeros((1, 64), I32)], axis=1)
    row = lax.broadcasted_iota(I32, (16, 128), 0)
    info = jnp.where(row == 0, seg >> 8, jnp.where(row == 1, seg & 255, lag_ref[0]))
    stores = []
    for half in range(2):
        rows_ref[half, 256:, :128] = info.astype(F32).astype(BF)
        rows_ref[half, 256:, 128:] = jnp.zeros((16, 896), BF)
        loads[half].wait()
        for i in (half * 2, half * 2 + 1):
            store = pltpu.make_async_copy(rows_ref.at[half], out_ref.at[i], sems.at[2 + i])
            store.start()
            stores.append(store)
    for store in stores:
        store.wait()


def project_kernel(
    place_ref, own_ref, other_ref, frames_ref, tails_ref, keep_ref, send_ref, panel_ref
):
    own_yh = place_ref[0] & 1
    c = place_ref[2]
    for kind in range(2):
        z2 = c if kind == 0 else 1 - c
        for yh, ref in ((own_yh, own_ref), (1 - own_yh, other_ref)):
            for z3 in range(2):
                src = pl.multiple_of(z3 * 128 + z2 * 64, 64)
                dst = pl.multiple_of(kind * 256 + yh * 128 + z3 * 64, 64)
                panel_ref[pl.ds(dst, 64), :] = ref[pl.ds(src, 64), :]
    panel = panel_ref[...]
    for t in range(5):
        frames = frames_ref[t, :256] if t < 4 else tails_ref[...]
        lanes = slice(t * 256, t * 256 + 256) if t < 4 else slice(1024, 1152)
        acc = lax.dot_general(panel, frames, NT, preferred_element_type=F32)
        for kind, ref in enumerate((keep_ref, send_ref)):
            for yh in range(2):
                for z3 in range(2):
                    for half in range(2):
                        for yl in range(2):
                            row = kind * 256 + yh * 128 + z3 * 64 + half * 16 + yl * 8
                            both = jnp.concatenate(
                                [acc[row : row + 8], acc[row + 32 : row + 40]], axis=0
                            )
                            at = ((yl * 4 + half * 2 + z3) * 2 + yh) * 16
                            ref[at : at + 16, lanes] = both.astype(BF)


def sum_kernel(parts_ref, basis_ref, tiled_ref):
    for z0 in range(2):
        sums = []
        for yh in range(2):
            total = parts_ref[0, 0, yh, z0].astype(F32)
            for i in range(1, 8):
                total = total + parts_ref[i // 4, i % 4, yh, z0].astype(F32)
            sums.append(total)
        basis = jnp.concatenate(sums, axis=0).astype(BF)
        for rep in range(2):
            at = rep * 1024 + z0 * 512
            block = basis[:, rep * 512 : (rep + 1) * 512]
            basis_ref[:, at : at + 512] = block
            for d in range(8):
                tiled_ref[d, :, at : at + 512] = block
        if z0 == 0:
            basis_ref[:, 2048:] = basis[:, 1024:]


def mask_kernel(place_ref, info_ref, out_ref):
    first = (place_ref[0] >> 1) * 1024
    tri = lax.broadcasted_iota(I32, (64, 64), 1) <= lax.broadcasted_iota(I32, (64, 64), 0)
    for rep in range(2):
        info = info_ref[rep].astype(F32)
        seg = info[0:1, :64] * 256.0 + info[1:2, :64]
        lag = info[2:3, 0:1]
        ends = jnp.sum(jnp.where(tri, seg, 0.0), axis=1, keepdims=True)
        here = (lax.broadcasted_iota(I32, (1, 1024), 1) + first).astype(F32)
        ahead = here + lag
        behind = here - lag
        cut = jnp.where((ends > here) & (ends <= ahead), 1.0, 0.0)
        cut_end = jnp.where((ends > behind) & (ends <= here), 1.0, 0.0)
        inside = jnp.where(behind >= 0.0, 1.0, 0.0)
        at = slice(rep * 1024, (rep + 1) * 1024)
        out_ref[0:1, at] = 1.0 - jnp.max(cut, axis=0, keepdims=True)
        out_ref[1:2, at] = (1.0 - jnp.max(cut_end, axis=0, keepdims=True)) * inside
        out_ref[2 + rep : 3 + rep, :] = jnp.broadcast_to(lag, (1, 2048))


def cov_kernel(mask_ref, left_ref, right_ref, out_ref):
    perm = one_hot(
        128,
        128,
        lambda r, c: c
        == ((r >> 1) & 1) * 64 + (r >> 5) * 16 + ((r >> 2) & 7) * 2 + (r & 1),
    )
    now = jnp.dot(perm, right_ref[...], preferred_element_type=F32)
    now_bf = now.astype(BF)
    lane = lax.broadcasted_iota(I32, (128, 128), 1)
    lagged = []
    for rep in range(2):
        lag = jnp.max(mask_ref[2 + rep : 3 + rep, :128]).astype(I32)
        tails = left_ref[:, 2048:].astype(F32)
        before = pltpu.roll(tails, lag if rep == 1 else lag + 64, 1)
        for j in range(8):
            at = rep * 1024 + j * 128
            block = pltpu.roll(left_ref[:, at : at + 128].astype(F32), lag, 1)
            lagged.append(jnp.where(lane < lag, before, block).astype(BF))
            before = block
    lagged = jnp.concatenate(lagged, axis=1)
    keep, keep_end = mask_ref[0:1, :], mask_ref[1:2, :]
    left = left_ref[:, :2048]
    start_bf, end_bf = keep.astype(BF), keep_end.astype(BF)
    for m, lhs in enumerate((left * start_bf, lagged * end_bf, left * end_bf)):
        block = lax.dot_general(lhs, now_bf, NT, preferred_element_type=F32)
        for d in range(8):
            at = (d >> 1 & 1) * 4 + (d >> 2) * 2 + (d & 1)
            out_ref[at, m * 16 : (m + 1) * 16, :] = block[d * 16 : (d + 1) * 16, :]
    var = lax.dot_general(
        jnp.ones((8, 2048), F32), now * now * keep_end, NT, precision=HI, preferred_element_type=F32
    )
    for d in range(8):
        out_ref[d, 48:56, :] = var


def rows_kernel(parts_ref, out_ref):
    total = parts_ref[0]
    for d in range(1, 8):
        total = total + parts_ref[d]
    for f in range(8):
        for m in range(3):
            src = m * 16 + f * 2
            out_ref[f, m * 2 : m * 2 + 2, :] = total[src : src + 2, :]
        out_ref[f, 6:8, :] = total[48:50, :]


def final_kernel(scale, place_ref, parts_ref, ridge_ref, row_ref, cov_ref, score_ref):
    first = place_ref[1]
    ridge = ridge_ref[...]
    lane = lax.broadcasted_iota(I32, (2, 128), 1)
    row = lax.broadcasted_iota(I32, (2, 128), 0)
    diag = jnp.zeros((2, 1), F32)
    weighted = [jnp.zeros((32, 128), F32) for _ in range(2)]
    for f in range(8):
        total = parts_ref[f] * scale
        for m in range(3):
            cov_ref[m, :, f * 128 : (f + 1) * 128] = total[m * 2 : m * 2 + 2, :]
        own = lane + f * 128 == first + row
        diag = diag + jnp.sum(jnp.where(own, total[0:2, :], 0.0), axis=1, keepdims=True)
        inverse = 1.0 / (total[6:7, :] + ridge)
        for e in range(2):
            cross = total[2 + e : 3 + e, :]
            weighted[e] = weighted[e] + (cross * cross) * inverse
    both = jnp.concatenate([*weighted, jnp.zeros((64, 128), F32)], axis=0)
    score = lax.dot_general(
        jnp.ones((8, 128), F32), both, NT, precision=HI, preferred_element_type=F32
    )
    for e in range(2):
        ridge_row = diag[e : e + 1, :] + row_ref[...]
        score_ref[e : e + 1, :] = score[0:1, e * 32 : e * 32 + 32] / ridge_row


def call(kernel, out, *args, smem=0, scratch=()):
    specs = [pl.BlockSpec(memory_space=pltpu.SMEM)] * smem
    specs += [pl.BlockSpec(memory_space=pltpu.VMEM)] * (len(args) - smem)
    shapes = [jax.ShapeDtypeStruct(*o) for o in out]
    outs = [pl.BlockSpec(memory_space=pltpu.VMEM)] * len(out)
    got = pl.pallas_call(
        kernel,
        out_shape=shapes,
        in_specs=specs,
        out_specs=outs,
        scratch_shapes=scratch,
        compiler_params=VMEM,
    )(*args)
    return got[0] if len(out) == 1 else got


def all_to_all(x, axes):
    return lax.all_to_all(x, axes, split_axis=0, concat_axis=0, tiled=True)


def local(frames, panel_low, panel_high, lags, seg_lengths, ridge):
    z = lax.axis_index(Z).astype(I32)
    yl = lax.axis_index("yl").astype(I32)
    c = lax.axis_index("c").astype(I32)
    own_first = ((z * 2 + lax.axis_index("yh")) * 8 + lax.axis_index(FE)) * 4 + yl * 2
    place = jnp.stack([z, own_first.astype(I32), c])

    halves = pl.pallas_call(
        halves_kernel,
        out_shape=pltpu.HBM((4, 272, 1024), BF),
        in_specs=[
            pl.BlockSpec(memory_space=pltpu.SMEM),
            pl.BlockSpec(memory_space=pltpu.HBM),
            pl.BlockSpec(memory_space=pltpu.HBM),
        ],
        out_specs=pl.BlockSpec(memory_space=pltpu.HBM),
        scratch_shapes=[
            pltpu.VMEM((2, 272, 1024), BF),
            pltpu.VMEM((1, 64), I32),
            pltpu.SemaphoreType.DMA((7,)),
        ],
        compiler_params=VMEM,
    )(
        lags,
        pltpu.with_memory_space_constraint(seg_lengths, pltpu.HBM),
        pltpu.with_memory_space_constraint(frames, pltpu.HBM),
    )
    frames_h = all_to_all(halves, ("yl", "yh"))

    packed = call(
        pack_kernel, [((32, 1024), BF)], yl[None], panel_low.T, panel_high.T, smem=1
    )
    panel_own = lax.all_gather(packed, Z8, axis=0, tiled=True)
    panel_other = lax.ppermute(panel_own, "z0", [(0, 1), (1, 0)])

    by_run = frames_h.reshape(2, 2, 272, 1024)
    tails = lax.ppermute(
        by_run[:, 1, 192:256].reshape(128, 1024), Z, [(i, i + 1) for i in range(1, 15, 2)]
    )
    masks = call(mask_kernel, [((8, 2048), F32)], place, by_run[:, 0, 256:, :128], smem=1)
    panel_other, masks = lax.optimization_barrier((panel_other, masks))

    keep, send = call(
        project_kernel,
        [((256, 1152), BF)] * 2,
        place,
        panel_own,
        panel_other,
        frames_h,
        tails,
        smem=1,
        scratch=[pltpu.VMEM((512, 1024), BF)],
    )
    got = lax.ppermute(send, "c", [(0, 1), (1, 0)])
    pairs = (keep.astype(F32) + got.astype(F32)).astype(BF)
    parts = all_to_all(pairs.reshape(32, 8, 1152), PLANE)
    basis, tiled = call(
        sum_kernel,
        [((16, 2176), BF), ((8, 16, 2048), BF)],
        parts.reshape(2, 4, 2, 2, 8, 1152),
    )

    right = all_to_all(tiled, RIGHT)
    left = lax.all_gather(basis, FE, axis=0, tiled=True)

    terms = call(
        cov_kernel, [((8, 56, 128), F32)], masks, left, right.reshape(128, 2048)
    )
    rows = call(rows_kernel, [((8, 8, 128), F32)], all_to_all(terms, FAR))
    by_row = all_to_all(rows, FE)
    return call(
        lambda *refs: final_kernel(1.0 / 16384.0, *refs),
        [((3, 2, 1024), F32), ((2, 32), F32)],
        place,
        by_row,
        ridge[:, None],
        ridge[None, :],
        smem=1,
    )


def solution(mesh):
    fine = Mesh(
        np.asarray(mesh.devices).reshape(2, 2, 2, 2, 2, 4, 2, 2),
        ("z3", "z2", "z1", "z0", "yh", "x", "c", "yl"),
    )
    tm = Z + ("yh",)
    in_specs = (P("yl", tm, FE), P(FE, tm), P(FE, tm), P("yl"), P("yl", None), P())
    rows = tm + FE + ("yl",)
    out_specs = (P(None, rows, None), P(rows, None))
    return jax.shard_map(local, mesh=fine, in_specs=in_specs, out_specs=out_specs, check_vma=False)
```

```python
import jax
import jax.numpy as jnp
import numpy as np
from jax import lax
from jax.experimental import pallas as pl
from jax.experimental.pallas import tpu as pltpu
from jax.sharding import Mesh, PartitionSpec as P

BF = jnp.bfloat16
F32 = jnp.float32
I32 = jnp.int32
HI = lax.Precision.HIGHEST
NT = (((1,), (1,)), ((), ()))
VMEM = pltpu.CompilerParams(vmem_limit_bytes=48 * 1024 * 1024)

Z = ("z3", "z2", "z1", "z0")
Z8 = ("z3", "z2", "z1")
FE = ("x", "c")
PLANE = ("yl", "x", "yh", "z0")
RIGHT = ("yl", "z0", "yh")
FAR = ("z1", "z2", "z3")


def one_hot(rows, cols, hit):
    r = lax.broadcasted_iota(I32, (rows, cols), 0)
    c = lax.broadcasted_iota(I32, (rows, cols), 1)
    return jnp.where(hit(r, c), 1.0, 0.0).astype(BF)


def pack_kernel(yl_ref, low_ref, high_ref, out_ref):
    off = pl.multiple_of(yl_ref[0] * 1024, 1024)
    src = one_hot(16, 16, lambda r, c: c == ((r >> 1) & 3) * 4 + (r >> 3) * 2 + (r & 1))
    for half, ref in enumerate((low_ref, high_ref)):
        rows = jnp.dot(src, ref[:, pl.ds(off, 1024)], preferred_element_type=F32)
        out_ref[half * 16 : half * 16 + 16, :] = rows.astype(BF)


def halves_kernel(lag_ref, seg_hbm, frames_ref, out_ref, rows_ref, seg_ref, sems):
    seg_load = pltpu.make_async_copy(seg_hbm, seg_ref, sems.at[12])
    seg_load.start()
    loads = []
    for n in range(4):
        half, rows = n // 2, pl.ds((n % 2) * 128, 128)
        part = frames_ref.at[0, rows, pl.ds(half * 1024, 1024)]
        load = pltpu.make_async_copy(part, rows_ref.at[half, rows], sems.at[n])
        load.start()
        loads.append(load)
    seg_load.wait()
    seg = jnp.concatenate([seg_ref[...], jnp.zeros((1, 64), I32)], axis=1)
    row = lax.broadcasted_iota(I32, (16, 128), 0)
    info = jnp.where(row == 0, seg >> 8, jnp.where(row == 1, seg & 255, lag_ref[0]))
    for half in range(2):
        rows_ref[half, 256:, :128] = info.astype(F32).astype(BF)
        rows_ref[half, 256:, 128:] = jnp.zeros((16, 896), BF)
    stores = []
    for n in range(4):
        half, rows = n // 2, pl.ds(0, 128) if n % 2 == 0 else pl.ds(128, 144)
        loads[n].wait()
        for i in range(2):
            store = pltpu.make_async_copy(
                rows_ref.at[half, rows], out_ref.at[half * 2 + i, rows], sems.at[4 + n * 2 + i]
            )
            store.start()
            stores.append(store)
    for store in stores:
        store.wait()


def project_kernel(
    place_ref, own_ref, other_ref, frames_ref, tails_ref, keep_ref, send_ref, panel_ref
):
    own_yh = place_ref[0] & 1
    c = place_ref[2]
    for kind in range(2):
        z2 = c if kind == 0 else 1 - c
        for yh, ref in ((own_yh, own_ref), (1 - own_yh, other_ref)):
            for z3 in range(2):
                src = pl.multiple_of(z3 * 128 + z2 * 64, 64)
                dst = pl.multiple_of(kind * 256 + yh * 128 + z3 * 64, 64)
                panel_ref[pl.ds(dst, 64), :] = ref[pl.ds(src, 64), :]
    panel = panel_ref[...]
    for t in range(5):
        frames = frames_ref[t, :256] if t < 4 else tails_ref[...]
        lanes = slice(t * 256, t * 256 + 256) if t < 4 else slice(1024, 1152)
        acc = lax.dot_general(panel, frames, NT, preferred_element_type=F32)
        for kind, ref in enumerate((keep_ref, send_ref)):
            for yh in range(2):
                for z3 in range(2):
                    for half in range(2):
                        for yl in range(2):
                            row = kind * 256 + yh * 128 + z3 * 64 + half * 16 + yl * 8
                            both = jnp.concatenate(
                                [acc[row : row + 8], acc[row + 32 : row + 40]], axis=0
                            )
                            at = ((yl * 4 + half * 2 + z3) * 2 + yh) * 16
                            ref[at : at + 16, lanes] = both.astype(BF)


def sum_kernel(parts_ref, basis_ref, tiled_ref):
    for z0 in range(2):
        sums = []
        for yh in range(2):
            total = parts_ref[0, 0, yh, z0].astype(F32)
            for i in range(1, 8):
                total = total + parts_ref[i // 4, i % 4, yh, z0].astype(F32)
            sums.append(total)
        basis = jnp.concatenate(sums, axis=0).astype(BF)
        for rep in range(2):
            at = rep * 1024 + z0 * 512
            block = basis[:, rep * 512 : (rep + 1) * 512]
            basis_ref[:, at : at + 512] = block
            for d in range(8):
                tiled_ref[d, :, at : at + 512] = block
        if z0 == 0:
            basis_ref[:, 2048:] = basis[:, 1024:]


def mask_kernel(place_ref, info_ref, out_ref):
    first = (place_ref[0] >> 1) * 1024
    tri = lax.broadcasted_iota(I32, (64, 64), 1) <= lax.broadcasted_iota(I32, (64, 64), 0)
    for rep in range(2):
        info = info_ref[rep].astype(F32)
        seg = info[0:1, :64] * 256.0 + info[1:2, :64]
        lag = info[2:3, 0:1]
        ends = jnp.sum(jnp.where(tri, seg, 0.0), axis=1, keepdims=True)
        here = (lax.broadcasted_iota(I32, (1, 1024), 1) + first).astype(F32)
        ahead = here + lag
        behind = here - lag
        cut = jnp.where((ends > here) & (ends <= ahead), 1.0, 0.0)
        cut_end = jnp.where((ends > behind) & (ends <= here), 1.0, 0.0)
        inside = jnp.where(behind >= 0.0, 1.0, 0.0)
        at = slice(rep * 1024, (rep + 1) * 1024)
        out_ref[0:1, at] = 1.0 - jnp.max(cut, axis=0, keepdims=True)
        out_ref[1:2, at] = (1.0 - jnp.max(cut_end, axis=0, keepdims=True)) * inside
        out_ref[2 + rep : 3 + rep, :] = jnp.broadcast_to(lag, (1, 2048))


def cov_kernel(mask_ref, left_ref, right_ref, out_ref):
    perm = one_hot(
        128,
        128,
        lambda r, c: c
        == ((r >> 1) & 1) * 64 + (r >> 5) * 16 + ((r >> 2) & 7) * 2 + (r & 1),
    )
    now = jnp.dot(perm, right_ref[...], preferred_element_type=F32)
    now_bf = now.astype(BF)
    lane = lax.broadcasted_iota(I32, (128, 128), 1)
    lagged = []
    for rep in range(2):
        lag = jnp.max(mask_ref[2 + rep : 3 + rep, :128]).astype(I32)
        tails = left_ref[:, 2048:].astype(F32)
        before = pltpu.roll(tails, lag if rep == 1 else lag + 64, 1)
        for j in range(8):
            at = rep * 1024 + j * 128
            block = pltpu.roll(left_ref[:, at : at + 128].astype(F32), lag, 1)
            lagged.append(jnp.where(lane < lag, before, block).astype(BF))
            before = block
    lagged = jnp.concatenate(lagged, axis=1)
    keep, keep_end = mask_ref[0:1, :], mask_ref[1:2, :]
    left = left_ref[:, :2048]
    start_bf, end_bf = keep.astype(BF), keep_end.astype(BF)
    for m, lhs in enumerate((left * start_bf, lagged * end_bf, left * end_bf)):
        block = lax.dot_general(lhs, now_bf, NT, preferred_element_type=F32)
        for d in range(8):
            at = sum(((d >> int(a[1]) - 1) & 1) << (2 - i) for i, a in enumerate(FAR))
            out_ref[at, m * 16 : (m + 1) * 16, :] = block[d * 16 : (d + 1) * 16, :]
    var = lax.dot_general(
        jnp.ones((8, 2048), F32), now * now * keep_end, NT, precision=HI, preferred_element_type=F32
    )
    for d in range(8):
        out_ref[d, 48:56, :] = var


def rows_kernel(parts_ref, out_ref):
    total = parts_ref[0]
    for d in range(1, 8):
        total = total + parts_ref[d]
    for f in range(8):
        for m in range(3):
            src = m * 16 + f * 2
            out_ref[f, m * 2 : m * 2 + 2, :] = total[src : src + 2, :]
        out_ref[f, 6:8, :] = total[48:50, :]


def final_kernel(scale, place_ref, parts_ref, ridge_ref, row_ref, cov_ref, score_ref):
    first = place_ref[1]
    ridge = ridge_ref[...]
    lane = lax.broadcasted_iota(I32, (2, 128), 1)
    row = lax.broadcasted_iota(I32, (2, 128), 0)
    diag = jnp.zeros((2, 1), F32)
    weighted = [jnp.zeros((32, 128), F32) for _ in range(2)]
    for f in range(8):
        total = parts_ref[f] * scale
        for m in range(3):
            cov_ref[m, :, f * 128 : (f + 1) * 128] = total[m * 2 : m * 2 + 2, :]
        own = lane + f * 128 == first + row
        diag = diag + jnp.sum(jnp.where(own, total[0:2, :], 0.0), axis=1, keepdims=True)
        inverse = 1.0 / (total[6:7, :] + ridge)
        for e in range(2):
            cross = total[2 + e : 3 + e, :]
            weighted[e] = weighted[e] + (cross * cross) * inverse
    both = jnp.concatenate([*weighted, jnp.zeros((64, 128), F32)], axis=0)
    score = lax.dot_general(
        jnp.ones((8, 128), F32), both, NT, precision=HI, preferred_element_type=F32
    )
    for e in range(2):
        ridge_row = diag[e : e + 1, :] + row_ref[...]
        score_ref[e : e + 1, :] = score[0:1, e * 32 : e * 32 + 32] / ridge_row


def call(kernel, out, *args, smem=0, scratch=()):
    specs = [pl.BlockSpec(memory_space=pltpu.SMEM)] * smem
    specs += [pl.BlockSpec(memory_space=pltpu.VMEM)] * (len(args) - smem)
    shapes = [jax.ShapeDtypeStruct(*o) for o in out]
    outs = [pl.BlockSpec(memory_space=pltpu.VMEM)] * len(out)
    got = pl.pallas_call(
        kernel,
        out_shape=shapes,
        in_specs=specs,
        out_specs=outs,
        scratch_shapes=scratch,
        compiler_params=VMEM,
    )(*args)
    return got[0] if len(out) == 1 else got


def all_to_all(x, axes):
    return lax.all_to_all(x, axes, split_axis=0, concat_axis=0, tiled=True)


def local(frames, panel_low, panel_high, lags, seg_lengths, ridge):
    z = lax.axis_index(Z).astype(I32)
    yl = lax.axis_index("yl").astype(I32)
    c = lax.axis_index("c").astype(I32)
    own_first = ((z * 2 + lax.axis_index("yh")) * 8 + lax.axis_index(FE)) * 4 + yl * 2
    place = jnp.stack([z, own_first.astype(I32), c])

    halves = pl.pallas_call(
        halves_kernel,
        out_shape=pltpu.HBM((4, 272, 1024), BF),
        in_specs=[
            pl.BlockSpec(memory_space=pltpu.SMEM),
            pl.BlockSpec(memory_space=pltpu.HBM),
            pl.BlockSpec(memory_space=pltpu.HBM),
        ],
        out_specs=pl.BlockSpec(memory_space=pltpu.HBM),
        scratch_shapes=[
            pltpu.VMEM((2, 272, 1024), BF),
            pltpu.VMEM((1, 64), I32),
            pltpu.SemaphoreType.DMA((13,)),
        ],
        compiler_params=VMEM,
    )(
        lags,
        pltpu.with_memory_space_constraint(seg_lengths, pltpu.HBM),
        pltpu.with_memory_space_constraint(frames, pltpu.HBM),
    )
    frames_h = all_to_all(halves, ("yl", "yh"))

    packed = call(
        pack_kernel, [((32, 1024), BF)], yl[None], panel_low.T, panel_high.T, smem=1
    )
    panel_own = lax.all_gather(packed, Z8, axis=0, tiled=True)
    panel_other = lax.ppermute(panel_own, "z0", [(0, 1), (1, 0)])

    by_run = frames_h.reshape(2, 2, 272, 1024)
    tails = lax.ppermute(
        by_run[:, 1, 192:256].reshape(128, 1024), Z, [(i, i + 1) for i in range(1, 15, 2)]
    )
    masks = call(mask_kernel, [((8, 2048), F32)], place, by_run[:, 0, 256:, :128], smem=1)
    panel_other, masks = lax.optimization_barrier((panel_other, masks))

    keep, send = call(
        project_kernel,
        [((256, 1152), BF)] * 2,
        place,
        panel_own,
        panel_other,
        frames_h,
        tails,
        smem=1,
        scratch=[pltpu.VMEM((512, 1024), BF)],
    )
    got = lax.ppermute(send, "c", [(0, 1), (1, 0)])
    pairs = (keep.astype(F32) + got.astype(F32)).astype(BF)
    parts = all_to_all(pairs.reshape(32, 8, 1152), PLANE)
    basis, tiled = call(
        sum_kernel,
        [((16, 2176), BF), ((8, 16, 2048), BF)],
        parts.reshape(2, 4, 2, 2, 8, 1152),
    )

    right = all_to_all(tiled, RIGHT)
    left = lax.all_gather(basis, FE, axis=0, tiled=True)

    terms = call(
        cov_kernel, [((8, 56, 128), F32)], masks, left, right.reshape(128, 2048)
    )
    rows = call(rows_kernel, [((8, 8, 128), F32)], all_to_all(terms, FAR))
    by_row = all_to_all(rows, FE)
    return call(
        lambda *refs: final_kernel(1.0 / 16384.0, *refs),
        [((3, 2, 1024), F32), ((2, 32), F32)],
        place,
        by_row,
        ridge[:, None],
        ridge[None, :],
        smem=1,
    )


def solution(mesh):
    fine = Mesh(
        np.asarray(mesh.devices).reshape(2, 2, 2, 2, 2, 4, 2, 2),
        ("z3", "z2", "z1", "z0", "yh", "x", "c", "yl"),
    )
    tm = Z + ("yh",)
    in_specs = (P("yl", tm, FE), P(FE, tm), P(FE, tm), P("yl"), P("yl", None), P())
    rows = tm + FE + ("yl",)
    out_specs = (P(None, rows, None), P(rows, None))
    return jax.shard_map(local, mesh=fine, in_specs=in_specs, out_specs=out_specs, check_vma=False)
```

```python
import jax
import jax.numpy as jnp
import numpy as np
from jax import lax
from jax.experimental import pallas as pl
from jax.experimental.pallas import tpu as pltpu
from jax.sharding import Mesh, PartitionSpec as P

BF = jnp.bfloat16
F32 = jnp.float32
I32 = jnp.int32
HI = lax.Precision.HIGHEST
NT = (((1,), (1,)), ((), ()))
VMEM = pltpu.CompilerParams(vmem_limit_bytes=48 * 1024 * 1024)

Z = ("z3", "z2", "z1", "z0")
Z8 = ("z3", "z2", "z1")
FE = ("x", "c")
PLANE = ("yl", "x", "yh", "z0")
RIGHT = ("yl", "z0", "yh")
FAR = ("z1", "z2", "z3")


def one_hot(rows, cols, hit):
    r = lax.broadcasted_iota(I32, (rows, cols), 0)
    c = lax.broadcasted_iota(I32, (rows, cols), 1)
    return jnp.where(hit(r, c), 1.0, 0.0).astype(BF)


def pack_kernel(yl_ref, low_ref, high_ref, out_ref):
    off = pl.multiple_of(yl_ref[0] * 1024, 1024)
    src = one_hot(16, 16, lambda r, c: c == ((r >> 1) & 3) * 4 + (r >> 3) * 2 + (r & 1))
    for half, ref in enumerate((low_ref, high_ref)):
        rows = jnp.dot(src, ref[:, pl.ds(off, 1024)], preferred_element_type=F32)
        out_ref[half * 16 : half * 16 + 16, :] = rows.astype(BF)


def halves_kernel(lag_ref, seg_hbm, frames_ref, out_ref, rows_ref, seg_ref, sems):
    seg_load = pltpu.make_async_copy(seg_hbm, seg_ref, sems.at[12])
    seg_load.start()
    loads = []
    for n in range(4):
        half, rows = n // 2, pl.ds((n % 2) * 128, 128)
        part = frames_ref.at[0, rows, pl.ds(half * 1024, 1024)]
        load = pltpu.make_async_copy(part, rows_ref.at[half, rows], sems.at[n])
        load.start()
        loads.append(load)
    seg_load.wait()
    seg = jnp.concatenate([seg_ref[...], jnp.zeros((1, 64), I32)], axis=1)
    row = lax.broadcasted_iota(I32, (16, 128), 0)
    info = jnp.where(row == 0, seg >> 8, jnp.where(row == 1, seg & 255, lag_ref[0]))
    for half in range(2):
        rows_ref[half, 256:, :128] = info.astype(F32).astype(BF)
        rows_ref[half, 256:, 128:] = jnp.zeros((16, 896), BF)
    stores = []
    for n in range(4):
        half, rows = n // 2, pl.ds(0, 128) if n % 2 == 0 else pl.ds(128, 144)
        loads[n].wait()
        for i in range(2):
            store = pltpu.make_async_copy(
                rows_ref.at[half, rows], out_ref.at[half * 2 + i, rows], sems.at[4 + n * 2 + i]
            )
            store.start()
            stores.append(store)
    for store in stores:
        store.wait()


def project_kernel(own_ref, other_ref, frames_ref, tails_ref, keep_ref, send_ref, panel_ref):
    own_yh = lax.axis_index("z0").astype(I32)
    c = lax.axis_index("c").astype(I32)
    for kind in range(2):
        z2 = c if kind == 0 else 1 - c
        for yh, ref in ((own_yh, own_ref), (1 - own_yh, other_ref)):
            for z3 in range(2):
                src = pl.multiple_of(z3 * 128 + z2 * 64, 64)
                dst = pl.multiple_of(kind * 256 + yh * 128 + z3 * 64, 64)
                panel_ref[pl.ds(dst, 64), :] = ref[pl.ds(src, 64), :]
    panel = panel_ref[...]
    for t in range(5):
        frames = frames_ref[t, :256] if t < 4 else tails_ref[...]
        lanes = slice(t * 256, t * 256 + 256) if t < 4 else slice(1024, 1152)
        acc = lax.dot_general(panel, frames, NT, preferred_element_type=F32)
        for kind, ref in enumerate((keep_ref, send_ref)):
            for yh in range(2):
                for z3 in range(2):
                    for half in range(2):
                        for yl in range(2):
                            row = kind * 256 + yh * 128 + z3 * 64 + half * 16 + yl * 8
                            both = jnp.concatenate(
                                [acc[row : row + 8], acc[row + 32 : row + 40]], axis=0
                            )
                            at = ((yl * 4 + half * 2 + z3) * 2 + yh) * 16
                            ref[at : at + 16, lanes] = both.astype(BF)


def sum_kernel(parts_ref, basis_ref, tiled_ref):
    for z0 in range(2):
        sums = []
        for yh in range(2):
            total = parts_ref[0, 0, yh, z0].astype(F32)
            for i in range(1, 8):
                total = total + parts_ref[i // 4, i % 4, yh, z0].astype(F32)
            sums.append(total)
        basis = jnp.concatenate(sums, axis=0).astype(BF)
        for rep in range(2):
            at = rep * 1024 + z0 * 512
            block = basis[:, rep * 512 : (rep + 1) * 512]
            basis_ref[:, at : at + 512] = block
            for d in range(8):
                tiled_ref[d, :, at : at + 512] = block
        if z0 == 0:
            basis_ref[:, 2048:] = basis[:, 1024:]


def mask_kernel(z_ref, info_ref, out_ref):
    first = (z_ref[0] >> 1) * 1024
    tri = lax.broadcasted_iota(I32, (64, 64), 1) <= lax.broadcasted_iota(I32, (64, 64), 0)
    for rep in range(2):
        info = info_ref[rep].astype(F32)
        seg = info[0:1, :64] * 256.0 + info[1:2, :64]
        lag = info[2:3, 0:1]
        ends = jnp.sum(jnp.where(tri, seg, 0.0), axis=1, keepdims=True)
        here = (lax.broadcasted_iota(I32, (1, 1024), 1) + first).astype(F32)
        ahead = here + lag
        behind = here - lag
        cut = jnp.where((ends > here) & (ends <= ahead), 1.0, 0.0)
        cut_end = jnp.where((ends > behind) & (ends <= here), 1.0, 0.0)
        inside = jnp.where(behind >= 0.0, 1.0, 0.0)
        at = slice(rep * 1024, (rep + 1) * 1024)
        out_ref[0:1, at] = 1.0 - jnp.max(cut, axis=0, keepdims=True)
        out_ref[1:2, at] = (1.0 - jnp.max(cut_end, axis=0, keepdims=True)) * inside
        out_ref[2 + rep : 3 + rep, :] = jnp.broadcast_to(lag, (1, 2048))


def cov_kernel(mask_ref, left_ref, right_ref, out_ref):
    perm = one_hot(
        128,
        128,
        lambda r, c: c
        == ((r >> 1) & 1) * 64 + (r >> 5) * 16 + ((r >> 2) & 7) * 2 + (r & 1),
    )
    now = jnp.dot(perm, right_ref[...], preferred_element_type=F32)
    now_bf = now.astype(BF)
    lane = lax.broadcasted_iota(I32, (128, 128), 1)
    lagged = []
    for rep in range(2):
        lag = jnp.max(mask_ref[2 + rep : 3 + rep, :128]).astype(I32)
        tails = left_ref[:, 2048:].astype(F32)
        before = pltpu.roll(tails, lag if rep == 1 else lag + 64, 1)
        for j in range(8):
            at = rep * 1024 + j * 128
            block = pltpu.roll(left_ref[:, at : at + 128].astype(F32), lag, 1)
            lagged.append(jnp.where(lane < lag, before, block).astype(BF))
            before = block
    lagged = jnp.concatenate(lagged, axis=1)
    keep, keep_end = mask_ref[0:1, :], mask_ref[1:2, :]
    left = left_ref[:, :2048]
    start_bf, end_bf = keep.astype(BF), keep_end.astype(BF)
    for m, lhs in enumerate((left * start_bf, lagged * end_bf, left * end_bf)):
        block = lax.dot_general(lhs, now_bf, NT, preferred_element_type=F32)
        for d in range(8):
            at = sum(((d >> int(a[1]) - 1) & 1) << (2 - i) for i, a in enumerate(FAR))
            out_ref[at, m * 16 : (m + 1) * 16, :] = block[d * 16 : (d + 1) * 16, :]
    var = lax.dot_general(
        jnp.ones((8, 2048), F32), now * now * keep_end, NT, precision=HI, preferred_element_type=F32
    )
    for d in range(8):
        out_ref[d, 48:56, :] = var


def rows_kernel(parts_ref, out_ref):
    total = parts_ref[0]
    for d in range(1, 8):
        total = total + parts_ref[d]
    for f in range(8):
        for m in range(3):
            src = m * 16 + f * 2
            out_ref[f, m * 2 : m * 2 + 2, :] = total[src : src + 2, :]
        out_ref[f, 6:8, :] = total[48:50, :]


def final_kernel(scale, parts_ref, own_ref, ridge_ref, row_ref, cov_ref, score_ref):
    ridge = ridge_ref[...]
    diag = jnp.zeros((2, 1), F32)
    weighted = [jnp.zeros((32, 128), F32) for _ in range(2)]
    for f in range(8):
        total = parts_ref[f] * scale
        for m in range(3):
            cov_ref[m, :, f * 128 : (f + 1) * 128] = total[m * 2 : m * 2 + 2, :]
        own = own_ref[:, f * 128 : (f + 1) * 128] > 0.0
        diag = diag + jnp.sum(jnp.where(own, total[0:2, :], 0.0), axis=1, keepdims=True)
        inverse = 1.0 / (total[6:7, :] + ridge)
        for e in range(2):
            cross = total[2 + e : 3 + e, :]
            weighted[e] = weighted[e] + (cross * cross) * inverse
    both = jnp.concatenate([*weighted, jnp.zeros((64, 128), F32)], axis=0)
    score = lax.dot_general(
        jnp.ones((8, 128), F32), both, NT, precision=HI, preferred_element_type=F32
    )
    for e in range(2):
        ridge_row = diag[e : e + 1, :] + row_ref[...]
        score_ref[e : e + 1, :] = score[0:1, e * 32 : e * 32 + 32] / ridge_row


def call(kernel, out, *args, smem=0, scratch=()):
    specs = [pl.BlockSpec(memory_space=pltpu.SMEM)] * smem
    specs += [pl.BlockSpec(memory_space=pltpu.VMEM)] * (len(args) - smem)
    shapes = [jax.ShapeDtypeStruct(*o) for o in out]
    outs = [pl.BlockSpec(memory_space=pltpu.VMEM)] * len(out)
    got = pl.pallas_call(
        kernel,
        out_shape=shapes,
        in_specs=specs,
        out_specs=outs,
        scratch_shapes=scratch,
        compiler_params=VMEM,
    )(*args)
    return got[0] if len(out) == 1 else got


def all_to_all(x, axes):
    return lax.all_to_all(x, axes, split_axis=0, concat_axis=0, tiled=True)


def local(frames, panel_low, panel_high, lags, seg_lengths, ridge):
    z = lax.axis_index(Z).astype(I32)
    yl = lax.axis_index("yl").astype(I32)
    own_first = ((z * 2 + lax.axis_index("yh")) * 8 + lax.axis_index(FE)) * 4 + yl * 2
    rows = lax.broadcasted_iota(I32, (2, 1024), 0) + own_first.astype(I32)
    own = (lax.broadcasted_iota(I32, (2, 1024), 1) == rows).astype(F32)

    halves = pl.pallas_call(
        halves_kernel,
        out_shape=pltpu.HBM((4, 272, 1024), BF),
        in_specs=[
            pl.BlockSpec(memory_space=pltpu.SMEM),
            pl.BlockSpec(memory_space=pltpu.HBM),
            pl.BlockSpec(memory_space=pltpu.HBM),
        ],
        out_specs=pl.BlockSpec(memory_space=pltpu.HBM),
        scratch_shapes=[
            pltpu.VMEM((2, 272, 1024), BF),
            pltpu.VMEM((1, 64), I32),
            pltpu.SemaphoreType.DMA((13,)),
        ],
        compiler_params=VMEM,
    )(
        lags,
        pltpu.with_memory_space_constraint(seg_lengths, pltpu.HBM),
        pltpu.with_memory_space_constraint(frames, pltpu.HBM),
    )
    frames_h = all_to_all(halves, ("yl", "yh"))

    packed = call(
        pack_kernel, [((32, 1024), BF)], yl[None], panel_low.T, panel_high.T, smem=1
    )
    panel_own = lax.all_gather(packed, Z8, axis=0, tiled=True)
    panel_other = lax.ppermute(panel_own, "z0", [(0, 1), (1, 0)])

    by_run = frames_h.reshape(2, 2, 272, 1024)
    tails = lax.ppermute(
        by_run[:, 1, 192:256].reshape(128, 1024), Z, [(i, i + 1) for i in range(1, 15, 2)]
    )
    masks = call(mask_kernel, [((8, 2048), F32)], z[None], by_run[:, 0, 256:, :128], smem=1)
    panel_other, masks, own, ridge_column, ridge_row = lax.optimization_barrier(
        (panel_other, masks, own, ridge[:, None], ridge[None, :])
    )

    keep, send = call(
        project_kernel,
        [((256, 1152), BF)] * 2,
        panel_own,
        panel_other,
        frames_h,
        tails,
        scratch=[pltpu.VMEM((512, 1024), BF)],
    )
    got = lax.ppermute(send, "c", [(0, 1), (1, 0)])
    pairs = (keep.astype(F32) + got.astype(F32)).astype(BF)
    parts = all_to_all(pairs.reshape(32, 8, 1152), PLANE)
    basis, tiled = call(
        sum_kernel,
        [((16, 2176), BF), ((8, 16, 2048), BF)],
        parts.reshape(2, 4, 2, 2, 8, 1152),
    )

    right = all_to_all(tiled, RIGHT)
    left = lax.all_gather(basis, FE, axis=0, tiled=True)

    terms = call(
        cov_kernel, [((8, 56, 128), F32)], masks, left, right.reshape(128, 2048)
    )
    rows = call(rows_kernel, [((8, 8, 128), F32)], all_to_all(terms, FAR))
    by_row = all_to_all(rows, FE)
    return call(
        lambda *refs: final_kernel(1.0 / 16384.0, *refs),
        [((3, 2, 1024), F32), ((2, 32), F32)],
        by_row,
        own,
        ridge_column,
        ridge_row,
    )


def solution(mesh):
    fine = Mesh(
        np.asarray(mesh.devices).reshape(2, 2, 2, 2, 2, 4, 2, 2),
        ("z3", "z2", "z1", "z0", "yh", "x", "c", "yl"),
    )
    tm = Z + ("yh",)
    in_specs = (P("yl", tm, FE), P(FE, tm), P(FE, tm), P("yl"), P("yl", None), P())
    rows = tm + FE + ("yl",)
    out_specs = (P(None, rows, None), P(rows, None))
    return jax.shard_map(local, mesh=fine, in_specs=in_specs, out_specs=out_specs, check_vma=False)
```

```python
import jax
import jax.numpy as jnp
import numpy as np
from jax import lax
from jax.experimental import pallas as pl
from jax.experimental.pallas import tpu as pltpu
from jax.sharding import Mesh, PartitionSpec as P

BF = jnp.bfloat16
F32 = jnp.float32
I32 = jnp.int32
HI = lax.Precision.HIGHEST
NT = (((1,), (1,)), ((), ()))
VMEM = pltpu.CompilerParams(vmem_limit_bytes=48 * 1024 * 1024)

Z = ("z3", "z2", "z1", "z0")
Z8 = ("z3", "z2", "z1")
FE = ("x", "c")
PLANE = ("yl", "x", "yh", "z0")
RIGHT = ("yl", "z0", "yh")
FAR = ("z1", "z2", "z3")


def one_hot(rows, cols, hit):
    r = lax.broadcasted_iota(I32, (rows, cols), 0)
    c = lax.broadcasted_iota(I32, (rows, cols), 1)
    return jnp.where(hit(r, c), 1.0, 0.0).astype(BF)


def pack_kernel(yl_ref, low_ref, high_ref, out_ref):
    off = pl.multiple_of(yl_ref[0] * 1024, 1024)
    src = one_hot(16, 16, lambda r, c: c == ((r >> 1) & 3) * 4 + (r >> 3) * 2 + (r & 1))
    for half, ref in enumerate((low_ref, high_ref)):
        rows = jnp.dot(src, ref[:, pl.ds(off, 1024)], preferred_element_type=F32)
        out_ref[half * 16 : half * 16 + 16, :] = rows.astype(BF)


def halves_kernel(lag_ref, seg_hbm, frames_ref, out_ref, rows_ref, seg_ref, sems):
    seg_load = pltpu.make_async_copy(seg_hbm, seg_ref, sems.at[12])
    seg_load.start()
    loads = []
    for n in range(4):
        half, rows = n // 2, pl.ds((n % 2) * 128, 128)
        part = frames_ref.at[0, rows, pl.ds(half * 1024, 1024)]
        load = pltpu.make_async_copy(part, rows_ref.at[half, rows], sems.at[n])
        load.start()
        loads.append(load)
    seg_load.wait()
    seg = jnp.concatenate([seg_ref[...], jnp.zeros((1, 64), I32)], axis=1)
    row = lax.broadcasted_iota(I32, (16, 128), 0)
    info = jnp.where(row == 0, seg >> 8, jnp.where(row == 1, seg & 255, lag_ref[0]))
    for half in range(2):
        rows_ref[half, 256:, :128] = info.astype(F32).astype(BF)
        rows_ref[half, 256:, 128:] = jnp.zeros((16, 896), BF)
    stores = []
    for n in range(4):
        half, rows = n // 2, pl.ds(0, 128) if n % 2 == 0 else pl.ds(128, 144)
        loads[n].wait()
        for i in range(2):
            store = pltpu.make_async_copy(
                rows_ref.at[half, rows], out_ref.at[half * 2 + i, rows], sems.at[4 + n * 2 + i]
            )
            store.start()
            stores.append(store)
    for store in stores:
        store.wait()


def project_kernel(own_ref, other_ref, frames_ref, tails_ref, keep_ref, send_ref, panel_ref):
    own_yh = lax.axis_index("z0").astype(I32)
    c = lax.axis_index("c").astype(I32)
    for kind in range(2):
        z2 = c if kind == 0 else 1 - c
        for yh, ref in ((own_yh, own_ref), (1 - own_yh, other_ref)):
            for z3 in range(2):
                src = pl.multiple_of(z3 * 128 + z2 * 64, 64)
                dst = pl.multiple_of(kind * 256 + yh * 128 + z3 * 64, 64)
                panel_ref[pl.ds(dst, 64), :] = ref[pl.ds(src, 64), :]
    panel = panel_ref[...]
    for t in range(5):
        frames = frames_ref[t, :256] if t < 4 else tails_ref[...]
        lanes = slice(t * 256, t * 256 + 256) if t < 4 else slice(1024, 1152)
        acc = lax.dot_general(panel, frames, NT, preferred_element_type=F32)
        for kind, ref in enumerate((keep_ref, send_ref)):
            for yh in range(2):
                for z3 in range(2):
                    for half in range(2):
                        for yl in range(2):
                            row = kind * 256 + yh * 128 + z3 * 64 + half * 16 + yl * 8
                            both = jnp.concatenate(
                                [acc[row : row + 8], acc[row + 32 : row + 40]], axis=0
                            )
                            at = ((yl * 4 + half * 2 + z3) * 2 + yh) * 16
                            ref[at : at + 16, lanes] = both.astype(BF)


def sum_kernel(parts_ref, basis_ref, tiled_ref):
    for z0 in range(2):
        sums = []
        for yh in range(2):
            total = parts_ref[0, 0, yh, z0].astype(F32)
            for i in range(1, 8):
                total = total + parts_ref[i // 4, i % 4, yh, z0].astype(F32)
            sums.append(total)
        basis = jnp.concatenate(sums, axis=0).astype(BF)
        for rep in range(2):
            at = rep * 1024 + z0 * 512
            block = basis[:, rep * 512 : (rep + 1) * 512]
            basis_ref[:, at : at + 512] = block
            for d in range(8):
                tiled_ref[d, :, at : at + 512] = block
        if z0 == 0:
            basis_ref[:, 2048:] = basis[:, 1024:]


def mask_kernel(z_ref, info_ref, out_ref):
    first = (z_ref[0] >> 1) * 1024
    tri = lax.broadcasted_iota(I32, (64, 64), 1) <= lax.broadcasted_iota(I32, (64, 64), 0)
    for rep in range(2):
        info = info_ref[rep].astype(F32)
        seg = info[0:1, :64] * 256.0 + info[1:2, :64]
        lag = info[2:3, 0:1]
        ends = jnp.sum(jnp.where(tri, seg, 0.0), axis=1, keepdims=True)
        here = (lax.broadcasted_iota(I32, (1, 1024), 1) + first).astype(F32)
        ahead = here + lag
        behind = here - lag
        cut = jnp.where((ends > here) & (ends <= ahead), 1.0, 0.0)
        cut_end = jnp.where((ends > behind) & (ends <= here), 1.0, 0.0)
        inside = jnp.where(behind >= 0.0, 1.0, 0.0)
        at = slice(rep * 1024, (rep + 1) * 1024)
        out_ref[0:1, at] = 1.0 - jnp.max(cut, axis=0, keepdims=True)
        out_ref[1:2, at] = (1.0 - jnp.max(cut_end, axis=0, keepdims=True)) * inside
        out_ref[2 + rep : 3 + rep, :] = jnp.broadcast_to(lag, (1, 2048))


def cov_kernel(mask_ref, left_ref, right_ref, out_ref):
    perm = one_hot(
        128,
        128,
        lambda r, c: c
        == ((r >> 1) & 1) * 64 + (r >> 5) * 16 + ((r >> 2) & 7) * 2 + (r & 1),
    )
    now = jnp.dot(perm, right_ref[...], preferred_element_type=F32)
    now_bf = now.astype(BF)
    lane = lax.broadcasted_iota(I32, (128, 128), 1)
    lagged = []
    for rep in range(2):
        lag = jnp.max(mask_ref[2 + rep : 3 + rep, :128]).astype(I32)
        tails = left_ref[:, 2048:].astype(F32)
        before = pltpu.roll(tails, lag if rep == 1 else lag + 64, 1)
        for j in range(8):
            at = rep * 1024 + j * 128
            block = pltpu.roll(left_ref[:, at : at + 128].astype(F32), lag, 1)
            lagged.append(jnp.where(lane < lag, before, block).astype(BF))
            before = block
    lagged = jnp.concatenate(lagged, axis=1)
    keep, keep_end = mask_ref[0:1, :], mask_ref[1:2, :]
    left = left_ref[:, :2048]
    start_bf, end_bf = keep.astype(BF), keep_end.astype(BF)
    for m, lhs in enumerate((left * start_bf, lagged * end_bf, left * end_bf)):
        block = lax.dot_general(lhs, now_bf, NT, preferred_element_type=F32)
        for d in range(8):
            at = sum(((d >> int(a[1]) - 1) & 1) << (2 - i) for i, a in enumerate(FAR))
            value = block[d * 16 : (d + 1) * 16, :]
            high = value.astype(BF)
            out_ref[at, m * 16 : (m + 1) * 16, :] = high
            out_ref[at, 48 + m * 16 : 64 + m * 16, :] = (value - high.astype(F32)).astype(BF)
    var = lax.dot_general(
        jnp.ones((8, 2048), F32), now * now * keep_end, NT, precision=HI, preferred_element_type=F32
    )
    high = var.astype(BF).astype(F32)
    row = lax.broadcasted_iota(I32, (8, 128), 0)
    var = jnp.where(row == 0, high, var - high).astype(BF)
    for d in range(8):
        out_ref[d, 96:104, :] = var


def rows_kernel(parts_ref, out_ref):
    total = parts_ref[0].astype(F32)
    for d in range(1, 8):
        total = total + parts_ref[d].astype(F32)
    var = total[96:97, :] + total[97:98, :]
    total = total[:48, :] + total[48:96, :]
    for f in range(8):
        for m in range(3):
            src = m * 16 + f * 2
            out_ref[f, m * 2 : m * 2 + 2, :] = total[src : src + 2, :]
        out_ref[f, 6:8, :] = jnp.broadcast_to(var, (2, 128))


def final_kernel(scale, parts_ref, own_ref, ridge_ref, row_ref, cov_ref, score_ref):
    ridge = ridge_ref[...]
    diag = jnp.zeros((2, 1), F32)
    weighted = [jnp.zeros((32, 128), F32) for _ in range(2)]
    for f in range(8):
        total = parts_ref[f] * scale
        for m in range(3):
            cov_ref[m, :, f * 128 : (f + 1) * 128] = total[m * 2 : m * 2 + 2, :]
        own = own_ref[:, f * 128 : (f + 1) * 128] > 0.0
        diag = diag + jnp.sum(jnp.where(own, total[0:2, :], 0.0), axis=1, keepdims=True)
        inverse = 1.0 / (total[6:7, :] + ridge)
        for e in range(2):
            cross = total[2 + e : 3 + e, :]
            weighted[e] = weighted[e] + (cross * cross) * inverse
    both = jnp.concatenate([*weighted, jnp.zeros((64, 128), F32)], axis=0)
    score = lax.dot_general(
        jnp.ones((8, 128), F32), both, NT, precision=HI, preferred_element_type=F32
    )
    for e in range(2):
        ridge_row = diag[e : e + 1, :] + row_ref[...]
        score_ref[e : e + 1, :] = score[0:1, e * 32 : e * 32 + 32] / ridge_row


def call(kernel, out, *args, smem=0, scratch=()):
    specs = [pl.BlockSpec(memory_space=pltpu.SMEM)] * smem
    specs += [pl.BlockSpec(memory_space=pltpu.VMEM)] * (len(args) - smem)
    shapes = [jax.ShapeDtypeStruct(*o) for o in out]
    outs = [pl.BlockSpec(memory_space=pltpu.VMEM)] * len(out)
    got = pl.pallas_call(
        kernel,
        out_shape=shapes,
        in_specs=specs,
        out_specs=outs,
        scratch_shapes=scratch,
        compiler_params=VMEM,
    )(*args)
    return got[0] if len(out) == 1 else got


def all_to_all(x, axes):
    return lax.all_to_all(x, axes, split_axis=0, concat_axis=0, tiled=True)


def local(frames, panel_low, panel_high, lags, seg_lengths, ridge):
    z = lax.axis_index(Z).astype(I32)
    yl = lax.axis_index("yl").astype(I32)
    own_first = ((z * 2 + lax.axis_index("yh")) * 8 + lax.axis_index(FE)) * 4 + yl * 2
    rows = lax.broadcasted_iota(I32, (2, 1024), 0) + own_first.astype(I32)
    own = (lax.broadcasted_iota(I32, (2, 1024), 1) == rows).astype(F32)

    halves = pl.pallas_call(
        halves_kernel,
        out_shape=pltpu.HBM((4, 272, 1024), BF),
        in_specs=[
            pl.BlockSpec(memory_space=pltpu.SMEM),
            pl.BlockSpec(memory_space=pltpu.HBM),
            pl.BlockSpec(memory_space=pltpu.HBM),
        ],
        out_specs=pl.BlockSpec(memory_space=pltpu.HBM),
        scratch_shapes=[
            pltpu.VMEM((2, 272, 1024), BF),
            pltpu.VMEM((1, 64), I32),
            pltpu.SemaphoreType.DMA((13,)),
        ],
        compiler_params=VMEM,
    )(
        lags,
        pltpu.with_memory_space_constraint(seg_lengths, pltpu.HBM),
        pltpu.with_memory_space_constraint(frames, pltpu.HBM),
    )
    frames_h = all_to_all(halves, ("yl", "yh"))

    packed = call(
        pack_kernel, [((32, 1024), BF)], yl[None], panel_low.T, panel_high.T, smem=1
    )
    panel_own = lax.all_gather(packed, Z8, axis=0, tiled=True)
    panel_other = lax.ppermute(panel_own, "z0", [(0, 1), (1, 0)])

    by_run = frames_h.reshape(2, 2, 272, 1024)
    tails = lax.ppermute(
        by_run[:, 1, 192:256].reshape(128, 1024), Z, [(i, i + 1) for i in range(1, 15, 2)]
    )
    masks = call(mask_kernel, [((8, 2048), F32)], z[None], by_run[:, 0, 256:, :128], smem=1)
    panel_other, masks, own, ridge_column, ridge_row = lax.optimization_barrier(
        (panel_other, masks, own, ridge[:, None], ridge[None, :])
    )

    keep, send = call(
        project_kernel,
        [((256, 1152), BF)] * 2,
        panel_own,
        panel_other,
        frames_h,
        tails,
        scratch=[pltpu.VMEM((512, 1024), BF)],
    )
    got = lax.ppermute(send, "c", [(0, 1), (1, 0)])
    pairs = (keep.astype(F32) + got.astype(F32)).astype(BF)
    parts = all_to_all(pairs.reshape(32, 8, 1152), PLANE)
    basis, tiled = call(
        sum_kernel,
        [((16, 2176), BF), ((8, 16, 2048), BF)],
        parts.reshape(2, 4, 2, 2, 8, 1152),
    )

    right = all_to_all(tiled, RIGHT)
    left = lax.all_gather(basis, FE, axis=0, tiled=True)

    terms = call(
        cov_kernel, [((8, 104, 128), BF)], masks, left, right.reshape(128, 2048)
    )
    rows = call(rows_kernel, [((8, 8, 128), F32)], all_to_all(terms, FAR))
    by_row = all_to_all(rows, FE)
    return call(
        lambda *refs: final_kernel(1.0 / 16384.0, *refs),
        [((3, 2, 1024), F32), ((2, 32), F32)],
        by_row,
        own,
        ridge_column,
        ridge_row,
    )


def solution(mesh):
    fine = Mesh(
        np.asarray(mesh.devices).reshape(2, 2, 2, 2, 2, 4, 2, 2),
        ("z3", "z2", "z1", "z0", "yh", "x", "c", "yl"),
    )
    tm = Z + ("yh",)
    in_specs = (P("yl", tm, FE), P(FE, tm), P(FE, tm), P("yl"), P("yl", None), P())
    rows = tm + FE + ("yl",)
    out_specs = (P(None, rows, None), P(rows, None))
    return jax.shard_map(local, mesh=fine, in_specs=in_specs, out_specs=out_specs, check_vma=False)
```

```python
import jax
import jax.numpy as jnp
import numpy as np
from jax import lax
from jax.experimental import pallas as pl
from jax.experimental.pallas import tpu as pltpu
from jax.sharding import Mesh, PartitionSpec as P

BF = jnp.bfloat16
F32 = jnp.float32
I32 = jnp.int32
HI = lax.Precision.HIGHEST
NT = (((1,), (1,)), ((), ()))
VMEM = pltpu.CompilerParams(vmem_limit_bytes=48 * 1024 * 1024)

Z = ("z3", "z2", "z1", "z0")
Z8 = ("z3", "z2", "z1")
FE = ("x", "c")
PLANE = ("yl", "x", "yh", "z0")
RIGHT = ("yl", "z0", "yh")
FAR = ("z1", "z2", "z3")


def one_hot(rows, cols, hit):
    r = lax.broadcasted_iota(I32, (rows, cols), 0)
    c = lax.broadcasted_iota(I32, (rows, cols), 1)
    return jnp.where(hit(r, c), 1.0, 0.0).astype(BF)


def pack_kernel(yl_ref, low_ref, high_ref, out_ref):
    off = pl.multiple_of(yl_ref[0] * 1024, 1024)
    src = one_hot(16, 16, lambda r, c: c == ((r >> 1) & 3) * 4 + (r >> 3) * 2 + (r & 1))
    for half, ref in enumerate((low_ref, high_ref)):
        rows = jnp.dot(src, ref[:, pl.ds(off, 1024)], preferred_element_type=F32)
        out_ref[half * 16 : half * 16 + 16, :] = rows.astype(BF)


def halves_kernel(lag_ref, seg_hbm, frames_ref, out_ref, rows_ref, seg_ref, sems):
    seg_load = pltpu.make_async_copy(seg_hbm, seg_ref, sems.at[12])
    seg_load.start()
    loads = []
    for n in range(4):
        half, rows = n // 2, pl.ds((n % 2) * 128, 128)
        part = frames_ref.at[0, rows, pl.ds(half * 1024, 1024)]
        load = pltpu.make_async_copy(part, rows_ref.at[half, rows], sems.at[n])
        load.start()
        loads.append(load)
    seg_load.wait()
    seg = jnp.concatenate([seg_ref[...], jnp.zeros((1, 64), I32)], axis=1)
    row = lax.broadcasted_iota(I32, (16, 128), 0)
    info = jnp.where(row == 0, seg >> 8, jnp.where(row == 1, seg & 255, lag_ref[0]))
    for half in range(2):
        rows_ref[half, 256:, :128] = info.astype(F32).astype(BF)
        rows_ref[half, 256:, 128:] = jnp.zeros((16, 896), BF)
    stores = []
    for n in range(4):
        half, rows = n // 2, pl.ds(0, 128) if n % 2 == 0 else pl.ds(128, 144)
        loads[n].wait()
        for i in range(2):
            store = pltpu.make_async_copy(
                rows_ref.at[half, rows], out_ref.at[half * 2 + i, rows], sems.at[4 + n * 2 + i]
            )
            store.start()
            stores.append(store)
    for store in stores:
        store.wait()


def project_kernel(own_ref, other_ref, frames_ref, tails_ref, keep_ref, send_ref, panel_ref):
    own_yh = lax.axis_index("z0").astype(I32)
    c = lax.axis_index("c").astype(I32)
    for kind in range(2):
        z2 = c if kind == 0 else 1 - c
        for yh, ref in ((own_yh, own_ref), (1 - own_yh, other_ref)):
            for z3 in range(2):
                src = pl.multiple_of(z3 * 128 + z2 * 64, 64)
                dst = pl.multiple_of(kind * 256 + yh * 128 + z3 * 64, 64)
                panel_ref[pl.ds(dst, 64), :] = ref[pl.ds(src, 64), :]
    panel = panel_ref[...]
    for t in range(5):
        frames = frames_ref[t, :256] if t < 4 else tails_ref[...]
        lanes = slice(t * 256, t * 256 + 256) if t < 4 else slice(1024, 1152)
        acc = lax.dot_general(panel, frames, NT, preferred_element_type=F32)
        for kind, ref in enumerate((keep_ref, send_ref)):
            for yh in range(2):
                for z3 in range(2):
                    for half in range(2):
                        for yl in range(2):
                            row = kind * 256 + yh * 128 + z3 * 64 + half * 16 + yl * 8
                            both = jnp.concatenate(
                                [acc[row : row + 8], acc[row + 32 : row + 40]], axis=0
                            )
                            at = ((yl * 4 + half * 2 + z3) * 2 + yh) * 16
                            ref[at : at + 16, lanes] = both.astype(BF)


def sum_kernel(parts_ref, basis_ref, tiled_ref):
    for z0 in range(2):
        sums = []
        for yh in range(2):
            total = parts_ref[0, 0, yh, z0].astype(F32)
            for i in range(1, 8):
                total = total + parts_ref[i // 4, i % 4, yh, z0].astype(F32)
            sums.append(total)
        basis = jnp.concatenate(sums, axis=0).astype(BF)
        for rep in range(2):
            at = rep * 1024 + z0 * 512
            block = basis[:, rep * 512 : (rep + 1) * 512]
            basis_ref[:, at : at + 512] = block
            for d in range(8):
                tiled_ref[d, :, at : at + 512] = block
        if z0 == 0:
            basis_ref[:, 2048:] = basis[:, 1024:]


def mask_kernel(z_ref, info_ref, out_ref):
    first = (z_ref[0] >> 1) * 1024
    tri = lax.broadcasted_iota(I32, (64, 64), 1) <= lax.broadcasted_iota(I32, (64, 64), 0)
    for rep in range(2):
        info = info_ref[rep].astype(F32)
        seg = info[0:1, :64] * 256.0 + info[1:2, :64]
        lag = info[2:3, 0:1]
        ends = jnp.sum(jnp.where(tri, seg, 0.0), axis=1, keepdims=True)
        here = (lax.broadcasted_iota(I32, (1, 1024), 1) + first).astype(F32)
        ahead = here + lag
        behind = here - lag
        cut = jnp.where((ends > here) & (ends <= ahead), 1.0, 0.0)
        cut_end = jnp.where((ends > behind) & (ends <= here), 1.0, 0.0)
        inside = jnp.where(behind >= 0.0, 1.0, 0.0)
        at = slice(rep * 1024, (rep + 1) * 1024)
        out_ref[0:1, at] = 1.0 - jnp.max(cut, axis=0, keepdims=True)
        out_ref[1:2, at] = (1.0 - jnp.max(cut_end, axis=0, keepdims=True)) * inside
        out_ref[2 + rep : 3 + rep, :] = jnp.broadcast_to(lag, (1, 2048))


def cov_kernel(mask_ref, left_ref, right_ref, out_ref):
    perm = one_hot(
        128,
        128,
        lambda r, c: c
        == ((r >> 1) & 1) * 64 + (r >> 5) * 16 + ((r >> 2) & 7) * 2 + (r & 1),
    )
    now = jnp.dot(perm, right_ref[...], preferred_element_type=F32)
    now_bf = now.astype(BF)
    lane = lax.broadcasted_iota(I32, (128, 128), 1)
    lagged = []
    for rep in range(2):
        lag = jnp.max(mask_ref[2 + rep : 3 + rep, :128]).astype(I32)
        tails = left_ref[:, 2048:].astype(F32)
        before = pltpu.roll(tails, lag if rep == 1 else lag + 64, 1)
        for j in range(8):
            at = rep * 1024 + j * 128
            block = pltpu.roll(left_ref[:, at : at + 128].astype(F32), lag, 1)
            lagged.append(jnp.where(lane < lag, before, block).astype(BF))
            before = block
    lagged = jnp.concatenate(lagged, axis=1)
    keep, keep_end = mask_ref[0:1, :], mask_ref[1:2, :]
    left = left_ref[:, :2048]
    start_bf, end_bf = keep.astype(BF), keep_end.astype(BF)
    for m, lhs in enumerate((left * start_bf, lagged * end_bf, left * end_bf)):
        block = lax.dot_general(lhs, now_bf, NT, preferred_element_type=F32)
        for d in range(8):
            at = sum(((d >> int(a[1]) - 1) & 1) << (2 - i) for i, a in enumerate(FAR))
            value = block[d * 16 : (d + 1) * 16, :]
            high = value.astype(BF)
            out_ref[at, m * 16 : (m + 1) * 16, :] = high
            out_ref[at, 48 + m * 16 : 64 + m * 16, :] = (value - high.astype(F32)).astype(BF)
    square = now * now * keep_end
    head = square.astype(BF)
    rest = (square - head.astype(F32)).astype(BF)
    ones = jnp.ones((8, 2048), BF)
    var = lax.dot_general(ones, head, NT, preferred_element_type=F32)
    var = var + lax.dot_general(ones, rest, NT, preferred_element_type=F32)
    high = var.astype(BF).astype(F32)
    row = lax.broadcasted_iota(I32, (8, 128), 0)
    var = jnp.where(row == 0, high, var - high).astype(BF)
    for d in range(8):
        out_ref[d, 96:104, :] = var


def rows_kernel(parts_ref, out_ref):
    total = parts_ref[0].astype(F32)
    for d in range(1, 8):
        total = total + parts_ref[d].astype(F32)
    var = total[96:97, :] + total[97:98, :]
    total = total[:48, :] + total[48:96, :]
    for f in range(8):
        for m in range(3):
            src = m * 16 + f * 2
            out_ref[f, m * 2 : m * 2 + 2, :] = total[src : src + 2, :]
        out_ref[f, 6:8, :] = jnp.broadcast_to(var, (2, 128))


def final_kernel(scale, parts_ref, own_ref, ridge_ref, row_ref, cov_ref, score_ref):
    ridge = ridge_ref[...]
    diag = jnp.zeros((2, 1), F32)
    weighted = [jnp.zeros((32, 128), F32) for _ in range(2)]
    for f in range(8):
        total = parts_ref[f] * scale
        for m in range(3):
            cov_ref[m, :, f * 128 : (f + 1) * 128] = total[m * 2 : m * 2 + 2, :]
        own = own_ref[:, f * 128 : (f + 1) * 128] > 0.0
        diag = diag + jnp.sum(jnp.where(own, total[0:2, :], 0.0), axis=1, keepdims=True)
        inverse = 1.0 / (total[6:7, :] + ridge)
        for e in range(2):
            cross = total[2 + e : 3 + e, :]
            weighted[e] = weighted[e] + (cross * cross) * inverse
    both = jnp.concatenate([*weighted, jnp.zeros((64, 128), F32)], axis=0)
    score = lax.dot_general(
        jnp.ones((8, 128), F32), both, NT, precision=HI, preferred_element_type=F32
    )
    for e in range(2):
        ridge_row = diag[e : e + 1, :] + row_ref[...]
        score_ref[e : e + 1, :] = score[0:1, e * 32 : e * 32 + 32] / ridge_row


def call(kernel, out, *args, smem=0, scratch=()):
    specs = [pl.BlockSpec(memory_space=pltpu.SMEM)] * smem
    specs += [pl.BlockSpec(memory_space=pltpu.VMEM)] * (len(args) - smem)
    shapes = [jax.ShapeDtypeStruct(*o) for o in out]
    outs = [pl.BlockSpec(memory_space=pltpu.VMEM)] * len(out)
    got = pl.pallas_call(
        kernel,
        out_shape=shapes,
        in_specs=specs,
        out_specs=outs,
        scratch_shapes=scratch,
        compiler_params=VMEM,
    )(*args)
    return got[0] if len(out) == 1 else got


def all_to_all(x, axes):
    return lax.all_to_all(x, axes, split_axis=0, concat_axis=0, tiled=True)


def local(frames, panel_low, panel_high, lags, seg_lengths, ridge):
    z = lax.axis_index(Z).astype(I32)
    yl = lax.axis_index("yl").astype(I32)
    own_first = ((z * 2 + lax.axis_index("yh")) * 8 + lax.axis_index(FE)) * 4 + yl * 2
    rows = lax.broadcasted_iota(I32, (2, 1024), 0) + own_first.astype(I32)
    own = (lax.broadcasted_iota(I32, (2, 1024), 1) == rows).astype(F32)

    halves = pl.pallas_call(
        halves_kernel,
        out_shape=pltpu.HBM((4, 272, 1024), BF),
        in_specs=[
            pl.BlockSpec(memory_space=pltpu.SMEM),
            pl.BlockSpec(memory_space=pltpu.HBM),
            pl.BlockSpec(memory_space=pltpu.HBM),
        ],
        out_specs=pl.BlockSpec(memory_space=pltpu.HBM),
        scratch_shapes=[
            pltpu.VMEM((2, 272, 1024), BF),
            pltpu.VMEM((1, 64), I32),
            pltpu.SemaphoreType.DMA((13,)),
        ],
        compiler_params=VMEM,
    )(
        lags,
        pltpu.with_memory_space_constraint(seg_lengths, pltpu.HBM),
        pltpu.with_memory_space_constraint(frames, pltpu.HBM),
    )
    frames_h = all_to_all(halves, ("yl", "yh"))

    packed = call(
        pack_kernel, [((32, 1024), BF)], yl[None], panel_low.T, panel_high.T, smem=1
    )
    panel_own = lax.all_gather(packed, Z8, axis=0, tiled=True)
    panel_other = lax.ppermute(panel_own, "z0", [(0, 1), (1, 0)])

    by_run = frames_h.reshape(2, 2, 272, 1024)
    tails = lax.ppermute(
        by_run[:, 1, 192:256].reshape(128, 1024), Z, [(i, i + 1) for i in range(1, 15, 2)]
    )
    masks = call(mask_kernel, [((8, 2048), F32)], z[None], by_run[:, 0, 256:, :128], smem=1)
    panel_other, masks, own, ridge_column, ridge_row = lax.optimization_barrier(
        (panel_other, masks, own, ridge[:, None], ridge[None, :])
    )

    keep, send = call(
        project_kernel,
        [((256, 1152), BF)] * 2,
        panel_own,
        panel_other,
        frames_h,
        tails,
        scratch=[pltpu.VMEM((512, 1024), BF)],
    )
    got = lax.ppermute(send, "c", [(0, 1), (1, 0)])
    pairs = (keep.astype(F32) + got.astype(F32)).astype(BF)
    parts = all_to_all(pairs.reshape(32, 8, 1152), PLANE)
    basis, tiled = call(
        sum_kernel,
        [((16, 2176), BF), ((8, 16, 2048), BF)],
        parts.reshape(2, 4, 2, 2, 8, 1152),
    )

    right = all_to_all(tiled, RIGHT)
    left = lax.all_gather(basis, FE, axis=0, tiled=True)

    terms = call(
        cov_kernel, [((8, 104, 128), BF)], masks, left, right.reshape(128, 2048)
    )
    rows = call(rows_kernel, [((8, 8, 128), F32)], all_to_all(terms, FAR))
    by_row = all_to_all(rows, FE)
    return call(
        lambda *refs: final_kernel(1.0 / 16384.0, *refs),
        [((3, 2, 1024), F32), ((2, 32), F32)],
        by_row,
        own,
        ridge_column,
        ridge_row,
    )


def solution(mesh):
    fine = Mesh(
        np.asarray(mesh.devices).reshape(2, 2, 2, 2, 2, 4, 2, 2),
        ("z3", "z2", "z1", "z0", "yh", "x", "c", "yl"),
    )
    tm = Z + ("yh",)
    in_specs = (P("yl", tm, FE), P(FE, tm), P(FE, tm), P("yl"), P("yl", None), P())
    rows = tm + FE + ("yl",)
    out_specs = (P(None, rows, None), P(rows, None))
    return jax.shard_map(local, mesh=fine, in_specs=in_specs, out_specs=out_specs, check_vma=False)
```

```python
import jax
import jax.numpy as jnp
import numpy as np
from jax import lax
from jax.experimental import pallas as pl
from jax.experimental.pallas import tpu as pltpu
from jax.sharding import Mesh, PartitionSpec as P

BF = jnp.bfloat16
F32 = jnp.float32
I32 = jnp.int32
HI = lax.Precision.HIGHEST
NT = (((1,), (1,)), ((), ()))
VMEM = pltpu.CompilerParams(vmem_limit_bytes=48 * 1024 * 1024)

Z = ("z3", "z2", "z1", "z0")
Z8 = ("z3", "z2", "z1")
FE = ("x", "c")
PLANE = ("yl", "x", "yh", "z0")
RIGHT = ("yl", "z0", "yh")
FAR = ("z1", "z2", "z3")


def one_hot(rows, cols, hit):
    r = lax.broadcasted_iota(I32, (rows, cols), 0)
    c = lax.broadcasted_iota(I32, (rows, cols), 1)
    return jnp.where(hit(r, c), 1.0, 0.0).astype(BF)


def pack_kernel(yl_ref, low_ref, high_ref, out_ref):
    off = pl.multiple_of(yl_ref[0] * 1024, 1024)
    src = one_hot(16, 16, lambda r, c: c == ((r >> 1) & 3) * 4 + (r >> 3) * 2 + (r & 1))
    for half, ref in enumerate((low_ref, high_ref)):
        rows = jnp.dot(src, ref[:, pl.ds(off, 1024)], preferred_element_type=F32)
        out_ref[half * 16 : half * 16 + 16, :] = rows.astype(BF)


def halves_kernel(lag_ref, seg_hbm, frames_ref, out_ref, rows_ref, seg_ref, sems):
    seg_load = pltpu.make_async_copy(seg_hbm, seg_ref, sems.at[12])
    seg_load.start()
    loads = []
    for n in range(4):
        half, rows = n // 2, pl.ds((n % 2) * 128, 128)
        part = frames_ref.at[0, rows, pl.ds(half * 1024, 1024)]
        load = pltpu.make_async_copy(part, rows_ref.at[half, rows], sems.at[n])
        load.start()
        loads.append(load)
    seg_load.wait()
    seg = jnp.concatenate([seg_ref[...], jnp.zeros((1, 64), I32)], axis=1)
    row = lax.broadcasted_iota(I32, (16, 128), 0)
    info = jnp.where(row == 0, seg >> 8, jnp.where(row == 1, seg & 255, lag_ref[0]))
    for half in range(2):
        rows_ref[half, 256:, :128] = info.astype(F32).astype(BF)
        rows_ref[half, 256:, 128:] = jnp.zeros((16, 896), BF)
    stores = []
    for n in range(4):
        half, rows = n // 2, pl.ds(0, 128) if n % 2 == 0 else pl.ds(128, 144)
        loads[n].wait()
        for i in range(2):
            store = pltpu.make_async_copy(
                rows_ref.at[half, rows], out_ref.at[half * 2 + i, rows], sems.at[4 + n * 2 + i]
            )
            store.start()
            stores.append(store)
    for store in stores:
        store.wait()


def project_kernel(own_ref, other_ref, frames_ref, tails_ref, keep_ref, send_ref, panel_ref):
    own_yh = lax.axis_index("z0").astype(I32)
    c = lax.axis_index("c").astype(I32)
    for kind in range(2):
        z2 = c if kind == 0 else 1 - c
        for yh, ref in ((own_yh, own_ref), (1 - own_yh, other_ref)):
            for z3 in range(2):
                src = pl.multiple_of(z3 * 128 + z2 * 64, 64)
                dst = pl.multiple_of(kind * 256 + yh * 128 + z3 * 64, 64)
                panel_ref[pl.ds(dst, 64), :] = ref[pl.ds(src, 64), :]
    panel = panel_ref[...]
    for t in range(5):
        frames = frames_ref[t, :256] if t < 4 else tails_ref[...]
        lanes = slice(t * 256, t * 256 + 256) if t < 4 else slice(1024, 1152)
        acc = lax.dot_general(panel, frames, NT, preferred_element_type=F32)
        for kind, ref in enumerate((keep_ref, send_ref)):
            for yh in range(2):
                for z3 in range(2):
                    for half in range(2):
                        for yl in range(2):
                            row = kind * 256 + yh * 128 + z3 * 64 + half * 16 + yl * 8
                            both = jnp.concatenate(
                                [acc[row : row + 8], acc[row + 32 : row + 40]], axis=0
                            )
                            at = ((yl * 4 + half * 2 + z3) * 2 + yh) * 16
                            ref[at : at + 16, lanes] = both.astype(BF)


def sum_kernel(parts_ref, basis_ref, tiled_ref):
    for z0 in range(2):
        sums = []
        for yh in range(2):
            total = parts_ref[0, 0, yh, z0].astype(F32)
            for i in range(1, 8):
                total = total + parts_ref[i // 4, i % 4, yh, z0].astype(F32)
            sums.append(total)
        basis = jnp.concatenate(sums, axis=0).astype(BF)
        for rep in range(2):
            at = rep * 1024 + z0 * 512
            block = basis[:, rep * 512 : (rep + 1) * 512]
            basis_ref[:, at : at + 512] = block
            for d in range(8):
                tiled_ref[d, :, at : at + 512] = block
        if z0 == 0:
            basis_ref[:, 2048:] = basis[:, 1024:]


def mask_kernel(z_ref, info_ref, out_ref):
    first = (z_ref[0] >> 1) * 1024
    tri = lax.broadcasted_iota(I32, (64, 64), 1) <= lax.broadcasted_iota(I32, (64, 64), 0)
    for rep in range(2):
        info = info_ref[rep].astype(F32)
        seg = info[0:1, :64] * 256.0 + info[1:2, :64]
        lag = info[2:3, 0:1]
        ends = jnp.sum(jnp.where(tri, seg, 0.0), axis=1, keepdims=True)
        here = (lax.broadcasted_iota(I32, (1, 1024), 1) + first).astype(F32)
        ahead = here + lag
        behind = here - lag
        cut = jnp.where((ends > here) & (ends <= ahead), 1.0, 0.0)
        cut_end = jnp.where((ends > behind) & (ends <= here), 1.0, 0.0)
        inside = jnp.where(behind >= 0.0, 1.0, 0.0)
        at = slice(rep * 1024, (rep + 1) * 1024)
        out_ref[0:1, at] = 1.0 - jnp.max(cut, axis=0, keepdims=True)
        out_ref[1:2, at] = (1.0 - jnp.max(cut_end, axis=0, keepdims=True)) * inside
        out_ref[2 + rep : 3 + rep, :] = jnp.broadcast_to(lag, (1, 2048))


def cov_kernel(mask_ref, left_ref, right_ref, out_ref):
    perm = one_hot(
        128,
        128,
        lambda r, c: c
        == ((r >> 1) & 1) * 64 + (r >> 5) * 16 + ((r >> 2) & 7) * 2 + (r & 1),
    )
    now = jnp.dot(perm, right_ref[...], preferred_element_type=F32)
    now_bf = now.astype(BF)
    lane = lax.broadcasted_iota(I32, (128, 128), 1)
    lagged = []
    for rep in range(2):
        lag = jnp.max(mask_ref[2 + rep : 3 + rep, :128]).astype(I32)
        tails = left_ref[:, 2048:].astype(F32)
        before = pltpu.roll(tails, lag if rep == 1 else lag + 64, 1)
        for j in range(8):
            at = rep * 1024 + j * 128
            block = pltpu.roll(left_ref[:, at : at + 128].astype(F32), lag, 1)
            lagged.append(jnp.where(lane < lag, before, block).astype(BF))
            before = block
    lagged = jnp.concatenate(lagged, axis=1)
    keep, keep_end = mask_ref[0:1, :], mask_ref[1:2, :]
    left = left_ref[:, :2048]
    start_bf, end_bf = keep.astype(BF), keep_end.astype(BF)
    for m, lhs in enumerate((left * start_bf, lagged * end_bf, left * end_bf)):
        block = lax.dot_general(lhs, now_bf, NT, preferred_element_type=F32)
        for d in range(8):
            at = sum(((d >> int(a[1]) - 1) & 1) << (2 - i) for i, a in enumerate(FAR))
            value = block[d * 16 : (d + 1) * 16, :]
            high = value.astype(BF)
            out_ref[at, m * 16 : (m + 1) * 16, :] = high
            out_ref[at, 48 + m * 16 : 64 + m * 16, :] = (value - high.astype(F32)).astype(BF)
    square = now * now * keep_end
    head = square.astype(BF)
    rest = (square - head.astype(F32)).astype(BF)
    ones = jnp.ones((8, 2048), BF)
    var = lax.dot_general(ones, head, NT, preferred_element_type=F32)
    var = var + lax.dot_general(ones, rest, NT, preferred_element_type=F32)
    high = var.astype(BF).astype(F32)
    row = lax.broadcasted_iota(I32, (8, 128), 0)
    var = jnp.where(row == 0, high, var - high).astype(BF)
    for d in range(8):
        out_ref[d, 96:104, :] = var


def rows_kernel(parts_ref, out_ref):
    total = parts_ref[0].astype(F32)
    for d in range(1, 8):
        total = total + parts_ref[d].astype(F32)
    var = total[96:97, :] + total[97:98, :]
    total = total[:48, :] + total[48:96, :]
    for f in range(8):
        for m in range(3):
            src = m * 16 + f * 2
            out_ref[f, m * 2 : m * 2 + 2, :] = total[src : src + 2, :]
        out_ref[f, 6:8, :] = jnp.broadcast_to(var, (2, 128))


def final_kernel(scale, parts_ref, own_ref, ridge_ref, row_ref, cov_ref, score_ref):
    ridge = ridge_ref[...]
    diag = jnp.zeros((2, 1), F32)
    weighted = [jnp.zeros((32, 128), F32) for _ in range(2)]
    for f in range(8):
        total = parts_ref[f] * scale
        for m in range(3):
            cov_ref[m, :, f * 128 : (f + 1) * 128] = total[m * 2 : m * 2 + 2, :]
        own = own_ref[:, f * 128 : (f + 1) * 128] > 0.0
        diag = diag + jnp.sum(jnp.where(own, total[0:2, :], 0.0), axis=1, keepdims=True)
        inverse = 1.0 / (total[6:7, :] + ridge)
        for e in range(2):
            cross = total[2 + e : 3 + e, :]
            weighted[e] = weighted[e] + (cross * cross) * inverse
    both = jnp.concatenate([*weighted, jnp.zeros((64, 128), F32)], axis=0)
    score = lax.dot_general(
        jnp.ones((8, 128), F32), both, NT, precision=HI, preferred_element_type=F32
    )
    for e in range(2):
        ridge_row = diag[e : e + 1, :] + row_ref[...]
        score_ref[e : e + 1, :] = score[0:1, e * 32 : e * 32 + 32] / ridge_row


def call(kernel, out, *args, smem=0, scratch=()):
    specs = [pl.BlockSpec(memory_space=pltpu.SMEM)] * smem
    specs += [pl.BlockSpec(memory_space=pltpu.VMEM)] * (len(args) - smem)
    shapes = [jax.ShapeDtypeStruct(*o) for o in out]
    outs = [pl.BlockSpec(memory_space=pltpu.VMEM)] * len(out)
    got = pl.pallas_call(
        kernel,
        out_shape=shapes,
        in_specs=specs,
        out_specs=outs,
        scratch_shapes=scratch,
        compiler_params=VMEM,
    )(*args)
    return got[0] if len(out) == 1 else got


def all_to_all(x, axes):
    return lax.all_to_all(x, axes, split_axis=0, concat_axis=0, tiled=True)


def local(frames, panel_low, panel_high, lags, seg_lengths, ridge):
    z = lax.axis_index(Z).astype(I32)
    yl = lax.axis_index("yl").astype(I32)
    own_first = ((z * 2 + lax.axis_index("yh")) * 8 + lax.axis_index(FE)) * 4 + yl * 2
    rows = lax.broadcasted_iota(I32, (2, 1024), 0) + own_first.astype(I32)
    own = (lax.broadcasted_iota(I32, (2, 1024), 1) == rows).astype(F32)

    halves = pl.pallas_call(
        halves_kernel,
        out_shape=pltpu.HBM((4, 272, 1024), BF),
        in_specs=[
            pl.BlockSpec(memory_space=pltpu.SMEM),
            pl.BlockSpec(memory_space=pltpu.HBM),
            pl.BlockSpec(memory_space=pltpu.HBM),
        ],
        out_specs=pl.BlockSpec(memory_space=pltpu.HBM),
        scratch_shapes=[
            pltpu.VMEM((2, 272, 1024), BF),
            pltpu.VMEM((1, 64), I32),
            pltpu.SemaphoreType.DMA((13,)),
        ],
        compiler_params=VMEM,
    )(
        lags,
        pltpu.with_memory_space_constraint(seg_lengths, pltpu.HBM),
        pltpu.with_memory_space_constraint(frames, pltpu.HBM),
    )
    frames_h = all_to_all(halves, ("yl", "yh"))

    packed = call(
        pack_kernel, [((32, 1024), BF)], yl[None], panel_low.T, panel_high.T, smem=1
    )
    panel_own = lax.all_gather(packed, Z8, axis=0, tiled=True)
    panel_other = lax.ppermute(panel_own, "z0", [(0, 1), (1, 0)])

    by_run = frames_h.reshape(2, 2, 272, 1024)
    tails = lax.ppermute(
        by_run[:, 1, 192:256].reshape(128, 1024), Z, [(i, i + 1) for i in range(1, 15, 2)]
    )
    masks = call(mask_kernel, [((8, 2048), F32)], z[None], by_run[:, 0, 256:, :128], smem=1)
    panel_other, masks, own, ridge_column, ridge_row = lax.optimization_barrier(
        (panel_other, masks, own, ridge[:, None], ridge[None, :])
    )

    keep, send = call(
        project_kernel,
        [((256, 1152), BF)] * 2,
        panel_own,
        panel_other,
        frames_h,
        tails,
        scratch=[pltpu.VMEM((512, 1024), BF)],
    )
    got = lax.ppermute(send, "c", [(0, 1), (1, 0)])
    pairs = (keep.astype(F32) + got.astype(F32)).astype(BF)
    parts = all_to_all(pairs.reshape(32, 8, 1152), PLANE)
    basis, tiled = call(
        sum_kernel,
        [((16, 2176), BF), ((8, 16, 2048), BF)],
        parts.reshape(2, 4, 2, 2, 8, 1152),
    )

    right = all_to_all(tiled, RIGHT)
    left = lax.all_gather(basis, "c", axis=0, tiled=True)
    left = lax.all_gather(left, "x", axis=0, tiled=True)

    terms = call(
        cov_kernel, [((8, 104, 128), BF)], masks, left, right.reshape(128, 2048)
    )
    rows = call(rows_kernel, [((8, 8, 128), F32)], all_to_all(terms, FAR))
    by_row = all_to_all(rows, FE)
    return call(
        lambda *refs: final_kernel(1.0 / 16384.0, *refs),
        [((3, 2, 1024), F32), ((2, 32), F32)],
        by_row,
        own,
        ridge_column,
        ridge_row,
    )


def solution(mesh):
    fine = Mesh(
        np.asarray(mesh.devices).reshape(2, 2, 2, 2, 2, 4, 2, 2),
        ("z3", "z2", "z1", "z0", "yh", "x", "c", "yl"),
    )
    tm = Z + ("yh",)
    in_specs = (P("yl", tm, FE), P(FE, tm), P(FE, tm), P("yl"), P("yl", None), P())
    rows = tm + FE + ("yl",)
    out_specs = (P(None, rows, None), P(rows, None))
    return jax.shard_map(local, mesh=fine, in_specs=in_specs, out_specs=out_specs, check_vma=False)
```
